32 devices in a mesh: frow: 4 (over x, core), fcol: 8 (over z, y).
Axes of the slice: x: 2, y: 2, z: 4, core: 2. Of those that a mesh axis runs over, the one named last changes fastest.
Arguments:
- facet_image: bfloat16 [2048, 4096], P('frow', 'fcol'), may hold values from -6 to 6
- row_offsets: int32 [2], replicated, may hold values from 0 to 65280
- col_offsets: int32 [2], replicated, may hold values from 0 to 65280
- vis_subgrid: int32 [16384], P(('frow', 'fcol')), may hold values from 0 to 3
- vis_u: int32 [16384], P(('frow', 'fcol')), may hold values from 0 to 255
- vis_v: int32 [16384], P(('frow', 'fcol')), may hold values from 0 to 255
- observed: float32 [2, 16384], P(None, ('frow', 'fcol')), may hold values from -6 to 6
Outputs:
- facet_residual: float32 [2048, 4096], P('frow', 'fcol')
- residual_vis: float32 [2, 16384], P(None, ('frow', 'fcol'))
The draws below stay inside these ranges and needn't reach their ends.
Inputs may be any that keep to these rules, and one draw needn't show every extreme that they name: `vis_subgrid`: subgrid numbers count row by row over the 2 x 2 subgrids.
All inputs are finite; a program needn't handle non-finite values.
Results may differ from the reference program's by a relative error of at most 0.023.
Values may be sent and summed in bfloat16 or wider, within the bound.
A program may use at most 64 MiB of HBM per device.

```python
import math
import jax
import jax.numpy as jnp
import numpy as np
from jax import lax

SKY = 65536
FS = 512
SG = 256
NR = 2
NC = 2
NVIS = 16384
N_FROW = 4
N_FCOL = 8


def with_ends(drawn, rng, least, largest):
    index_at = [jax.random.randint(jax.random.fold_in(rng, axis), (), 0, length) for axis, length in enumerate(drawn.shape)]
    main_axis = drawn.shape.index(max(drawn.shape))
    next_to = index_at[:main_axis] + [(index_at[main_axis] + 1) % drawn.shape[main_axis]] + index_at[main_axis + 1:]
    return drawn.at[tuple(index_at)].set(least).at[tuple(next_to)].set(largest)


def block_levels(key, extent, split, low, largest):
    loudness = 1.0
    for dim, parts in split:
        heights = jax.random.uniform(jax.random.fold_in(jax.random.fold_in(key, 6), dim), (parts,), jnp.float32, low / len(split), largest / len(split))
        loudness = loudness * jnp.repeat(jnp.exp(heights), extent[dim] // parts).reshape((-1,) + (1,) * (len(extent) - 1 - dim))
    return loudness


def rank_table(number_of, slope):
    loads = [(1 << 20) // math.isqrt(rank ** slope) + 1 for rank in range(1, number_of + 1)]
    deviation = 1 + sum(loads) // (1 << 30)
    return np.cumsum(np.array([max(1, weight // deviation) for weight in loads]))


def ranked(key, shape, amount, lean):
    table = rank_table(amount, lean)
    pick = jax.random.randint(jax.random.fold_in(key, 1), shape, 0, int(table[amount - 1]))
    standing = jnp.searchsorted(jnp.asarray(table, jnp.int32), pick, side="right")
    return jax.random.permutation(jax.random.fold_in(key, 2), amount)[standing].astype(jnp.int32)


def scatter_about(stream_key, dims, deviation, bound, pieces=(), kind=jnp.bfloat16):
    values = jax.random.normal(stream_key, dims, jnp.float32) * deviation
    if len(pieces) > 0:
        values = block_levels(stream_key, dims, pieces, -0.22, 0.18) * values
    return jnp.clip(values, min=-bound, max=bound).astype(kind)


def setup_inputs(seed: int = 0) -> dict:
    streams_of = jax.random.split(jax.random.key(seed), 8)
    facet_image = scatter_about(streams_of[0], (FS * N_FROW, FS * N_FCOL), 1.0, 6.0, ((0, 4), (1, 8)))
    row_offsets = jax.random.randint(streams_of[1], (NR,), 0, SKY - SG + 1).astype(jnp.int32)
    col_offsets = jax.random.randint(streams_of[2], (NC,), 0, SKY - SG + 1).astype(jnp.int32)
    vis_subgrid = with_ends(ranked(streams_of[3], (NVIS,), NR * NC, 2), jax.random.fold_in(streams_of[3], 3), 0, (NR * NC) - 1).astype(jnp.int32)
    vis_u = with_ends(jax.random.randint(streams_of[4], (NVIS,), 0, SG), jax.random.fold_in(streams_of[4], 1), 0, SG - 1).astype(jnp.int32)
    vis_v = with_ends(jax.random.randint(streams_of[5], (NVIS,), 0, SG), jax.random.fold_in(streams_of[5], 1), 0, SG - 1).astype(jnp.int32)
    observed = scatter_about(streams_of[6], (2, NVIS), 1.0, 6.0, ((1, 32),), jnp.float32)
    return dict(facet_image=facet_image, row_offsets=row_offsets, col_offsets=col_offsets, vis_subgrid=vis_subgrid, vis_u=vis_u, vis_v=vis_v, observed=observed)


def wrapped(frequency, position):
    high_part = frequency // 256
    low_part = frequency % 256
    return (high_part * (position * 256 % SKY) + low_part * position) % SKY

def sky_tables(start, positions):
    frequency = start + jnp.arange(SG, dtype=jnp.int32)[:, None]
    angles = wrapped(frequency, positions[None, :]).astype(jnp.float32) * (2.0 * math.pi / SKY)
    return (jnp.cos(angles).astype(jnp.bfloat16), jnp.sin(angles).astype(jnp.bfloat16))

def grid_tables():
    counter = jnp.arange(SG, dtype=jnp.int32)
    angles = (counter[:, None] * counter[None, :] % SG).astype(jnp.float32) * (2.0 * math.pi / SG)
    return (jnp.cos(angles).astype(jnp.bfloat16), jnp.sin(angles).astype(jnp.bfloat16))

def reference(facet_image, row_offsets, col_offsets, vis_subgrid, vis_u, vis_v, observed):
    f32 = jnp.float32
    hp = lax.Precision.HIGHEST
    scale_in = 1.0 / (FS * math.sqrt(N_FROW * N_FCOL))
    scale_out = 1.0 / (SG * math.sqrt(NR * NC))
    row_pos = (jnp.arange(N_FROW, dtype=jnp.int32)[:, None] * (SKY // N_FROW) + jnp.arange(FS, dtype=jnp.int32)[None, :] * (SKY // (N_FROW * FS))).reshape(-1)
    col_pos = (jnp.arange(N_FCOL, dtype=jnp.int32)[:, None] * (SKY // N_FCOL) + jnp.arange(FS, dtype=jnp.int32)[None, :] * (SKY // (N_FCOL * FS))).reshape(-1)
    row_tabs = [sky_tables(row_offsets[row_pick], row_pos) for row_pick in range(NR)]
    col_tabs = [sky_tables(col_offsets[col_pick], col_pos) for col_pick in range(NC)]
    blocks = facet_image.astype(f32).reshape(N_FROW * FS, N_FCOL, FS)
    col_sums = []
    for col_pick in range(NC):
        cos_tab, sin_tab = col_tabs[col_pick]
        p_full = jnp.einsum('xjy,bjy->xjb', blocks, cos_tab.astype(f32).reshape(SG, N_FCOL, FS)).astype(jnp.bfloat16)
        q_full = jnp.einsum('xjy,bjy->xjb', blocks, sin_tab.astype(f32).reshape(SG, N_FCOL, FS)).astype(jnp.bfloat16)
        col_sums.append((p_full.astype(f32).sum(axis=1), q_full.astype(f32).sum(axis=1)))
    real_list = []
    imag_list = []
    for row_pick in range(NR):
        crow = row_tabs[row_pick][0].astype(f32)
        srow = row_tabs[row_pick][1].astype(f32)
        for col_pick in range(NC):
            psum, qsum = col_sums[col_pick]
            real_list.append((jnp.dot(crow, psum, precision=hp) - jnp.dot(srow, qsum, precision=hp)) * scale_in)
            imag_list.append(-(jnp.dot(crow, qsum, precision=hp) + jnp.dot(srow, psum, precision=hp)) * scale_in)
    sub_real = jnp.stack(real_list).astype(jnp.bfloat16).reshape(NR * NC * SG, SG)
    sub_imag = jnp.stack(imag_list).astype(jnp.bfloat16).reshape(NR * NC * SG, SG)
    kcos, ksin = grid_tables()
    w_real = (jnp.dot(sub_real, kcos, preferred_element_type=f32) - jnp.dot(sub_imag, ksin, preferred_element_type=f32)).astype(jnp.bfloat16)
    w_imag = (jnp.dot(sub_real, ksin, preferred_element_type=f32) + jnp.dot(sub_imag, kcos, preferred_element_type=f32)).astype(jnp.bfloat16)
    w_real = w_real.astype(f32).reshape(NR * NC, SG, SG)
    w_imag = w_imag.astype(f32).reshape(NR * NC, SG, SG)
    kc32 = kcos.astype(f32)
    ks32 = ksin.astype(f32)
    hat_real = (jnp.einsum('au,sav->suv', kc32, w_real) - jnp.einsum('au,sav->suv', ks32, w_imag)) / SG
    hat_imag = (jnp.einsum('au,sav->suv', ks32, w_real) + jnp.einsum('au,sav->suv', kc32, w_imag)) / SG
    cell_ids = ((vis_subgrid * SG + vis_u) * SG + vis_v).astype(jnp.int32)
    model_vis = jnp.stack([hat_real.reshape(-1)[cell_ids], hat_imag.reshape(-1)[cell_ids]])
    residual = observed - model_vis
    cells_all = NR * NC * SG * SG
    ghat_real = jax.ops.segment_sum(residual[0], cell_ids, num_segments=cells_all).astype(jnp.bfloat16).reshape(NR * NC * SG, SG)
    ghat_imag = jax.ops.segment_sum(residual[1], cell_ids, num_segments=cells_all).astype(jnp.bfloat16).reshape(NR * NC * SG, SG)
    v_real = (jnp.dot(ghat_real, kcos, preferred_element_type=f32) + jnp.dot(ghat_imag, ksin, preferred_element_type=f32)).astype(jnp.bfloat16)
    v_imag = (jnp.dot(ghat_imag, kcos, preferred_element_type=f32) - jnp.dot(ghat_real, ksin, preferred_element_type=f32)).astype(jnp.bfloat16)
    v_real = v_real.astype(f32).reshape(NR * NC, SG, SG)
    v_imag = v_imag.astype(f32).reshape(NR * NC, SG, SG)
    back_real = ((jnp.einsum('au,sub->sab', kc32, v_real) + jnp.einsum('au,sub->sab', ks32, v_imag)) / SG).astype(jnp.bfloat16)
    back_imag = ((jnp.einsum('au,sub->sab', kc32, v_imag) - jnp.einsum('au,sub->sab', ks32, v_real)) / SG).astype(jnp.bfloat16)
    image = jnp.zeros((N_FROW * FS, N_FCOL * FS), f32)
    for col_pick in range(NC):
        u_real = jnp.zeros((N_FROW * FS, SG), f32)
        u_imag = jnp.zeros((N_FROW * FS, SG), f32)
        for row_pick in range(NR):
            crow, srow = row_tabs[row_pick]
            sub_index = row_pick * NC + col_pick
            g_real = back_real[sub_index]
            g_imag = back_imag[sub_index]
            u_real = u_real + jnp.dot(crow.T, g_real, preferred_element_type=f32) - jnp.dot(srow.T, g_imag, preferred_element_type=f32)
            u_imag = u_imag + jnp.dot(crow.T, g_imag, preferred_element_type=f32) + jnp.dot(srow.T, g_real, preferred_element_type=f32)
        ccol, scol = col_tabs[col_pick]
        image = image + jnp.dot(u_real.astype(jnp.bfloat16), ccol, preferred_element_type=f32) - jnp.dot(u_imag.astype(jnp.bfloat16), scol, preferred_element_type=f32)
    return (image * scale_out, residual)
```

```python
import functools
import math

import jax
import jax.numpy as jnp
from jax import lax
from jax.experimental import pallas as pl
from jax.experimental.pallas import tpu as pltpu
from jax.sharding import PartitionSpec as P

SKY = 65536
SG = 256
NR = 2
NC = 2
f32 = jnp.float32
bf16 = jnp.bfloat16
i32 = jnp.int32
MESH = pl.DeviceIdType.MESH
VM = pl.BlockSpec(memory_space=pltpu.VMEM)
SM = pl.BlockSpec(memory_space=pltpu.SMEM)
LIMIT = 24 << 20


def geometry():
    rows = lax.axis_size("frow")
    cols = lax.axis_size("fcol")
    nx = rows // 2
    ny = 1 << ((cols.bit_length() - 1) // 2)
    nz = cols // ny
    return rows, cols, nx, ny, nz


def position():
    _, _, _, ny, _ = geometry()
    frow = lax.axis_index("frow")
    fcol = lax.axis_index("fcol")
    return frow // 2, frow % 2, fcol % ny, fcol // ny


def dims(contract):
    return ((contract, contract), ((), ()))


def phase(product):
    angle = (product & (SKY - 1)).astype(f32) * (2.0 * math.pi / SKY)
    return jnp.cos(angle), jnp.sin(angle)


def expand(first, places, c_ref, s_ref):
    n = places.shape[1]
    steps = lax.broadcasted_iota(i32, (16, n), 0)
    c0, s0 = phase(steps * places)
    c1, s1 = phase((first + 16 * steps) * places)
    for k in range(SG // 16):
        ck = c1[k : k + 1]
        sk = s1[k : k + 1]
        c_ref[k * 16 : k * 16 + 16, :] = (ck * c0 - sk * s0).astype(bf16)
        s_ref[k * 16 : k * 16 + 16, :] = (sk * c0 + ck * s0).astype(bf16)


def place(q):
    _, _, _, ny, nz = geometry()
    return q // (ny * nz), (q // nz) % ny, q % nz


def device(q, h):
    _, _, _, ny, _ = geometry()
    x, y, z = place(q)
    return (2 * x + h, z * ny + y)


def hots(vis, h, base, rows_own):
    n = vis.shape[1]
    cell = vis[0:1].astype(i32)
    sub = cell // (SG * SG)
    row = (sub // NC) * SG + (cell // SG) % SG - base
    row = jnp.where(sub % NC == h, row, -1)
    hot_row = lax.broadcasted_iota(i32, (rows_own, n), 0) == row
    hot_col = lax.broadcasted_iota(i32, (SG, n), 0) == cell % SG
    return hot_row, jnp.where(hot_col, 1.0, 0.0).astype(bf16)


def main_kernel(
    scale, ro_ref, co_ref, sub_ref, u_ref, v_ref, obs_ref, facet_ref,
    g_ref, ar_ref, ai_ref, bt_ref, res_ref,
    kk, ks, rc, rs, vis_ref, vis_all, other, z_ref, zb_ref, grid_acc,
    acc_a, acc_b, send_a, send_b, got_a1, got_b1, got_a2, got_b2,
    own_z, send_z, got_z, gz, model, vals, pair_vals, slots,
    ssem, rsem, vs, vr, ws, wr, lsem,
):
    rows, cols, nx, ny, nz = geometry()
    x, h, y, z = position()
    chips = nx * ny * nz
    me = (x * ny + y) * nz + z
    fs = facet_ref.shape[0]
    nv = vis_ref.shape[1]
    rows_own = NR * SG // chips
    sib = (2 * x + 1 - h, lax.axis_index("fcol"))
    barrier = pltpu.get_barrier_semaphore()

    def peers(act):
        def step(d, carry):
            act(d, lax.rem(me + d, chips), lax.rem(me - d + chips, chips))
            return carry

        lax.fori_loop(1, chips, step, 0)

    peers(lambda d, to, frm: pl.semaphore_signal(barrier, inc=1, device_id=device(to, h), device_id_type=MESH))
    pl.semaphore_signal(barrier, inc=1, device_id=sib, device_id_type=MESH)
    cell = (sub_ref[...] * SG + u_ref[...]) * SG + v_ref[...]
    vis_ref[0:1] = cell.astype(f32)
    vis_ref[1:3] = obs_ref[...]
    vis_ref[3:4] = jnp.zeros((1, nv), f32)
    mine = pltpu.make_async_copy(vis_ref, vis_all.at[h, me], lsem)
    mine.start()
    expand(0, lax.broadcasted_iota(i32, (1, SG), 1) * (SKY // SG), kk, ks)
    used = [0]
    sent = []

    def send(src, dst, to):
        k = used[0]
        used[0] += 1
        copy = pltpu.make_async_remote_copy(
            src, dst, ssem.at[k], rsem.at[k], device_id=to, device_id_type=MESH
        )
        copy.start()
        sent.append(copy)
        return k

    def land(k, dst):
        pltpu.make_async_remote_copy(
            dst, dst, ssem.at[k], rsem.at[k], device_id=sib, device_id_type=MESH
        ).wait_recv()

    def link(d, to, slot):
        return pltpu.make_async_remote_copy(
            vis_ref, vis_all.at[h, slot], vs.at[d], vr.at[d],
            device_id=device(to, h), device_id_type=MESH,
        )


    kcos = kk[...]
    ksin = ks[...]
    wide = SG // 2
    waves = range(2)

    def compose(n, start, unit):
        places = (start + lax.broadcasted_iota(i32, (1, n), 1)) * unit
        expand(0, places, rc.at[:, :n], rs.at[:, :n])
        c = rc[:, :n]
        s = rs[:, :n]
        re = jnp.dot(kcos, c, preferred_element_type=f32) + jnp.dot(ksin, s, preferred_element_type=f32)
        im = jnp.dot(ksin, c, preferred_element_type=f32) - jnp.dot(kcos, s, preferred_element_type=f32)

        def shifted(offset):
            cos, sin = phase(offset * places)
            return (re * cos + im * sin).astype(bf16), (im * cos - re * sin).astype(bf16)

        return shifted

    shifted = compose(fs, lax.axis_index("fcol") * fs, SKY // (cols * fs))
    for c in range(NC):
        bt_ref[c, :SG], bt_ref[c, SG:] = shifted(co_ref[c])
    pl.semaphore_wait(barrier, chips)
    k_facet = send(facet_ref, other, sib)
    peers(lambda d, to, frm: link(d, to, me).start())
    shifted = compose(2 * fs, x * (2 * fs), SKY // (rows * fs))
    for r in range(NR):
        cut = slice(r * SG, r * SG + SG)
        ar_ref[cut], ai_ref[cut] = shifted(ro_ref[r])

    mine.wait()

    def project(ref, w):
        re = bt_ref[h, w * wide : (w + 1) * wide]
        im = bt_ref[h, SG + w * wide : SG + (w + 1) * wide]
        b = jnp.concatenate([re, im], 0)
        return lax.dot_general(ref[...], b, (((1,), (1,)), ((), ())), preferred_element_type=f32).astype(bf16)

    part = NR * SG // (nx * ny)
    own_cut = pl.ds(pl.multiple_of(h * fs, fs), fs)
    other_cut = pl.ds(pl.multiple_of((1 - h) * fs, fs), fs)
    first_a, first_b, second_a, second_b = [[], []], [[], []], [[], []], [[], []]
    third, fourth, fifth_a, fifth_b = [[], []], [[], []], [[], []], [[], []]
    sixth_a, sixth_b = [[], []], [[], []]

    def to_x(d):
        return device((lax.rem(x + d, nx) * ny + y) * nz + z, h)

    def to_y(d):
        return device((x * ny + lax.rem(y + d, ny)) * nz + z, h)

    def to_z(d):
        return device((x * ny + y) * nz + lax.rem(z + d, nz), h)

    for w in waves:
        own_p = project(facet_ref, w)
        if w == 0:
            land(k_facet, other)
        other_p = project(other, w)
        for dx in list(range(1, nx)) + [0]:
            px = lax.rem(x + dx, nx)
            for dy in list(range(1, ny)) + [0]:
                py = lax.rem(y + dy, ny)
                cut = pl.ds(pl.multiple_of((px * ny + py) * part, part), part)
                one = jnp.dot(ar_ref[cut, own_cut], own_p, preferred_element_type=f32)
                one += jnp.dot(ar_ref[cut, other_cut], other_p, preferred_element_type=f32)
                two = jnp.dot(ai_ref[cut, own_cut], own_p, preferred_element_type=f32)
                two += jnp.dot(ai_ref[cut, other_cut], other_p, preferred_element_type=f32)
                zr = one[:, :wide] - two[:, wide:]
                zi = one[:, wide:] + two[:, :wide]
                z_ref[w, 0, px, py] = zr
                z_ref[w, 1, px, py] = zi
                zb_ref[w, 0, px, py] = zr.astype(bf16)
                zb_ref[w, 1, px, py] = zi.astype(bf16)
                if dx == 0 and dy > 0:
                    first_b[w].append(send(zb_ref.at[w, 1, :, py], got_b1.at[w, dy - 1], to_y(dy)))
            if dx > 0:
                first_a[w].append(send(zb_ref.at[w, 0, px], got_a1.at[w, dx - 1], to_x(dx)))

    peers(lambda d, to, frm: link(d, to, frm).wait_recv())
    k_vis = send(vis_all.at[h], vis_all.at[h], sib)

    base = me * rows_own
    grid_acc[...] = jnp.zeros_like(grid_acc)

    def gridding(side, lo, hi):
        def one(q):
            vis = vis_all[side, q]
            hot_row, hot_col = hots(vis, h, base, rows_own)
            parts = []
            for p in (1, 2):
                val = vis[p : p + 1]
                high = val.astype(bf16).astype(f32)
                parts += [high, val - high]
            parts.append(jnp.ones_like(vis[0:1]))
            left = jnp.concatenate([jnp.where(hot_row, t, 0.0) for t in parts], 0).astype(bf16)
            return lax.dot_general(left, hot_col, (((1,), (1,)), ((), ())), preferred_element_type=f32)

        def body(t, carry):
            got = one(lo + 2 * t) + one(lo + 2 * t + 1)
            grid_acc[...] += got
            return carry

        lax.fori_loop(0, (hi - lo) // 2, body, 0)

    half = chips // 2

    def stage_two(w):
        for d in range(nx - 1):
            land(first_a[w][d], got_a1.at[w, d])
        total = z_ref[w, 0, x]
        for d in range(nx - 1):
            total = total + got_a1[w, d].astype(f32)
        acc_a[w] = total
        send_a[w] = total.astype(bf16)
        for d in range(1, ny):
            second_a[w].append(send(send_a.at[w, lax.rem(y + d, ny)], got_a2.at[w, d - 1], to_y(d)))
        for d in range(ny - 1):
            land(first_b[w][d], got_b1.at[w, d])
        total = z_ref[w, 1, :, y]
        for d in range(ny - 1):
            total = total + got_b1[w, d].astype(f32)
        acc_b[w] = total
        send_b[w] = total.astype(bf16)
        for d in range(1, nx):
            second_b[w].append(send(send_b.at[w, lax.rem(x + d, nx)], got_b2.at[w, d - 1], to_x(d)))

    def stage_three(w):
        for d in range(ny - 1):
            land(second_a[w][d], got_a2.at[w, d])
        re = acc_a[w, y]
        for d in range(ny - 1):
            re = re + got_a2[w, d].astype(f32)
        for d in range(nx - 1):
            land(second_b[w][d], got_b2.at[w, d])
        im = acc_b[w, x]
        for d in range(nx - 1):
            im = im + got_b2[w, d].astype(f32)
        for k in range(nz):
            cut = slice(k * rows_own, (k + 1) * rows_own)
            own_z[w, k, :, :wide] = re[cut]
            own_z[w, k, :, wide:] = im[cut]
            send_z[w, k, :, :wide] = re[cut].astype(bf16)
            send_z[w, k, :, wide:] = im[cut].astype(bf16)
        for d in range(1, nz):
            third[w].append(send(send_z.at[w, lax.rem(z + d, nz)], got_z.at[w, d - 1], to_z(d)))

    def turn(w):
        for d in range(nz - 1):
            land(third[w][d], got_z.at[w, d])
        total = own_z[w, z]
        for d in range(nz - 1):
            total = total + got_z[w, d].astype(f32)
        m = total * scale
        cut = slice(w * wide, (w + 1) * wide)
        got = [grid_acc[p * rows_own : (p + 1) * rows_own, cut] for p in range(5)]
        hat_re = got[0] + got[1] - got[4] * m[:, :wide]
        hat_im = got[2] + got[3] - got[4] * m[:, wide:]
        gz[w, z, :, :wide] = hat_re.astype(bf16)
        gz[w, z, :, wide:] = hat_im.astype(bf16)
        for d in range(1, nz):
            fourth[w].append(send(gz.at[w, z], gz.at[w, z], to_z(d)))
        both = jnp.concatenate([m[:, :wide], m[:, wide:]], 0)
        high = both.astype(bf16)
        model[: 2 * rows_own, cut] = high
        model[2 * rows_own :, cut] = (both - high.astype(f32)).astype(bf16)

    cross = []

    def over(index):
        src = g_ref.at[(h,) + index]
        cross.append((send(src, src, sib), index))

    def stage_five(w):
        for d in range(1, nz):
            land(fourth[w][d - 1], gz.at[w, lax.rem(z - d + nz, nz)])
        for k in range(nz):
            cut = slice(k * rows_own, (k + 1) * rows_own)
            g_ref[h, w, 0, x, y, cut, :] = gz[w, k, :, :wide]
            g_ref[h, w, 1, x, y, cut, :] = gz[w, k, :, wide:]
        for d in range(1, ny):
            blk = g_ref.at[h, w, 0, x, y]
            fifth_a[w].append(send(blk, blk, to_y(d)))
        for d in range(1, nx):
            blk = g_ref.at[h, w, 1, x, y]
            fifth_b[w].append(send(blk, blk, to_x(d)))
        over((w, 0, x, y))
        over((w, 1, x, y))

    def stage_six(w):
        for d in range(1, ny):
            land(fifth_a[w][d - 1], g_ref.at[h, w, 0, x, lax.rem(y - d + ny, ny)])
        for d in range(1, nx):
            blk = g_ref.at[h, w, 0, x]
            sixth_a[w].append(send(blk, blk, to_x(d)))
        for d in range(1, nx):
            land(fifth_b[w][d - 1], g_ref.at[h, w, 1, lax.rem(x - d + nx, nx), y])
        for d in range(1, ny):
            blk = g_ref.at[h, w, 1, :, y]
            sixth_b[w].append(send(blk, blk, to_y(d)))
        for d in range(1, ny):
            over((w, 0, x, lax.rem(y - d + ny, ny)))
        for d in range(1, nx):
            over((w, 1, lax.rem(x - d + nx, nx), y))

    def finish(w):
        for d in range(1, nx):
            px = lax.rem(x - d + nx, nx)
            land(sixth_a[w][d - 1], g_ref.at[h, w, 0, px])
            over((w, 0, px))
        for d in range(1, ny):
            py = lax.rem(y - d + ny, ny)
            land(sixth_b[w][d - 1], g_ref.at[h, w, 1, :, py])
            over((w, 1, slice(None), py))

    def degrid(side, lo, hi):
        def one(q):
            hot_row, hot_col = hots(vis_all[side, q], h, base, rows_own)
            val = jnp.dot(model[...], hot_col, preferred_element_type=f32)
            val = val[: 2 * rows_own] + val[2 * rows_own :]
            vr_ = jnp.sum(jnp.where(hot_row, val[:rows_own], 0.0), 0, keepdims=True)
            vi_ = jnp.sum(jnp.where(hot_row, val[rows_own:], 0.0), 0, keepdims=True)
            return jnp.concatenate([vr_, vi_], 0)

        def body(t, carry):
            a = one(lo + 2 * t)
            b = one(lo + 2 * t + 1)
            vals[side, lo + 2 * t] = a
            vals[side, lo + 2 * t + 1] = b
            return carry

        lax.fori_loop(0, (hi - lo) // 2, body, 0)

    def back(d, to, slot):
        return pltpu.make_async_remote_copy(
            vals.at[h, to], slots.at[slot], ws.at[d], wr.at[d],
            device_id=device(to, h), device_id_type=MESH,
        )

    stage_two(0)
    gridding(h, 0, half)
    stage_two(1)
    gridding(h, half, chips)
    stage_three(0)
    land(k_vis, vis_all.at[1 - h])
    gridding(1 - h, 0, half)
    stage_three(1)
    gridding(1 - h, half, chips)
    turn(0)
    turn(1)
    degrid(1 - h, 0, half)
    stage_five(0)
    degrid(1 - h, half, chips)
    k_vals = send(vals.at[1 - h], pair_vals, sib)
    stage_five(1)
    degrid(h, 0, half)
    stage_six(0)
    degrid(h, half, chips)
    stage_six(1)
    land(k_vals, pair_vals)
    vals[h] = vals[h] + pair_vals[...]
    peers(lambda d, to, frm: back(d, to, me).start())
    finish(0)
    finish(1)
    peers(lambda d, to, frm: back(d, to, frm).wait_recv())
    start = vals[h, me]
    res_ref[...] = obs_ref[...] - lax.fori_loop(
        1, chips, lambda d, t: t + slots[lax.rem(me + d, chips)], start
    )
    for k, index in cross:
        land(k, g_ref.at[(1 - h,) + index])
    for copy in sent:
        copy.wait_send()
    peers(lambda d, to, frm: link(d, to, me).wait_send())
    peers(lambda d, to, frm: back(d, to, me).wait_send())


def main(ro, co, sub, u, v, obs, facet, scale):
    _, _, nx, ny, nz = geometry()
    chips = nx * ny * nz
    fs = facet.shape[0]
    nv = obs.shape[1]
    rows_own = NR * SG // chips
    long = nz * rows_own
    copies = 128
    dma = pltpu.SemaphoreType.DMA
    return pl.pallas_call(
        functools.partial(main_kernel, scale),
        out_shape=[
            jax.ShapeDtypeStruct((2, 2, 2, nx, ny, long, SG // 2), bf16),
            jax.ShapeDtypeStruct((NR * SG, 2 * fs), bf16),
            jax.ShapeDtypeStruct((NR * SG, 2 * fs), bf16),
            jax.ShapeDtypeStruct((NC, 2 * SG, fs), bf16),
            jax.ShapeDtypeStruct((2, nv), f32),
        ],
        in_specs=[SM, SM] + [VM] * 5,
        out_specs=[VM] * 5,
        scratch_shapes=[
            pltpu.VMEM((SG, SG), bf16),
            pltpu.VMEM((SG, SG), bf16),
            pltpu.VMEM((SG, 2 * fs), bf16),
            pltpu.VMEM((SG, 2 * fs), bf16),
            pltpu.VMEM((4, nv), f32),
            pltpu.VMEM((2, chips, 4, nv), f32),
            pltpu.VMEM((fs, fs), bf16),
            pltpu.VMEM((2, 2, nx, ny, long, SG // 2), f32),
            pltpu.VMEM((2, 2, nx, ny, long, SG // 2), bf16),
            pltpu.VMEM((5 * rows_own, SG), f32),
            pltpu.VMEM((2, ny, long, SG // 2), f32),
            pltpu.VMEM((2, nx, long, SG // 2), f32),
            pltpu.VMEM((2, ny, long, SG // 2), bf16),
            pltpu.VMEM((2, nx, long, SG // 2), bf16),
            pltpu.VMEM((2, nx - 1, ny, long, SG // 2), bf16),
            pltpu.VMEM((2, ny - 1, nx, long, SG // 2), bf16),
            pltpu.VMEM((2, ny - 1, long, SG // 2), bf16),
            pltpu.VMEM((2, nx - 1, long, SG // 2), bf16),
            pltpu.VMEM((2, nz, rows_own, SG), f32),
            pltpu.VMEM((2, nz, rows_own, SG), bf16),
            pltpu.VMEM((2, nz - 1, rows_own, SG), bf16),
            pltpu.VMEM((2, nz, rows_own, SG), bf16),
            pltpu.VMEM((4 * rows_own, SG), bf16),
            pltpu.VMEM((2, chips, 2, nv), f32),
            pltpu.VMEM((chips, 2, nv), f32),
            pltpu.VMEM((chips, 2, nv), f32),
            dma((copies,)),
            dma((copies,)),
            dma((chips,)),
            dma((chips,)),
            dma((chips,)),
            dma((chips,)),
            dma,
        ],
        compiler_params=pltpu.CompilerParams(
            collective_id=0, has_side_effects=True, vmem_limit_bytes=LIMIT
        ),
        name="cycle",
    )(ro, co, sub, u, v, obs, facet)


def backward_kernel(scale, g_ref, ar_ref, ai_ref, bt_ref, image_ref):
    _, h, _, _ = position()
    fs = image_ref.shape[0]
    cut = pl.ds(pl.multiple_of(h * fs, fs), fs)
    first = (((0,), (0,)), ((), ()))
    g = jnp.concatenate([g_ref[c, w, p] for c in range(NC) for p in range(2) for w in range(2)], 1)
    one = lax.dot_general(ar_ref[:, cut], g, first, preferred_element_type=f32)
    two = lax.dot_general(ai_ref[:, cut], g, first, preferred_element_type=f32)
    parts = []
    for c in range(NC):
        re = slice(2 * c * SG, (2 * c + 1) * SG)
        im = slice((2 * c + 1) * SG, (2 * c + 2) * SG)
        parts += [one[:, re] + two[:, im], one[:, im] - two[:, re]]
    u = jnp.concatenate(parts, 1).astype(bf16)
    b = bt_ref[...].reshape(2 * NC * SG, fs)
    image_ref[...] = jnp.dot(u, b, preferred_element_type=f32) * scale


def backward(g, ar, ai, bt, scale):
    fs = bt.shape[2]
    return pl.pallas_call(
        functools.partial(backward_kernel, scale),
        out_shape=jax.ShapeDtypeStruct((fs, fs), f32),
        in_specs=[VM] * 4,
        out_specs=VM,
        compiler_params=pltpu.CompilerParams(vmem_limit_bytes=LIMIT),
        name="backward",
    )(g, ar, ai, bt)


def shards(facet_image, row_offsets, col_offsets, vis_subgrid, vis_u, vis_v, observed):
    rows, cols, _, _, _ = geometry()
    fs = facet_image.shape[0]
    scale_in = 1.0 / (fs * math.sqrt(rows * cols))
    scale_out = 1.0 / (SG * math.sqrt(NR * NC))
    g, ar, ai, bt, residual = main(
        row_offsets, col_offsets, vis_subgrid[None], vis_u[None], vis_v[None],
        observed, facet_image, scale_in / SG,
    )
    image = backward(g.reshape(NC, 2, 2, NR * SG, SG // 2), ar, ai, bt, scale_out / SG)
    return (image, residual)


def solution(mesh):
    in_specs = (
        P("frow", "fcol"),
        P(),
        P(),
        P(("frow", "fcol")),
        P(("frow", "fcol")),
        P(("frow", "fcol")),
        P(None, ("frow", "fcol")),
    )
    out_specs = (P("frow", "fcol"), P(None, ("frow", "fcol")))
    return jax.shard_map(shards, mesh=mesh, in_specs=in_specs, out_specs=out_specs, check_vma=False)
```

```python
import functools
import math

import jax
import jax.numpy as jnp
from jax import lax
from jax.experimental import pallas as pl
from jax.experimental.pallas import tpu as pltpu
from jax.sharding import PartitionSpec as P

SKY = 65536
SG = 256
NR = 2
NC = 2
f32 = jnp.float32
bf16 = jnp.bfloat16
i32 = jnp.int32
MESH = pl.DeviceIdType.MESH
VM = pl.BlockSpec(memory_space=pltpu.VMEM)
HB = pl.BlockSpec(memory_space=pltpu.HBM)
LIMIT = 32 << 20


scope = jax.named_scope


def geometry():
    rows = lax.axis_size("frow")
    cols = lax.axis_size("fcol")
    nx = rows // 2
    ny = 1 << ((cols.bit_length() - 1) // 2)
    nz = cols // ny
    return rows, cols, nx, ny, nz


def position():
    _, _, _, ny, _ = geometry()
    frow = lax.axis_index("frow")
    fcol = lax.axis_index("fcol")
    return frow // 2, frow % 2, fcol % ny, fcol // ny


def phase(product):
    angle = (product & (SKY - 1)).astype(f32) * (2.0 * math.pi / SKY)
    return jnp.cos(angle), jnp.sin(angle)


def expand(first, places, c_ref, s_ref):
    n = places.shape[1]
    steps = lax.broadcasted_iota(i32, (16, n), 0)
    c0, s0 = phase(steps * places)
    c1, s1 = phase((first + 16 * steps) * places)
    for k in range(SG // 16):
        ck = c1[k : k + 1]
        sk = s1[k : k + 1]
        c_ref[k * 16 : k * 16 + 16, :] = (ck * c0 - sk * s0).astype(bf16)
        s_ref[k * 16 : k * 16 + 16, :] = (sk * c0 + ck * s0).astype(bf16)


def place(q):
    _, _, _, ny, nz = geometry()
    return lax.div(q, ny * nz), lax.rem(lax.div(q, nz), ny), lax.rem(q, nz)


def device(q, h):
    _, _, _, ny, _ = geometry()
    x, y, z = place(q)
    return (2 * x + h, z * ny + y)


def hots(vis, h, owned):
    n = vis.shape[1]
    cell = vis[0:1].astype(i32)
    sub = cell // (SG * SG)
    row = (sub // NC) * SG + (cell // SG) % SG
    row = jnp.where(sub % NC == h, row, -1)
    hot_col = lax.broadcasted_iota(i32, (SG, n), 0) == cell % SG
    return owned == row, jnp.where(hot_col, 1.0, 0.0).astype(bf16)


def semaphores():
    plan = {}
    total = 0
    for at, kind in enumerate((
        "xa", "yb", "ya", "xb", "z", "back_z", "back_ya", "back_xb", "back_xa", "back_yb", "cross",
        "facet", "vis", "cells", "values", "answers",
    )):
        count = 4 if at < 11 else 1
        plan[kind] = (at, total, count)
        total += count
    return plan, total


def main_kernel(
    scale, facet_hbm, ro_hbm, co_hbm, sub_hbm, u_hbm, v_hbm, obs_hbm,
    acc_ref, last_ref, bt_ref, res_ref,
    facet_ref, ro_ref, co_ref, sub_ref, u_ref, v_ref, obs_ref,
    kk, ks, rc, rs, a_tab, p_ref, vis_ref, vis_all, other, z_ref, zb_ref, g_ref, grid_acc,
    acc_a, acc_b, send_a, send_b, got_a1, got_b1, got_a2, got_b2,
    own_z, send_z, got_z, gz, model, vals, pair_vals, slots,
    ssem, rsem, lsem,
):
    rows, cols, nx, ny, nz = geometry()
    x, h, y, z = position()
    chips = nx * ny * nz
    me = (x * ny + y) * nz + z
    fs = facet_ref.shape[0]
    nv = vis_ref.shape[1]
    rows_own = NR * SG // chips
    hr = rows_own // 2
    hlong = nz * hr
    part = 2 * hlong
    wide = SG // 2
    waves = range(4)
    sib = (2 * x + 1 - h, lax.axis_index("fcol"))
    barrier = pltpu.get_barrier_semaphore()

    def peers(act):
        def step(d, carry):
            act(d, lax.rem(me + d, chips), lax.rem(me - d + chips, chips))
            return carry

        lax.fori_loop(1, chips, step, 0)

    peers(lambda d, to, frm: pl.semaphore_signal(barrier, inc=1, device_id=device(to, h), device_id_type=MESH))
    pl.semaphore_signal(barrier, inc=1, device_id=sib, device_id_type=MESH)
    loads = []
    for k, (src, dst) in enumerate((
        (ro_hbm, ro_ref), (co_hbm, co_ref), (sub_hbm, sub_ref), (u_hbm, u_ref), (v_hbm, v_ref),
        (obs_hbm, obs_ref), (facet_hbm, facet_ref),
    )):
        loads.append(pltpu.make_async_copy(src, dst, lsem.at[k]))
        loads[-1].start()
    plan = semaphores()[0]

    def send(kind, w, src, dst, to):
        at, base, _ = plan[kind]
        pltpu.make_async_remote_copy(
            src, dst, ssem.at[at], rsem.at[base + w], device_id=to, device_id_type=MESH
        ).start()

    def land(kind, w, like):
        at, base, _ = plan[kind]
        pltpu.make_async_remote_copy(
            like, like, ssem.at[at], rsem.at[base + w], device_id=sib, device_id_type=MESH
        ).wait_recv()

    def sentall(kind, like):
        at, base, _ = plan[kind]
        pltpu.make_async_remote_copy(
            like, like, ssem.at[at], rsem.at[base], device_id=sib, device_id_type=MESH
        ).wait_send()

    with scope("expandK"):
        expand(0, lax.broadcasted_iota(i32, (1, SG), 1) * (SKY // SG), kk, ks)
    kcos = kk[...]
    ksin = ks[...]

    def compose(n, start, unit):
        places = (start + lax.broadcasted_iota(i32, (1, n), 1)) * unit
        expand(0, places, rc.at[:, :n], rs.at[:, :n])
        c = rc[:, :n]
        s = rs[:, :n]
        re = jnp.dot(kcos, c, preferred_element_type=f32) + jnp.dot(ksin, s, preferred_element_type=f32)
        im = jnp.dot(ksin, c, preferred_element_type=f32) - jnp.dot(kcos, s, preferred_element_type=f32)

        def shifted(offset):
            cos, sin = phase(offset * places)
            return (re * cos + im * sin).astype(bf16), (im * cos - re * sin).astype(bf16)

        return shifted

    with scope("composeB"):
        shifted = compose(fs, lax.axis_index("fcol") * fs, SKY // (cols * fs))
        loads[0].wait()
        loads[1].wait()
        for c in range(NC):
            re, im = shifted(co_ref[c])
            for q in range(2):
                bt_ref[c, q, :wide] = re[q * wide : (q + 1) * wide]
                bt_ref[c, q, wide:] = im[q * wide : (q + 1) * wide]
    with scope("cells"):
        for copy in loads[2:6]:
            copy.wait()
        cell = (sub_ref[...] * SG + u_ref[...]) * SG + v_ref[...]
        vis_ref[0:1] = cell.astype(f32)
        vis_ref[1:3] = obs_ref[...]
        vis_ref[3:4] = jnp.zeros((1, nv), f32)
        mine = pltpu.make_async_copy(vis_ref, vis_all.at[h, me], lsem.at[7])
        mine.start()
    with scope("barwait"):
        pl.semaphore_wait(barrier, chips)
    send("facet", 0, facet_hbm, other, sib)
    peers(lambda d, to, frm: send("cells", 0, vis_ref, vis_all.at[h, me], device(to, h)))
    with scope("composeA"):
        shifted = compose(2 * fs, x * (2 * fs), SKY // (rows * fs))
        for r in range(NR):
            pair = shifted(ro_ref[r])
            for b in range(SG // part):
                blk = r * (SG // part) + b
                for e in range(2):
                    for p in range(2):
                        cut = slice(b * part + e * hlong, b * part + (e + 1) * hlong)
                        a_tab[p, e, blk * hlong : (blk + 1) * hlong] = pair[p][cut]

    mine.wait()
    loads[6].wait()

    def project(ref, q):
        return lax.dot_general(
            ref[...], bt_ref[h, q], (((1,), (1,)), ((), ())), preferred_element_type=f32
        ).astype(bf16)

    own_cut = pl.ds(pl.multiple_of(h * fs, fs), fs)
    other_cut = pl.ds(pl.multiple_of((1 - h) * fs, fs), fs)

    def to_x(d):
        return device((lax.rem(x + d, nx) * ny + y) * nz + z, h)

    def to_y(d):
        return device((x * ny + lax.rem(y + d, ny)) * nz + z, h)

    def to_z(d):
        return device((x * ny + y) * nz + lax.rem(z + d, nz), h)

    def produce(w):
        q, e = w // 2, w % 2
        if e == 0:
            p_ref[own_cut] = project(facet_ref, q)
            if q == 0:
                land("facet", 0, other)
            p_ref[other_cut] = project(other, q)
        both = jnp.dot(a_tab[:, e].reshape(2 * nx * ny * hlong, 2 * fs), p_ref[...], preferred_element_type=f32)
        one = both[: nx * ny * hlong]
        two = both[nx * ny * hlong :]
        zr = (one[:, :wide] - two[:, wide:]).reshape(nx, ny, hlong, wide)
        zi = (one[:, wide:] + two[:, :wide]).reshape(nx, ny, hlong, wide)
        z_ref[w, 0] = zr
        z_ref[w, 1] = zi
        zb_ref[w, 0] = zr.astype(bf16)
        zb_ref[w, 1] = zi.astype(bf16)
        for d in range(1, nx):
            send("xa", w, zb_ref.at[w, 0, lax.rem(x + d, nx)], got_a1.at[w, d - 1], to_x(d))
        for d in range(1, ny):
            send("yb", w, zb_ref.at[w, 1, :, lax.rem(y + d, ny)], got_b1.at[w, d - 1], to_y(d))

    owned_row = lax.broadcasted_iota(i32, (rows_own, nv), 0)
    owned_row = (x * ny + y) * part + z * hr + (owned_row // hr) * hlong + owned_row % hr

    def gridding(side, lo, hi):
        def one(q):
            vis = vis_all[side, q]
            hot_row, hot_col = hots(vis, h, owned_row)
            parts = [vis[1:2], vis[2:3], jnp.ones_like(vis[0:1])]
            left = jnp.concatenate([jnp.where(hot_row, t, 0.0) for t in parts], 0).astype(bf16)
            return lax.dot_general(left, hot_col, (((1,), (1,)), ((), ())), preferred_element_type=f32)

        def body(t, carry):
            got = one(lo + 2 * t) + one(lo + 2 * t + 1)
            grid_acc[...] += got
            return carry

        lax.fori_loop(0, (hi - lo) // 2, body, 0)

    def stage_two(w):
        land("xa", w, got_a1.at[w])
        total = z_ref[w, 0, x]
        for d in range(nx - 1):
            total = total + got_a1[w, d].astype(f32)
        acc_a[w] = total
        send_a[w] = total.astype(bf16)
        for d in range(1, ny):
            send("ya", w, send_a.at[w, lax.rem(y + d, ny)], got_a2.at[w, d - 1], to_y(d))
        land("yb", w, got_b1.at[w])
        total = z_ref[w, 1, :, y]
        for d in range(ny - 1):
            total = total + got_b1[w, d].astype(f32)
        acc_b[w] = total
        send_b[w] = total.astype(bf16)
        for d in range(1, nx):
            send("xb", w, send_b.at[w, lax.rem(x + d, nx)], got_b2.at[w, d - 1], to_x(d))

    def stage_three(w):
        land("ya", w, got_a2.at[w])
        re = acc_a[w, y]
        for d in range(ny - 1):
            re = re + got_a2[w, d].astype(f32)
        land("xb", w, got_b2.at[w])
        im = acc_b[w, x]
        for d in range(nx - 1):
            im = im + got_b2[w, d].astype(f32)
        for k in range(nz):
            cut = slice(k * hr, (k + 1) * hr)
            own_z[w, k, :, :wide] = re[cut]
            own_z[w, k, :, wide:] = im[cut]
            send_z[w, k, :, :wide] = re[cut].astype(bf16)
            send_z[w, k, :, wide:] = im[cut].astype(bf16)
        for d in range(1, nz):
            send("z", w, send_z.at[w, lax.rem(z + d, nz)], got_z.at[w, d - 1], to_z(d))

    def turn(w):
        q, e = w // 2, w % 2
        land("z", w, got_z.at[w])
        total = own_z[w, z]
        for d in range(nz - 1):
            total = total + got_z[w, d].astype(f32)
        m = total * scale
        cut = slice(q * wide, (q + 1) * wide)
        got = [grid_acc[p * rows_own + e * hr : p * rows_own + (e + 1) * hr, cut] for p in range(3)]
        hat_re = got[0] - got[2] * m[:, :wide]
        hat_im = got[1] - got[2] * m[:, wide:]
        gz[w, z, :, :wide] = hat_re.astype(bf16)
        gz[w, z, :, wide:] = hat_im.astype(bf16)
        for d in range(1, nz):
            send("back_z", w, gz.at[w, z], gz.at[w, z], to_z(d))
        model[e * hr : (e + 1) * hr, cut] = m[:, :wide]
        model[rows_own + e * hr : rows_own + (e + 1) * hr, cut] = m[:, wide:]

    def over(w, index):
        src = g_ref.at[(h, w) + index]
        send("cross", w, src, src, sib)

    def stage_five(w):
        land("back_z", w, gz.at[w, : nz - 1])
        for k in range(nz):
            cut = slice(k * hr, (k + 1) * hr)
            g_ref[h, w, 0, x, y, cut, :] = gz[w, k, :, :wide]
            g_ref[h, w, 1, x, y, cut, :] = gz[w, k, :, wide:]
        for d in range(1, ny):
            blk = g_ref.at[h, w, 0, x, y]
            send("back_ya", w, blk, blk, to_y(d))
        for d in range(1, nx):
            blk = g_ref.at[h, w, 1, x, y]
            send("back_xb", w, blk, blk, to_x(d))
        over(w, (0, x, y))
        over(w, (1, x, y))

    def stage_six(w):
        land("back_ya", w, g_ref.at[h, w, 0, x, : ny - 1])
        for d in range(1, nx):
            blk = g_ref.at[h, w, 0, x]
            send("back_xa", w, blk, blk, to_x(d))
        land("back_xb", w, g_ref.at[h, w, 1, : nx - 1, y])
        for d in range(1, ny):
            blk = g_ref.at[h, w, 1, :, y]
            send("back_yb", w, blk, blk, to_y(d))
        for d in range(1, ny):
            over(w, (0, x, lax.rem(y - d + ny, ny)))
        for d in range(1, nx):
            over(w, (1, lax.rem(x - d + nx, nx), y))

    def finish(w):
        land("back_xa", w, g_ref.at[h, w, 0, : nx - 1])
        for d in range(1, nx):
            over(w, (0, lax.rem(x - d + nx, nx)))
        land("back_yb", w, g_ref.at[h, w, 1, :, : ny - 1])
        for d in range(1, ny):
            over(w, (1, slice(None), lax.rem(y - d + ny, ny)))

    def crossed(w):
        land("cross", w, g_ref.at[1 - h, w])

    def degrid(side, lo, hi):
        m = model[...].astype(bf16)

        def one(q):
            hot_row, hot_col = hots(vis_all[side, q], h, owned_row)
            val = jnp.dot(m, hot_col, preferred_element_type=f32)
            vr_ = jnp.sum(jnp.where(hot_row, val[:rows_own], 0.0), 0, keepdims=True)
            vi_ = jnp.sum(jnp.where(hot_row, val[rows_own:], 0.0), 0, keepdims=True)
            return jnp.concatenate([vr_, vi_], 0)

        def body(t, carry):
            a = one(lo + 2 * t)
            b = one(lo + 2 * t + 1)
            vals[side, lo + 2 * t] = a
            vals[side, lo + 2 * t + 1] = b
            return carry

        lax.fori_loop(0, (hi - lo) // 2, body, 0)

    first = (((0,), (0,)), ((), ()))
    tall = 2 * nx * ny * hlong

    def spread(c, q):
        g = [
            jnp.concatenate([g_ref[c, 2 * q + e, p].reshape(tall // 2, wide) for e in range(2)], 0)
            for p in range(2)
        ]
        g = jnp.concatenate(g, 1)
        one = lax.dot_general(a_tab[0, :, :, own_cut].reshape(tall, fs), g, first, preferred_element_type=f32)
        two = lax.dot_general(a_tab[1, :, :, own_cut].reshape(tall, fs), g, first, preferred_element_type=f32)
        return jnp.concatenate([one[:, :wide] + two[:, wide:], one[:, wide:] - two[:, :wide]], 1).astype(bf16)

    def image(c, q):
        return jnp.dot(spread(c, q), bt_ref[c, q], preferred_element_type=f32)

    grid_acc[...] = jnp.zeros_like(grid_acc)
    half = chips // 2
    quarter = chips // 4
    seen = [0]

    def grid(n=quarter):
        lo = seen[0]
        seen[0] = lo + n
        side, at = lo // chips, lo % chips
        if side == 1 and at == 0:
            land("vis", 0, vis_all.at[1 - h])
        with scope("grid%d" % lo):
            gridding(h if side == 0 else 1 - h, at, at + n)

    def run(name, w):
        with scope("%s%d" % (name.__name__, w)):
            name(w)

    run(produce, 0)
    run(produce, 1)
    run(produce, 2)
    run(produce, 3)
    with scope("viswait"):
        land("cells", 0, vis_all.at[h, : chips - 1])
    send("vis", 0, vis_all.at[h], vis_all.at[h], sib)
    run(stage_two, 0)
    run(stage_two, 1)
    grid()
    run(stage_two, 2)
    run(stage_three, 0)
    run(stage_two, 3)
    run(stage_three, 1)
    grid()
    grid()
    run(stage_three, 2)
    grid()
    run(stage_three, 3)
    grid()
    grid()
    grid()
    grid()
    run(turn, 0)
    run(turn, 1)
    run(turn, 2)
    run(turn, 3)
    with scope("degrid0"):
        degrid(1 - h, 0, half)
    run(stage_five, 0)
    run(stage_five, 1)
    with scope("degrid1"):
        degrid(1 - h, half, chips)
    send("values", 0, vals.at[1 - h], pair_vals, sib)
    run(stage_five, 2)
    run(stage_six, 0)
    run(stage_five, 3)
    run(stage_six, 1)
    with scope("degrid2"):
        degrid(h, 0, half)
    run(stage_six, 2)
    run(finish, 0)
    run(stage_six, 3)
    run(finish, 1)
    with scope("degrid3"):
        degrid(h, half, chips)
    with scope("landvals"):
        land("values", 0, pair_vals)
        vals[h] = vals[h] + pair_vals[...]
    with scope("backstart"):
        peers(lambda d, to, frm: send("answers", 0, vals.at[h, to], slots.at[me], device(to, h)))
    with scope("imageown0"):
        acc_ref[...] = image(h, 0)
    run(finish, 2)
    run(crossed, 0)
    run(crossed, 1)
    run(finish, 3)
    with scope("imageother0"):
        acc_ref[...] += image(1 - h, 0)
    with scope("imageown1"):
        acc_ref[...] += image(h, 1)
    with scope("backwait"):
        land("answers", 0, slots.at[: chips - 1])
    with scope("result"):
        start = vals[h, me]
        res_ref[...] = obs_ref[...] - lax.fori_loop(
            1, chips, lambda d, t: t + slots[lax.rem(me + d, chips)], start
        )
    run(crossed, 2)
    run(crossed, 3)
    with scope("last"):
        last_ref[...] = spread(1 - h, 1)
    with scope("drain"):
        for kind, like in (
            ("xa", got_a1), ("yb", got_b1), ("ya", got_a2), ("xb", got_b2), ("z", got_z),
            ("back_z", got_z), ("back_ya", got_a2), ("back_xb", got_b2), ("back_xa", got_a1),
            ("back_yb", got_b1), ("cross", g_ref.at[h]), ("facet", other), ("vis", vis_all.at[h]),
            ("cells", vis_all.at[h, : chips - 1]), ("values", pair_vals),
            ("answers", slots.at[: chips - 1]),
        ):
            sentall(kind, like)


def main(ro, co, sub, u, v, obs, facet, scale):
    _, _, nx, ny, nz = geometry()
    chips = nx * ny * nz
    fs = facet.shape[0]
    nv = obs.shape[1]
    rows_own = NR * SG // chips
    hr = rows_own // 2
    hlong = nz * hr
    wide = SG // 2
    plan, total = semaphores()
    dma = pltpu.SemaphoreType.DMA
    return pl.pallas_call(
        functools.partial(main_kernel, scale),
        out_shape=[
            jax.ShapeDtypeStruct((fs, fs), f32),
            jax.ShapeDtypeStruct((fs, SG), bf16),
            jax.ShapeDtypeStruct((NC, 2, SG, fs), bf16),
            jax.ShapeDtypeStruct((2, nv), f32),
        ],
        in_specs=[HB] * 7,
        out_specs=[VM] * 4,
        scratch_shapes=[
            pltpu.VMEM((fs, fs), bf16),
            pltpu.SMEM((NR,), i32),
            pltpu.SMEM((NC,), i32),
            pltpu.VMEM((1, nv), i32),
            pltpu.VMEM((1, nv), i32),
            pltpu.VMEM((1, nv), i32),
            pltpu.VMEM((2, nv), f32),
            pltpu.VMEM((SG, SG), bf16),
            pltpu.VMEM((SG, SG), bf16),
            pltpu.VMEM((SG, 2 * fs), bf16),
            pltpu.VMEM((SG, 2 * fs), bf16),
            pltpu.VMEM((2, 2, nx * ny * hlong, 2 * fs), bf16),
            pltpu.VMEM((2 * fs, SG), bf16),
            pltpu.VMEM((4, nv), f32),
            pltpu.VMEM((2, chips, 4, nv), f32),
            pltpu.VMEM((fs, fs), bf16),
            pltpu.VMEM((4, 2, nx, ny, hlong, wide), f32),
            pltpu.VMEM((4, 2, nx, ny, hlong, wide), bf16),
            pltpu.VMEM((2, 4, 2, nx, ny, hlong, wide), bf16),
            pltpu.VMEM((3 * rows_own, SG), f32),
            pltpu.VMEM((4, ny, hlong, wide), f32),
            pltpu.VMEM((4, nx, hlong, wide), f32),
            pltpu.VMEM((4, ny, hlong, wide), bf16),
            pltpu.VMEM((4, nx, hlong, wide), bf16),
            pltpu.VMEM((4, nx - 1, ny, hlong, wide), bf16),
            pltpu.VMEM((4, ny - 1, nx, hlong, wide), bf16),
            pltpu.VMEM((4, ny - 1, hlong, wide), bf16),
            pltpu.VMEM((4, nx - 1, hlong, wide), bf16),
            pltpu.VMEM((4, nz, hr, SG), f32),
            pltpu.VMEM((4, nz, hr, SG), bf16),
            pltpu.VMEM((4, nz - 1, hr, SG), bf16),
            pltpu.VMEM((4, nz, hr, SG), bf16),
            pltpu.VMEM((2 * rows_own, SG), f32),
            pltpu.VMEM((2, chips, 2, nv), f32),
            pltpu.VMEM((chips, 2, nv), f32),
            pltpu.VMEM((chips, 2, nv), f32),
            dma((len(plan),)),
            dma((total,)),
            dma((8,)),
        ],
        compiler_params=pltpu.CompilerParams(
            collective_id=0, has_side_effects=True, vmem_limit_bytes=LIMIT
        ),
        name="cycle",
    )(*(pltpu.with_memory_space_constraint(a, pltpu.HBM) for a in (facet, ro, co, sub, u, v, obs)))


def finish_kernel(scale, acc_ref, last_ref, bt_ref, res_ref, image_hbm, out_hbm, buf, sem):
    _, h, _, _ = position()
    fs = acc_ref.shape[0]
    pieces = 4
    step = fs // pieces
    copies = [pltpu.make_async_copy(res_ref, out_hbm, sem.at[pieces])]
    copies[0].start()
    b = bt_ref[1 - h, 1]
    for k in range(pieces):
        cut = slice(k * step, (k + 1) * step)
        buf[cut] = (acc_ref[cut] + jnp.dot(last_ref[cut], b, preferred_element_type=f32)) * scale
        copies.append(pltpu.make_async_copy(buf.at[cut], image_hbm.at[cut], sem.at[k]))
        copies[-1].start()
    for copy in copies:
        copy.wait()


def finish(acc, last, bt, res, scale):
    fs = acc.shape[0]
    return pl.pallas_call(
        functools.partial(finish_kernel, scale),
        out_shape=[jax.ShapeDtypeStruct((fs, fs), f32), jax.ShapeDtypeStruct(res.shape, f32)],
        in_specs=[VM] * 4,
        out_specs=[HB] * 2,
        scratch_shapes=[pltpu.VMEM((fs, fs), f32), pltpu.SemaphoreType.DMA((5,))],
        compiler_params=pltpu.CompilerParams(vmem_limit_bytes=4 << 20),
        name="finish",
    )(acc, last, bt, res)


def shards(facet_image, row_offsets, col_offsets, vis_subgrid, vis_u, vis_v, observed):
    rows, cols, _, _, _ = geometry()
    fs = facet_image.shape[0]
    scale_in = 1.0 / (fs * math.sqrt(rows * cols))
    scale_out = 1.0 / (SG * math.sqrt(NR * NC))
    acc, last, bt, residual = main(
        row_offsets, col_offsets, vis_subgrid[None], vis_u[None], vis_v[None],
        observed, facet_image, scale_in / SG,
    )
    return tuple(finish(acc, last, bt, residual, scale_out / SG))


def solution(mesh):
    in_specs = (
        P("frow", "fcol"),
        P(),
        P(),
        P(("frow", "fcol")),
        P(("frow", "fcol")),
        P(("frow", "fcol")),
        P(None, ("frow", "fcol")),
    )
    out_specs = (P("frow", "fcol"), P(None, ("frow", "fcol")))
    return jax.shard_map(shards, mesh=mesh, in_specs=in_specs, out_specs=out_specs, check_vma=False)
```

```python
import functools
import math

import jax
import jax.numpy as jnp
from jax import lax
from jax.experimental import pallas as pl
from jax.experimental.pallas import tpu as pltpu
from jax.sharding import PartitionSpec as P

SKY = 65536
SG = 256
NR = 2
NC = 2
f32 = jnp.float32
bf16 = jnp.bfloat16
i32 = jnp.int32
MESH = pl.DeviceIdType.MESH
VM = pl.BlockSpec(memory_space=pltpu.VMEM)
HB = pl.BlockSpec(memory_space=pltpu.HBM)
LIMIT = 32 << 20
ORDER = (
    "p:0", "p:1", "v", "p:2", "p:3",
    "bt", "g:2", "r:0", "r:1", "r:2", "r:3",
    "g:6", "t:0", "t:1", "t:2", "t:3",
    "d:6", "b:0", "b:1", "b:2", "b:3",
    "d:2", "ans", "f:0", "f:1", "own0",
    "f:2", "f:3", "own1", "c:0", "c:1",
    "oth0", "res", "c:2", "c:3",
)

scope = jax.named_scope


def geometry():
    rows = lax.axis_size("frow")
    cols = lax.axis_size("fcol")
    nx = rows // 2
    ny = 1 << ((cols.bit_length() - 1) // 2)
    nz = cols // ny
    return rows, cols, nx, ny, nz


def position():
    _, _, _, ny, _ = geometry()
    frow = lax.axis_index("frow")
    fcol = lax.axis_index("fcol")
    return frow // 2, frow % 2, fcol % ny, fcol // ny


def phase(product):
    k = product & (SKY - 1)
    quarter = lax.shift_right_logical(k + SKY // 8, SKY.bit_length() - 3)
    t = (k - quarter * (SKY // 4)).astype(f32) * (2.0 * math.pi / SKY)
    t2 = t * t
    cos = 1.0 + t2 * (-1 / 2 + t2 * (1 / 24 + t2 * (-1 / 720 + t2 * (1 / 40320))))
    sin = t * (1.0 + t2 * (-1 / 6 + t2 * (1 / 120 + t2 * (-1 / 5040 + t2 * (1 / 362880)))))
    odd = (quarter & 1) == 1
    c = jnp.where(odd, sin, cos)
    s = jnp.where(odd, cos, sin)
    return jnp.where(((quarter + 1) & 2) == 0, c, -c), jnp.where((quarter & 2) == 0, s, -s)


def expand(first, places, c_ref, s_ref):
    n = places.shape[1]
    steps = lax.broadcasted_iota(i32, (16, n), 0)
    c0, s0 = phase(steps * places)
    c1, s1 = phase((first + 16 * steps) * places)
    for k in range(SG // 16):
        ck = c1[k : k + 1]
        sk = s1[k : k + 1]
        c_ref[k * 16 : k * 16 + 16, :] = (ck * c0 - sk * s0).astype(bf16)
        s_ref[k * 16 : k * 16 + 16, :] = (sk * c0 + ck * s0).astype(bf16)


def place(q):
    _, _, _, ny, nz = geometry()
    return lax.div(q, ny * nz), lax.rem(lax.div(q, nz), ny), lax.rem(q, nz)


def device(q, h):
    _, _, _, ny, _ = geometry()
    x, y, z = place(q)
    return (2 * x + h, z * ny + y)


def hots(vis, owned, lanes):
    v = jnp.broadcast_to(vis[1:2].astype(bf16), lanes.shape)
    return owned == vis[0:1], jnp.where(lanes == v, jnp.ones_like(v), jnp.zeros_like(v))


def semaphores():
    plan = {}
    total = 0
    for at, kind in enumerate((
        "plane", "z", "back_z", "back_plane", "cross",
        "facet", "cells", "cells_z", "pair", "pair_z", "values", "answers",
    )):
        count = 4 if at < 5 else 1
        plan[kind] = (at, total, count)
        total += count
    return plan, total


def spread_rows(g_ref, a_tab, c, q, cut):
    wide = g_ref.shape[-1]
    tall = a_tab.shape[1] * a_tab.shape[2]
    first = (((0,), (0,)), ((), ()))
    g = [
        jnp.concatenate([g_ref[c, 2 * q + e, :, :, p].reshape(tall // 2, wide) for e in range(2)], 0)
        for p in range(2)
    ]
    g = jnp.concatenate(g, 1)
    one, two = (
        lax.dot_general(a_tab[p, :, :, cut].reshape(tall, cut.size), g, first, preferred_element_type=f32)
        for p in range(2)
    )
    return jnp.concatenate([one[:, :wide] + two[:, wide:], one[:, wide:] - two[:, :wide]], 1).astype(bf16)


def main_kernel(
    scale, facet_hbm, ro_hbm, co_hbm, sub_hbm, u_hbm, v_hbm, obs_hbm,
    acc_ref, g_ref, a_tab, bt_ref, res_ref,
    facet_ref, ro_ref, co_ref, sub_ref, u_ref, v_ref, obs_ref,
    kl, rc, rs, keep_col, keep_row, p_ref, vis_all, other, z_ref, zb_ref, grid_acc, lanes,
    got, own_z, send_z, got_z, gz, model, vals, pair_vals, slots,
    ssem, rsem, lsem,
):
    rows, cols, nx, ny, nz = geometry()
    x, h, y, z = position()
    chips = nx * ny * nz
    me = (x * ny + y) * nz + z
    fs = facet_ref.shape[0]
    nv = obs_ref.shape[1]
    rows_own = NR * SG // chips
    hr = rows_own // 2
    hlong = nz * hr
    part = 2 * hlong
    wide = SG // 2
    waves = range(4)
    sib = (2 * x + 1 - h, lax.axis_index("fcol"))
    barrier = pltpu.get_barrier_semaphore()

    plane = [(dx, dy) for dx in range(nx) for dy in range(ny)][1:]

    def across(k):
        px, py = lax.rem(x + plane[k][0], nx), lax.rem(y + plane[k][1], ny)
        return px, py, (2 * px + h, z * ny + py)

    def to_z(d):
        return 2 * x + h, lax.rem(z + d, nz) * ny + y

    own_xy = x * ny + y
    near = [sib] + [across(k)[2] for k in range(nx * ny - 1)]
    near += [to_z(d) for d in range(1, nz)]
    for to in near:
        pl.semaphore_signal(barrier, inc=1, device_id=to, device_id_type=MESH)

    def peers(act):
        if chips > 16:
            def step(d, carry):
                to = lax.rem(me + d, chips)
                px, py, pz = place(to)
                act(pz, px * ny + py, to, (2 * px + h, pz * ny + py))
                return carry

            lax.fori_loop(1, chips, step, 0)
            return
        for dx in range(nx):
            for dy in range(ny):
                for dz in range(nz):
                    if dx + dy + dz > 0:
                        px = lax.rem(x + dx, nx)
                        py = lax.rem(y + dy, ny)
                        pz = lax.rem(z + dz, nz)
                        act(pz, px * ny + py, (px * ny + py) * nz + pz, (2 * px + h, pz * ny + py))

    loads = []
    for k, (src, dst) in enumerate((
        (ro_hbm, ro_ref), (co_hbm, co_ref), (sub_hbm, sub_ref), (u_hbm, u_ref), (v_hbm, v_ref),
        (obs_hbm, obs_ref), (facet_hbm, facet_ref),
    )):
        loads.append(pltpu.make_async_copy(src, dst, lsem.at[k]))
        loads[-1].start()
    plan = semaphores()[0]

    def send(kind, w, src, dst, to):
        at, base, _ = plan[kind]
        pltpu.make_async_remote_copy(
            src, dst, ssem.at[at], rsem.at[base + w], device_id=to, device_id_type=MESH
        ).start()

    def land(kind, w, like):
        at, base, _ = plan[kind]
        pltpu.make_async_remote_copy(
            like, like, ssem.at[at], rsem.at[base + w], device_id=sib, device_id_type=MESH
        ).wait_recv()

    def sentall(kind, like):
        at, base, _ = plan[kind]
        pltpu.make_async_remote_copy(
            like, like, ssem.at[at], rsem.at[base], device_id=sib, device_id_type=MESH
        ).wait_send()

    with scope("expandK"):
        expand(0, lax.broadcasted_iota(i32, (1, SG), 1) * (SKY // SG), kl.at[0, :SG], kl.at[0, SG:])
        kl[1, :SG] = kl[0, SG:]
        kl[1, SG:] = -kl[0, :SG]

    def compose(n, places, keep):
        expand(0, places, rc.at[:, :n], rs.at[:, :n])
        for cut in (slice(0, n // 2), slice(n // 2, n)):
            both = jnp.dot(kl[0], rc[:, cut], preferred_element_type=f32)
            both += jnp.dot(kl[1], rs[:, cut], preferred_element_type=f32)
            keep[:, cut] = both

    def shifted(re, im, places, offset):
        cos, sin = phase(offset * places)
        return (re * cos + im * sin).astype(bf16), (im * cos - re * sin).astype(bf16)

    col_places = (lax.axis_index("fcol") * fs + lax.broadcasted_iota(i32, (1, fs), 1)) * (SKY // (cols * fs))
    row_places = (x * (2 * fs) + lax.broadcasted_iota(i32, (1, 2 * fs), 1)) * (SKY // (rows * fs))

    def columns(c):
        re, im = shifted(keep_col[:SG], keep_col[SG:], col_places, co_ref[c])
        for q in range(2):
            bt_ref[c, q, :wide] = re[q * wide : (q + 1) * wide]
            bt_ref[c, q, wide:] = im[q * wide : (q + 1) * wide]

    with scope("composeB"):
        compose(fs, col_places, keep_col)
        loads[0].wait()
        loads[1].wait()
        columns(h)
    with scope("cells"):
        for copy in loads[2:6]:
            copy.wait()
        sub = sub_ref[...]
        row = (lax.rem(sub, NC) * NR + lax.div(sub, NC)) * SG + u_ref[...]
        vis_all[h, z, own_xy, 0:1] = row.astype(f32)
        vis_all[h, z, own_xy, 1:2] = v_ref[...].astype(f32)
        vis_all[h, z, own_xy, 2:4] = obs_ref[...]
    with scope("barwait"):
        pl.semaphore_wait(barrier, len(near))
    for k in range(nx * ny - 1):
        mine = vis_all.at[h, z, own_xy]
        send("cells", 0, mine, mine, across(k)[2])
    send("facet", 0, facet_hbm, other, sib)
    with scope("composeA"):
        compose(2 * fs, row_places, keep_row)
        for r in range(NR):
            pair = shifted(keep_row[:SG], keep_row[SG:], row_places, ro_ref[r])
            for b in range(SG // part):
                blk = r * (SG // part) + b
                for e in range(2):
                    for p in range(2):
                        cut = slice(b * part + e * hlong, b * part + (e + 1) * hlong)
                        a_tab[p, e, blk * hlong : (blk + 1) * hlong] = pair[p][cut]
    loads[6].wait()

    def project(ref, q, base):
        step = fs // 2
        for k in range(2):
            got = lax.dot_general(
                ref[k * step : (k + 1) * step], bt_ref[h, q], (((1,), (1,)), ((), ())),
                preferred_element_type=f32,
            )
            p_ref[pl.ds(pl.multiple_of(base + k * step, step), step)] = got.astype(bf16)

    own_cut = pl.ds(pl.multiple_of(h * fs, fs), fs)

    def produce(w):
        q, e = w // 2, w % 2
        if e == 0:
            project(facet_ref, q, h * fs)
            if q == 0:
                land("facet", 0, other)
            project(other, q, (1 - h) * fs)
        one = jnp.dot(a_tab[0, e], p_ref[...], preferred_element_type=f32)
        two = jnp.dot(a_tab[1, e], p_ref[...], preferred_element_type=f32)
        zr = (one[:, :wide] - two[:, wide:]).reshape(nx, ny, hlong, wide)
        zi = (one[:, wide:] + two[:, :wide]).reshape(nx, ny, hlong, wide)
        z_ref[w, :, :, 0] = zr
        z_ref[w, :, :, 1] = zi
        zb_ref[w, :, :, 0] = zr.astype(bf16)
        zb_ref[w, :, :, 1] = zi.astype(bf16)
        for k in range(nx * ny - 1):
            px, py, to = across(k)
            send("plane", w, zb_ref.at[w, px, py], got.at[w, k], to)

    owned_row = lax.broadcasted_iota(i32, (rows_own, nv), 0)
    owned_row = (x * ny + y) * part + z * hr + (owned_row // hr) * hlong + owned_row % hr
    owned_row = (owned_row + h * (NR * SG)).astype(f32)
    lanes[...] = lax.broadcasted_iota(i32, (SG, nv), 0).astype(f32).astype(bf16)

    def gridding(side, level):
        def one(k):
            vis = vis_all[side, level, k]
            hot_row, hot_col = hots(vis, owned_row, lanes[...])
            parts = [vis[2:3], vis[3:4], jnp.ones_like(vis[0:1])]
            left = jnp.concatenate([jnp.where(hot_row, t, 0.0) for t in parts], 0).astype(bf16)
            return lax.dot_general(left, hot_col, (((1,), (1,)), ((), ())), preferred_element_type=f32)

        def body(t, carry):
            grid_acc[0] += one(2 * t)
            grid_acc[1] += one(2 * t + 1)
            return carry

        lax.fori_loop(0, nx * ny // 2, body, 0)

    def reduce(w):
        land("plane", w, got.at[w])
        total = z_ref[w, x, y]
        for k in range(nx * ny - 1):
            total = total + got[w, k].astype(f32)
        for k in range(nz):
            for p in range(2):
                rows_k = total[p, k * hr : (k + 1) * hr]
                own_z[w, k, :, p * wide : (p + 1) * wide] = rows_k
                send_z[w, k, :, p * wide : (p + 1) * wide] = rows_k.astype(bf16)
        for d in range(1, nz):
            send("z", w, send_z.at[w, lax.rem(z + d, nz)], got_z.at[w, d - 1], to_z(d))

    def turn(w):
        q, e = w // 2, w % 2
        land("z", w, got_z.at[w])
        total = own_z[w, z]
        for d in range(nz - 1):
            total = total + got_z[w, d].astype(f32)
        m = total * scale
        cut = slice(q * wide, (q + 1) * wide)
        rows_of = [slice(p * rows_own + e * hr, p * rows_own + (e + 1) * hr) for p in range(3)]
        sums = [grid_acc[0, k, cut] + grid_acc[1, k, cut] for k in rows_of]
        hat_re = sums[0] - sums[2] * m[:, :wide]
        hat_im = sums[1] - sums[2] * m[:, wide:]
        gz[w, z, :, :wide] = hat_re.astype(bf16)
        gz[w, z, :, wide:] = hat_im.astype(bf16)
        for d in range(1, nz):
            send("back_z", w, gz.at[w, z], gz.at[w, z], to_z(d))
        model[e * hr : (e + 1) * hr, cut] = m[:, :wide]
        model[rows_own + e * hr : rows_own + (e + 1) * hr, cut] = m[:, wide:]

    def over(w, px, py):
        src = g_ref.at[h, w, px, py]
        send("cross", w, src, src, sib)

    def gather(w):
        land("back_z", w, gz.at[w, : nz - 1])
        for k in range(nz):
            cut = slice(k * hr, (k + 1) * hr)
            g_ref[h, w, x, y, 0, cut, :] = gz[w, k, :, :wide]
            g_ref[h, w, x, y, 1, cut, :] = gz[w, k, :, wide:]
        blk = g_ref.at[h, w, x, y]
        for k in range(nx * ny - 1):
            send("back_plane", w, blk, blk, across(k)[2])
        over(w, x, y)

    def finish(w):
        land("back_plane", w, got.at[w])
        for k in range(nx * ny - 1):
            px, py, _ = across(k)
            over(w, px, py)

    def crossed(w):
        land("cross", w, g_ref.at[1 - h, w])

    def degrid(side, level):
        m = model[...].astype(bf16)

        def one(k):
            hot_row, hot_col = hots(vis_all[side, level, k], owned_row, lanes[...])
            val = jnp.dot(m, hot_col, preferred_element_type=f32)
            vr_ = jnp.sum(jnp.where(hot_row, val[:rows_own], 0.0), 0, keepdims=True)
            vi_ = jnp.sum(jnp.where(hot_row, val[rows_own:], 0.0), 0, keepdims=True)
            return jnp.concatenate([vr_, vi_], 0)

        def body(t, carry):
            a = one(2 * t)
            b = one(2 * t + 1)
            vals[side, level, 2 * t] = a
            vals[side, level, 2 * t + 1] = b
            return carry

        lax.fori_loop(0, nx * ny // 2, body, 0)

    def spread(c, q):
        return spread_rows(g_ref, a_tab, c, q, own_cut)

    def image(c, q):
        return jnp.dot(spread(c, q), bt_ref[c, q], preferred_element_type=f32)

    grid_acc[...] = jnp.zeros_like(grid_acc)
    units = 2 * nz
    done = {"grid": 0, "degrid": 0}

    def grid(n):
        for _ in range(n * units // 8):
            k = done["grid"]
            done["grid"] += 1
            side, level = (k, 0) if k < 2 else ((k - 2) // (nz - 1), (k - 2) % (nz - 1) + 1)
            if k == 1:
                land("pair", 0, vis_all.at[1 - h, z])
            if k == 2:
                land("cells_z", 0, vis_all.at[h, : nz - 1])
                for d in range(1, nz):
                    sheet = vis_all.at[h, lax.rem(z + d, nz)]
                    send("pair_z", 0, sheet, sheet, sib)
            if k == nz + 1:
                land("pair_z", 0, vis_all.at[1 - h, : nz - 1])
            with scope("grid%d" % k):
                gridding(h if side == 0 else 1 - h, lax.rem(z + level, nz))

    def ungrid(n):
        for _ in range(n * units // 8):
            k = done["degrid"]
            done["degrid"] += 1
            with scope("degrid%d" % k):
                degrid(1 - h if k < nz else h, lax.rem(z + k % nz, nz))
            if k == nz - 1:
                send("values", 0, vals.at[1 - h], pair_vals, sib)

    def cells():
        land("cells", 0, vis_all.at[h, z, : nx * ny - 1])
        sheet = vis_all.at[h, z]
        for d in range(1, nz):
            send("cells_z", 0, sheet, sheet, to_z(d))
        send("pair", 0, sheet, sheet, sib)

    def answers():
        land("values", 0, pair_vals)
        vals[h] = vals[h] + pair_vals[...]
        peers(lambda pz, pxy, slot, to: send("answers", 0, vals.at[h, pz, pxy], slots.at[me], to))

    def result():
        land("answers", 0, slots.at[: chips - 1])
        start = vals[h, z, own_xy]
        if chips > 16:
            total = lax.fori_loop(1, chips, lambda d, t: t + slots[lax.rem(me + d, chips)], start)
        else:
            total = start
            for d in range(1, chips):
                total = total + slots[lax.rem(me + d, chips)]
        res_ref[...] = obs_ref[...] - total

    def own0():
        acc_ref[...] = image(h, 0)

    def own1():
        acc_ref[...] += image(h, 1)

    def other0():
        acc_ref[...] += image(1 - h, 0)

    acts = {
        "p": produce, "r": reduce, "t": turn, "b": gather, "f": finish, "c": crossed,
    }
    simple = {
        "v": cells, "ans": answers, "res": result, "own0": own0, "own1": own1,
        "oth0": other0, "bt": lambda: columns(1 - h),
    }
    for word in ORDER:
        name, _, arg = word.partition(":")
        if name == "g":
            grid(int(arg))
        elif name == "d":
            ungrid(int(arg))
        else:
            with scope(name + arg):
                acts[name](int(arg)) if arg else simple[name]()
    with scope("drain"):
        for kind, like in (
            ("plane", got), ("z", got_z), ("back_z", got_z), ("back_plane", got),
            ("cross", g_ref.at[h]), ("facet", other), ("cells", vis_all.at[h, z, : nx * ny - 1]),
            ("cells_z", vis_all.at[h, : nz - 1]), ("pair", vis_all.at[h, z]),
            ("pair_z", vis_all.at[h, : nz - 1]), ("values", pair_vals), ("answers", slots.at[: chips - 1]),
        ):
            sentall(kind, like)


def main(ro, co, sub, u, v, obs, facet, scale):
    _, _, nx, ny, nz = geometry()
    chips = nx * ny * nz
    fs = facet.shape[0]
    nv = obs.shape[1]
    rows_own = NR * SG // chips
    hr = rows_own // 2
    hlong = nz * hr
    wide = SG // 2
    plan, total = semaphores()
    dma = pltpu.SemaphoreType.DMA
    return pl.pallas_call(
        functools.partial(main_kernel, scale),
        out_shape=[
            jax.ShapeDtypeStruct((fs, fs), f32),
            jax.ShapeDtypeStruct((2, 4, nx, ny, 2, hlong, wide), bf16),
            jax.ShapeDtypeStruct((2, 2, nx * ny * hlong, 2 * fs), bf16),
            jax.ShapeDtypeStruct((NC, 2, SG, fs), bf16),
            jax.ShapeDtypeStruct((2, nv), f32),
        ],
        in_specs=[HB] * 7,
        out_specs=[VM] * 5,
        scratch_shapes=[
            pltpu.VMEM((fs, fs), bf16),
            pltpu.SMEM((NR,), i32),
            pltpu.SMEM((NC,), i32),
            pltpu.VMEM((1, nv), i32),
            pltpu.VMEM((1, nv), i32),
            pltpu.VMEM((1, nv), i32),
            pltpu.VMEM((2, nv), f32),
            pltpu.VMEM((2, 2 * SG, SG), bf16),
            pltpu.VMEM((SG, 2 * fs), bf16),
            pltpu.VMEM((SG, 2 * fs), bf16),
            pltpu.VMEM((2 * SG, fs), f32),
            pltpu.VMEM((2 * SG, 2 * fs), f32),
            pltpu.VMEM((2 * fs, SG), bf16),
            pltpu.VMEM((2, nz, nx * ny, 4, nv), f32),
            pltpu.VMEM((fs, fs), bf16),
            pltpu.VMEM((4, nx, ny, 2, hlong, wide), f32),
            pltpu.VMEM((4, nx, ny, 2, hlong, wide), bf16),
            pltpu.VMEM((2, 3 * rows_own, SG), f32),
            pltpu.VMEM((SG, nv), bf16),
            pltpu.VMEM((4, nx * ny - 1, 2, hlong, wide), bf16),
            pltpu.VMEM((4, nz, hr, SG), f32),
            pltpu.VMEM((4, nz, hr, SG), bf16),
            pltpu.VMEM((4, nz - 1, hr, SG), bf16),
            pltpu.VMEM((4, nz, hr, SG), bf16),
            pltpu.VMEM((2 * rows_own, SG), f32),
            pltpu.VMEM((2, nz, nx * ny, 2, nv), f32),
            pltpu.VMEM((nz, nx * ny, 2, nv), f32),
            pltpu.VMEM((chips, 2, nv), f32),
            dma((len(plan),)),
            dma((total,)),
            dma((8,)),
        ],
        compiler_params=pltpu.CompilerParams(
            collective_id=0, has_side_effects=True, vmem_limit_bytes=LIMIT
        ),
        name="cycle",
    )(*(pltpu.with_memory_space_constraint(a, pltpu.HBM) for a in (facet, ro, co, sub, u, v, obs)))


def finish_kernel(scale, acc_ref, g_ref, a_tab, bt_ref, res_ref, image_hbm, out_hbm, buf, sem):
    _, h, _, _ = position()
    fs = acc_ref.shape[0]
    pieces = sem.shape[0] - 1
    step = fs // pieces
    copies = [pltpu.make_async_copy(res_ref, out_hbm, sem.at[pieces])]
    copies[0].start()
    for k in range(pieces):
        cut = slice(k * step, (k + 1) * step)
        u = spread_rows(g_ref, a_tab, 1 - h, 1, pl.ds(pl.multiple_of(h * fs + k * step, step), step))
        buf[cut] = (acc_ref[cut] + jnp.dot(u, bt_ref[1 - h, 1], preferred_element_type=f32)) * scale
        copies.append(pltpu.make_async_copy(buf.at[cut], image_hbm.at[cut], sem.at[k]))
        copies[-1].start()
    for copy in copies:
        copy.wait()


def finish(acc, g, a_tab, bt, res, scale):
    fs = acc.shape[0]
    return pl.pallas_call(
        functools.partial(finish_kernel, scale),
        out_shape=[jax.ShapeDtypeStruct((fs, fs), f32), jax.ShapeDtypeStruct(res.shape, f32)],
        in_specs=[VM] * 5,
        out_specs=[HB] * 2,
        scratch_shapes=[pltpu.VMEM((fs, fs), f32), pltpu.SemaphoreType.DMA((3,))],
        compiler_params=pltpu.CompilerParams(vmem_limit_bytes=6 << 20),
        name="finish",
    )(acc, g, a_tab, bt, res)


def shards(facet_image, row_offsets, col_offsets, vis_subgrid, vis_u, vis_v, observed):
    rows, cols, _, _, _ = geometry()
    fs = facet_image.shape[0]
    scale_in = 1.0 / (fs * math.sqrt(rows * cols))
    scale_out = 1.0 / (SG * math.sqrt(NR * NC))
    acc, g, a_tab, bt, residual = main(
        row_offsets, col_offsets, vis_subgrid[None], vis_u[None], vis_v[None],
        observed, facet_image, scale_in / SG,
    )
    return tuple(finish(acc, g, a_tab, bt, residual, scale_out / SG))


def solution(mesh):
    in_specs = (
        P("frow", "fcol"),
        P(),
        P(),
        P(("frow", "fcol")),
        P(("frow", "fcol")),
        P(("frow", "fcol")),
        P(None, ("frow", "fcol")),
    )
    out_specs = (P("frow", "fcol"), P(None, ("frow", "fcol")))
    return jax.shard_map(shards, mesh=mesh, in_specs=in_specs, out_specs=out_specs, check_vma=False)
```

```python
import functools
import math

import jax
import jax.numpy as jnp
from jax import lax
from jax.experimental import pallas as pl
from jax.experimental.pallas import tpu as pltpu
from jax.sharding import PartitionSpec as P

SKY = 65536
SG = 256
NR = 2
NC = 2
f32 = jnp.float32
bf16 = jnp.bfloat16
i32 = jnp.int32
MESH = pl.DeviceIdType.MESH
VM = pl.BlockSpec(memory_space=pltpu.VMEM)
HB = pl.BlockSpec(memory_space=pltpu.HBM)
LIMIT = 32 << 20
ORDER = (
    "p:0", "rows1", "p:1", "v", "cols1",
    "p:2", "p:3", "bt", "g:1", "r:0",
    "r:1", "g:1", "r:2", "g:2", "x", "r:3",
    "t:0", "t:1", "t:2", "t:3", "m",
    "b:0", "d:1", "b:1", "d:1", "b:2", "d:2",
    "ans", "b:3", "f:0", "own:0", "f:1", "own:1",
    "c:0", "oth:0", "f:2", "own:2", "c:1", "oth:1",
    "res", "f:3", "c:2", "oth:2",
    "own:3", "c:3",
)

scope = jax.named_scope


def geometry():
    rows = lax.axis_size("frow")
    cols = lax.axis_size("fcol")
    nx = rows // 2
    ny = 1 << ((cols.bit_length() - 1) // 2)
    nz = cols // ny
    return rows, cols, nx, ny, nz


def position():
    _, _, _, ny, _ = geometry()
    frow = lax.axis_index("frow")
    fcol = lax.axis_index("fcol")
    return frow // 2, frow % 2, fcol % ny, fcol // ny


def phase(product):
    k = product & (SKY - 1)
    quarter = lax.shift_right_logical(k + SKY // 8, SKY.bit_length() - 3)
    t = (k - quarter * (SKY // 4)).astype(f32) * (2.0 * math.pi / SKY)
    t2 = t * t
    cos = 1.0 + t2 * (-1 / 2 + t2 * (1 / 24 + t2 * (-1 / 720 + t2 * (1 / 40320))))
    sin = t * (1.0 + t2 * (-1 / 6 + t2 * (1 / 120 + t2 * (-1 / 5040 + t2 * (1 / 362880)))))
    odd = (quarter & 1) == 1
    c = jnp.where(odd, sin, cos)
    s = jnp.where(odd, cos, sin)
    return jnp.where(((quarter + 1) & 2) == 0, c, -c), jnp.where((quarter & 2) == 0, s, -s)


def expand(first, places, c_ref, s_ref):
    n = places.shape[1]
    steps = lax.broadcasted_iota(i32, (16, n), 0)
    c0, s0 = phase(steps * places)
    c1, s1 = phase((first + 16 * steps) * places)
    for k in range(SG // 16):
        ck = c1[k : k + 1]
        sk = s1[k : k + 1]
        c_ref[k * 16 : k * 16 + 16, :] = (ck * c0 - sk * s0).astype(bf16)
        s_ref[k * 16 : k * 16 + 16, :] = (sk * c0 + ck * s0).astype(bf16)


def place(q):
    _, _, _, ny, nz = geometry()
    return lax.div(q, ny * nz), lax.rem(lax.div(q, nz), ny), lax.rem(q, nz)


def device(q, h):
    _, _, _, ny, _ = geometry()
    x, y, z = place(q)
    return (2 * x + h, z * ny + y)


def hots(vis, owned, lanes):
    n = lanes.shape[1]
    parts = []
    for t in range(0, vis.shape[1], n):
        v = jnp.broadcast_to(vis[1:2, t : t + n].astype(bf16), lanes.shape)
        parts.append(jnp.where(lanes == v, jnp.ones_like(v), jnp.zeros_like(v)))
    return owned == vis[0:1], jnp.concatenate(parts, 1)


def pairs(count, body):
    if count <= 4:
        for t in range(0, count, 2):
            body(t)
        return

    def step(t, carry):
        body(2 * t)
        return carry

    lax.fori_loop(0, count // 2, step, 0)


def semaphores():
    plan = {}
    total = 0
    for at, kind in enumerate((
        "plane", "z", "back_z", "back_plane", "cross",
        "facet", "cells", "cells_z", "sums", "model", "answers",
    )):
        count = 4 if at < 5 else 1
        plan[kind] = (at, total, count)
        total += count
    return plan, total


def spread_rows(g_ref, a_tab, c, w, cut):
    wide = g_ref.shape[-1]
    tall = a_tab.shape[2]
    e = w % 2
    first = (((0,), (0,)), ((), ()))
    g = jnp.concatenate([g_ref[c, w, :, :, p].reshape(tall, wide) for p in range(2)], 1)
    one, two = (
        lax.dot_general(a_tab[p, e, :, cut], g, first, preferred_element_type=f32) for p in range(2)
    )
    return jnp.concatenate([one[:, :wide] + two[:, wide:], one[:, wide:] - two[:, :wide]], 1)


def main_kernel(
    scale, facet_hbm, ro_hbm, co_hbm, sub_hbm, u_hbm, v_hbm, obs_hbm,
    acc_ref, g_ref, a_tab, bt_ref, res_ref, half_u,
    facet_ref, ro_ref, co_ref, sub_ref, u_ref, v_ref, obs_ref,
    kk, ks, kcol, krow, cc, cs, rc, rs, keep_col, keep_row, p_ref, vis_all, other, z_ref, zb_ref, grid_acc, own_sum, pair_sum, got_sum, own_model, got_model, lanes,
    got, own_z, send_z, got_z, gz, model, vals, slots,
    ssem, rsem, lsem,
):
    rows, cols, nx, ny, nz = geometry()
    x, h, y, z = position()
    chips = nx * ny * nz
    me = (x * ny + y) * nz + z
    fs = facet_ref.shape[0]
    nv = obs_ref.shape[1]
    rows_own = NR * SG // chips
    hr = rows_own // 2
    hlong = nz * hr
    part = 2 * hlong
    wide = SG // 2
    waves = range(4)
    sib = (2 * x + 1 - h, lax.axis_index("fcol"))
    barrier = pltpu.get_barrier_semaphore()

    plane = [(dx, dy) for dx in range(nx) for dy in range(ny)][1:]

    def across(k):
        px, py = lax.rem(x + plane[k][0], nx), lax.rem(y + plane[k][1], ny)
        return px, py, (2 * px + h, z * ny + py)

    def to_z(d):
        return 2 * x + h, lax.rem(z + d, nz) * ny + y

    own_xy = x * ny + y
    near = [sib] + [across(k)[2] for k in range(nx * ny - 1)]
    near += [to_z(d) for d in range(1, nz)]
    for to in near:
        pl.semaphore_signal(barrier, inc=1, device_id=to, device_id_type=MESH)

    def peers(act):
        if chips > 16:
            def step(d, carry):
                to = lax.rem(me + d, chips)
                px, py, pz = place(to)
                act(pz, px * ny + py, to, (2 * px + h, pz * ny + py))
                return carry

            lax.fori_loop(1, chips, step, 0)
            return
        for dx in range(nx):
            for dy in range(ny):
                for dz in range(nz):
                    if dx + dy + dz > 0:
                        px = lax.rem(x + dx, nx)
                        py = lax.rem(y + dy, ny)
                        pz = lax.rem(z + dz, nz)
                        act(pz, px * ny + py, (px * ny + py) * nz + pz, (2 * px + h, pz * ny + py))

    loads = []
    for k, (src, dst) in enumerate((
        (ro_hbm, ro_ref), (co_hbm, co_ref), (sub_hbm, sub_ref), (u_hbm, u_ref), (v_hbm, v_ref),
        (obs_hbm, obs_ref), (facet_hbm, facet_ref),
    )):
        loads.append(pltpu.make_async_copy(src, dst, lsem.at[k]))
        loads[-1].start()
    plan = semaphores()[0]

    def send(kind, w, src, dst, to):
        at, base, _ = plan[kind]
        pltpu.make_async_remote_copy(
            src, dst, ssem.at[at], rsem.at[base + w], device_id=to, device_id_type=MESH
        ).start()

    def land(kind, w, like):
        at, base, _ = plan[kind]
        pltpu.make_async_remote_copy(
            like, like, ssem.at[at], rsem.at[base + w], device_id=sib, device_id_type=MESH
        ).wait_recv()

    def sentall(kind, like):
        at, base, _ = plan[kind]
        pltpu.make_async_remote_copy(
            like, like, ssem.at[at], rsem.at[base], device_id=sib, device_id_type=MESH
        ).wait_send()

    with scope("expandK"):
        expand(0, lax.broadcasted_iota(i32, (1, SG), 1) * (SKY // SG), kk, ks)
        for q in range(2):
            cut = slice(q * wide, (q + 1) * wide)
            kcol[0, q, :wide] = kk[cut]
            kcol[0, q, wide:] = ks[cut]
            kcol[1, q, :wide] = ks[cut]
            kcol[1, q, wide:] = -kk[cut]
    col_places = (lax.axis_index("fcol") * fs + lax.broadcasted_iota(i32, (1, fs), 1)) * (SKY // (cols * fs))
    row_places = (x * (2 * fs) + lax.broadcasted_iota(i32, (1, 2 * fs), 1)) * (SKY // (rows * fs))

    def compose(k0, k1, c_ref, s_ref, out):
        n = c_ref.shape[1]
        for cut in (slice(0, n // 2), slice(n // 2, n)):
            both = jnp.dot(k0, c_ref[:, cut], preferred_element_type=f32)
            both += jnp.dot(k1, s_ref[:, cut], preferred_element_type=f32)
            out[:, cut] = both

    def shifted(both, places, offset):
        cos, sin = phase(offset * places)
        re = both[:wide]
        im = both[wide:]
        return (re * cos + im * sin).astype(bf16), (im * cos - re * sin).astype(bf16)

    def columns(c, q):
        bt_ref[c, q, :wide], bt_ref[c, q, wide:] = shifted(keep_col[q], col_places, co_ref[c])

    def columns_half(q):
        compose(kcol[0, q], kcol[1, q], cc, cs, keep_col.at[q])
        columns(h, q)

    def rows_half(e):
        compose(krow[0, e], krow[1, e], rc, rs, keep_row)
        for r in range(NR):
            cut = slice(r * wide, (r + 1) * wide)
            a_tab[0, e, cut], a_tab[1, e, cut] = shifted(keep_row[...], row_places, ro_ref[r])

    with scope("columns0"):
        expand(0, col_places, cc, cs)
        loads[0].wait()
        loads[1].wait()
        columns_half(0)
    with scope("cells"):
        for copy in loads[2:6]:
            copy.wait()
        sub = sub_ref[...]
        row = (lax.rem(sub, NC) * NR + lax.div(sub, NC)) * SG + u_ref[...]
        vis_all[z, own_xy, 0:1] = row.astype(f32)
        vis_all[z, own_xy, 1:2] = v_ref[...].astype(f32)
        vis_all[z, own_xy, 2:4] = obs_ref[...]
    with scope("barwait"):
        pl.semaphore_wait(barrier, len(near))
    send("facet", 0, facet_hbm, other, sib)
    for k in range(nx * ny - 1):
        mine = vis_all.at[z, own_xy]
        send("cells", 0, mine, mine, across(k)[2])
    with scope("rows0"):
        for e in range(2):
            for b in range(SG // part):
                src = slice(b * part + e * hlong, b * part + (e + 1) * hlong)
                dst = slice(b * hlong, (b + 1) * hlong)
                low = slice(wide + b * hlong, wide + (b + 1) * hlong)
                krow[0, e, dst] = kk[src]
                krow[0, e, low] = ks[src]
                krow[1, e, dst] = ks[src]
                krow[1, e, low] = -kk[src]
        expand(0, row_places, rc, rs)
        rows_half(0)
    loads[6].wait()

    def project(ref, q, base):
        step = fs // 2
        for k in range(2):
            got = lax.dot_general(
                ref[k * step : (k + 1) * step], bt_ref[h, q], (((1,), (1,)), ((), ())),
                preferred_element_type=f32,
            )
            p_ref[pl.ds(pl.multiple_of(base + k * step, step), step)] = got.astype(bf16)

    own_cut = pl.ds(pl.multiple_of(h * fs, fs), fs)

    def produce(w):
        q, e = w // 2, w % 2
        if e == 0:
            project(facet_ref, q, h * fs)
            if q == 0:
                land("facet", 0, other)
            project(other, q, (1 - h) * fs)
        one = jnp.dot(a_tab[0, e], p_ref[...], preferred_element_type=f32)
        two = jnp.dot(a_tab[1, e], p_ref[...], preferred_element_type=f32)
        zr = (one[:, :wide] - two[:, wide:]).reshape(nx, ny, hlong, wide)
        zi = (one[:, wide:] + two[:, :wide]).reshape(nx, ny, hlong, wide)
        z_ref[w, :, :, 0] = zr
        z_ref[w, :, :, 1] = zi
        zb_ref[w, :, :, 0] = zr.astype(bf16)
        zb_ref[w, :, :, 1] = zi.astype(bf16)
        for k in range(nx * ny - 1):
            px, py, to = across(k)
            send("plane", w, zb_ref.at[w, px, py], got.at[w, k], to)

    owned_row = lax.broadcasted_iota(i32, (2 * rows_own, nv), 0)
    column = owned_row // rows_own
    column = h + column - 2 * h * column
    owned_row = owned_row % rows_own
    owned_row = (x * ny + y) * part + z * hr + (owned_row // hr) * hlong + owned_row % hr
    owned_row = (owned_row + column * (NR * SG)).astype(f32)
    lanes[...] = lax.broadcasted_iota(i32, lanes.shape, 0).astype(f32).astype(bf16)

    def gridding(level):
        def one(k):
            vis = vis_all[level, k]
            hot_row, hot_col = hots(vis, owned_row, lanes[...])
            parts = [vis[2:3], vis[3:4], jnp.ones_like(vis[0:1])]
            left = jnp.concatenate([jnp.where(hot_row, t, 0.0) for t in parts], 0).astype(bf16)
            return lax.dot_general(left, hot_col, (((1,), (1,)), ((), ())), preferred_element_type=f32)

        def body(k):
            grid_acc[0] += one(k)
            grid_acc[1] += one(k + 1)

        pairs(nx * ny, body)

    def reduce(w):
        land("plane", w, got.at[w])
        total = z_ref[w, x, y]
        for k in range(nx * ny - 1):
            total = total + got[w, k].astype(f32)
        for k in range(nz):
            for p in range(2):
                rows_k = total[p, k * hr : (k + 1) * hr]
                own_z[w, k, :, p * wide : (p + 1) * wide] = rows_k
                send_z[w, k, :, p * wide : (p + 1) * wide] = rows_k.astype(bf16)
        for d in range(1, nz):
            send("z", w, send_z.at[w, lax.rem(z + d, nz)], got_z.at[w, d - 1], to_z(d))

    def turn(w):
        q, e = w // 2, w % 2
        if w == 0:
            land("sums", 0, got_sum)
        land("z", w, got_z.at[w])
        total = own_z[w, z]
        for d in range(nz - 1):
            total = total + got_z[w, d].astype(f32)
        m = total * scale
        cut = slice(q * wide, (q + 1) * wide)
        half = slice(e * hr, (e + 1) * hr)
        sums = [own_sum[p, half, cut] + got_sum[p, half, cut] for p in range(3)]
        hat_re = sums[0] - sums[2] * m[:, :wide]
        hat_im = sums[1] - sums[2] * m[:, wide:]
        gz[w, z, :, :wide] = hat_re.astype(bf16)
        gz[w, z, :, wide:] = hat_im.astype(bf16)
        for d in range(1, nz):
            send("back_z", w, gz.at[w, z], gz.at[w, z], to_z(d))
        model[e * hr : (e + 1) * hr, cut] = m[:, :wide]
        model[rows_own + e * hr : rows_own + (e + 1) * hr, cut] = m[:, wide:]

    def over(w, px, py):
        src = g_ref.at[h, w, px, py]
        send("cross", w, src, src, sib)

    def gather(w):
        land("back_z", w, gz.at[w, : nz - 1])
        for k in range(nz):
            cut = slice(k * hr, (k + 1) * hr)
            g_ref[h, w, x, y, 0, cut, :] = gz[w, k, :, :wide]
            g_ref[h, w, x, y, 1, cut, :] = gz[w, k, :, wide:]
        blk = g_ref.at[h, w, x, y]
        for k in range(nx * ny - 1):
            send("back_plane", w, blk, blk, across(k)[2])
        over(w, x, y)

    def finish(w):
        land("back_plane", w, got.at[w])
        for k in range(nx * ny - 1):
            px, py, _ = across(k)
            over(w, px, py)

    def crossed(w):
        land("cross", w, g_ref.at[1 - h, w])

    def degrid(level):
        m = jnp.concatenate([own_model[...], got_model[...]], 0)

        def one(k):
            hot_row, hot_col = hots(vis_all[level, k], owned_row, lanes[...])
            val = jnp.dot(m, hot_col, preferred_element_type=f32)
            out = []
            for p in range(2):
                picked = [
                    jnp.where(hot_row[c * rows_own : (c + 1) * rows_own], val[(2 * c + p) * rows_own : (2 * c + p + 1) * rows_own], 0.0)
                    for c in range(2)
                ]
                out.append(jnp.sum(picked[0] + picked[1], 0, keepdims=True))
            return jnp.concatenate(out, 0)

        def body(k):
            a = one(k)
            b = one(k + 1)
            vals[level, k] = a
            vals[level, k + 1] = b

        pairs(nx * ny, body)

    def image(side, w):
        c = h if side == 0 else 1 - h
        q, e = w // 2, w % 2
        u = spread_rows(g_ref, a_tab, c, w, own_cut)
        if e == 0:
            half_u[side] = u
            return
        total = (half_u[side] + u).astype(bf16)
        got = jnp.dot(total, bt_ref[c, q], preferred_element_type=f32)
        if q == 0 and side == 0:
            acc_ref[...] = got
        else:
            acc_ref[...] += got

    grid_acc[...] = jnp.zeros_like(grid_acc)
    done = {"grid": 0, "degrid": 0}

    def grid(n):
        for _ in range(n * nz // 4):
            k = done["grid"]
            done["grid"] += 1
            if k == 1:
                land("cells_z", 0, vis_all.at[: nz - 1])
            with scope("grid%d" % k):
                gridding(lax.rem(z + k, nz))

    def exchange():
        for p in range(3):
            base = 2 * p * rows_own
            total = grid_acc[0, base : base + 2 * rows_own] + grid_acc[1, base : base + 2 * rows_own]
            own_sum[p] = total[:rows_own]
            pair_sum[p] = total[rows_own:]
        send("sums", 0, pair_sum, got_sum, sib)

    def models():
        own_model[...] = model[...].astype(bf16)
        send("model", 0, own_model, got_model, sib)

    def ungrid(n):
        for _ in range(n * nz // 4):
            k = done["degrid"]
            done["degrid"] += 1
            if k == 0:
                land("model", 0, got_model)
            with scope("degrid%d" % k):
                degrid(lax.rem(z + k, nz))

    def cells():
        land("cells", 0, vis_all.at[z, : nx * ny - 1])
        sheet = vis_all.at[z]
        for d in range(1, nz):
            send("cells_z", 0, sheet, sheet, to_z(d))

    def answers():
        peers(lambda pz, pxy, slot, to: send("answers", 0, vals.at[pz, pxy], slots.at[me], to))

    def result():
        land("answers", 0, slots.at[: chips - 1])
        start = vals[z, own_xy]
        if chips > 16:
            total = lax.fori_loop(1, chips, lambda d, t: t + slots[lax.rem(me + d, chips)], start)
        else:
            total = start
            for d in range(1, chips):
                total = total + slots[lax.rem(me + d, chips)]
        res_ref[...] = obs_ref[...] - total

    def late_columns():
        columns(1 - h, 0)
        columns(1 - h, 1)

    acts = {
        "p": produce, "r": reduce, "t": turn, "b": gather, "f": finish, "c": crossed,
        "own": lambda w: image(0, w), "oth": lambda w: image(1, w),
    }
    simple = {
        "v": cells, "ans": answers, "res": result, "x": exchange, "m": models,
        "rows1": lambda: rows_half(1), "cols1": lambda: columns_half(1), "bt": late_columns,
    }
    for word in ORDER:
        name, _, arg = word.partition(":")
        if name == "g":
            grid(int(arg))
        elif name == "d":
            ungrid(int(arg))
        else:
            with scope(name + arg):
                acts[name](int(arg)) if arg else simple[name]()
    with scope("drain"):
        for kind, like in (
            ("plane", got), ("z", got_z), ("back_z", got_z), ("back_plane", got),
            ("cross", g_ref.at[h]), ("facet", other), ("cells", vis_all.at[z, : nx * ny - 1]),
            ("cells_z", vis_all.at[: nz - 1]), ("sums", got_sum), ("model", got_model), ("answers", slots.at[: chips - 1]),
        ):
            sentall(kind, like)


def main(ro, co, sub, u, v, obs, facet, scale):
    _, _, nx, ny, nz = geometry()
    chips = nx * ny * nz
    fs = facet.shape[0]
    nv = obs.shape[1]
    rows_own = NR * SG // chips
    hr = rows_own // 2
    hlong = nz * hr
    wide = SG // 2
    plan, total = semaphores()
    dma = pltpu.SemaphoreType.DMA
    return pl.pallas_call(
        functools.partial(main_kernel, scale),
        out_shape=[
            jax.ShapeDtypeStruct((fs, fs), f32),
            jax.ShapeDtypeStruct((2, 4, nx, ny, 2, hlong, wide), bf16),
            jax.ShapeDtypeStruct((2, 2, nx * ny * hlong, 2 * fs), bf16),
            jax.ShapeDtypeStruct((NC, 2, SG, fs), bf16),
            jax.ShapeDtypeStruct((2, nv), f32),
            jax.ShapeDtypeStruct((2, fs, SG), f32),
        ],
        in_specs=[HB] * 7,
        out_specs=[VM] * 6,
        scratch_shapes=[
            pltpu.VMEM((fs, fs), bf16),
            pltpu.SMEM((NR,), i32),
            pltpu.SMEM((NC,), i32),
            pltpu.VMEM((1, nv), i32),
            pltpu.VMEM((1, nv), i32),
            pltpu.VMEM((1, nv), i32),
            pltpu.VMEM((2, nv), f32),
            pltpu.VMEM((SG, SG), bf16),
            pltpu.VMEM((SG, SG), bf16),
            pltpu.VMEM((2, 2, SG, SG), bf16),
            pltpu.VMEM((2, 2, SG, SG), bf16),
            pltpu.VMEM((SG, fs), bf16),
            pltpu.VMEM((SG, fs), bf16),
            pltpu.VMEM((SG, 2 * fs), bf16),
            pltpu.VMEM((SG, 2 * fs), bf16),
            pltpu.VMEM((2, SG, fs), f32),
            pltpu.VMEM((SG, 2 * fs), f32),
            pltpu.VMEM((2 * fs, SG), bf16),
            pltpu.VMEM((nz, nx * ny, 4, nv), f32),
            pltpu.VMEM((fs, fs), bf16),
            pltpu.VMEM((4, nx, ny, 2, hlong, wide), f32),
            pltpu.VMEM((4, nx, ny, 2, hlong, wide), bf16),
            pltpu.VMEM((2, 6 * rows_own, SG), f32),
            pltpu.VMEM((3, rows_own, SG), f32),
            pltpu.VMEM((3, rows_own, SG), f32),
            pltpu.VMEM((3, rows_own, SG), f32),
            pltpu.VMEM((2 * rows_own, SG), bf16),
            pltpu.VMEM((2 * rows_own, SG), bf16),
            pltpu.VMEM((SG, 128), bf16),
            pltpu.VMEM((4, nx * ny - 1, 2, hlong, wide), bf16),
            pltpu.VMEM((4, nz, hr, SG), f32),
            pltpu.VMEM((4, nz, hr, SG), bf16),
            pltpu.VMEM((4, nz - 1, hr, SG), bf16),
            pltpu.VMEM((4, nz, hr, SG), bf16),
            pltpu.VMEM((2 * rows_own, SG), f32),
            pltpu.VMEM((nz, nx * ny, 2, nv), f32),
            pltpu.VMEM((chips, 2, nv), f32),
            dma((len(plan),)),
            dma((total,)),
            dma((8,)),
        ],
        compiler_params=pltpu.CompilerParams(
            collective_id=0, has_side_effects=True, vmem_limit_bytes=LIMIT
        ),
        name="cycle",
    )(*(pltpu.with_memory_space_constraint(a, pltpu.HBM) for a in (facet, ro, co, sub, u, v, obs)))


def finish_kernel(scale, acc_ref, g_ref, a_tab, bt_ref, res_ref, half_u, image_hbm, out_hbm, buf, sem):
    _, h, _, _ = position()
    fs = acc_ref.shape[0]
    pieces = sem.shape[0] - 1
    step = fs // pieces
    copies = [pltpu.make_async_copy(res_ref, out_hbm, sem.at[pieces])]
    copies[0].start()
    for k in range(pieces):
        cut = slice(k * step, (k + 1) * step)
        u = spread_rows(g_ref, a_tab, 1 - h, 3, pl.ds(pl.multiple_of(h * fs + k * step, step), step))
        u = (half_u[1, cut] + u).astype(bf16)
        buf[cut] = (acc_ref[cut] + jnp.dot(u, bt_ref[1 - h, 1], preferred_element_type=f32)) * scale
        copies.append(pltpu.make_async_copy(buf.at[cut], image_hbm.at[cut], sem.at[k]))
        copies[-1].start()
    for copy in copies:
        copy.wait()


def finish(acc, g, a_tab, bt, res, u, scale):
    fs = acc.shape[0]
    return pl.pallas_call(
        functools.partial(finish_kernel, scale),
        out_shape=[jax.ShapeDtypeStruct((fs, fs), f32), jax.ShapeDtypeStruct(res.shape, f32)],
        in_specs=[VM] * 6,
        out_specs=[HB] * 2,
        scratch_shapes=[pltpu.VMEM((fs, fs), f32), pltpu.SemaphoreType.DMA((3,))],
        compiler_params=pltpu.CompilerParams(vmem_limit_bytes=6 << 20),
        name="finish",
    )(acc, g, a_tab, bt, res, u)


def shards(facet_image, row_offsets, col_offsets, vis_subgrid, vis_u, vis_v, observed):
    rows, cols, _, _, _ = geometry()
    fs = facet_image.shape[0]
    scale_in = 1.0 / (fs * math.sqrt(rows * cols))
    scale_out = 1.0 / (SG * math.sqrt(NR * NC))
    acc, g, a_tab, bt, residual, u = main(
        row_offsets, col_offsets, vis_subgrid[None], vis_u[None], vis_v[None],
        observed, facet_image, scale_in / SG,
    )
    return tuple(finish(acc, g, a_tab, bt, residual, u, scale_out / SG))


def solution(mesh):
    in_specs = (
        P("frow", "fcol"),
        P(),
        P(),
        P(("frow", "fcol")),
        P(("frow", "fcol")),
        P(("frow", "fcol")),
        P(None, ("frow", "fcol")),
    )
    out_specs = (P("frow", "fcol"), P(None, ("frow", "fcol")))
    return jax.shard_map(shards, mesh=mesh, in_specs=in_specs, out_specs=out_specs, check_vma=False)
```

```python
import functools
import math

import jax
import jax.numpy as jnp
from jax import lax
from jax.experimental import pallas as pl
from jax.experimental.pallas import tpu as pltpu
from jax.sharding import PartitionSpec as P

SKY = 65536
SG = 256
NR = 2
NC = 2
f32 = jnp.float32
bf16 = jnp.bfloat16
i32 = jnp.int32
MESH = pl.DeviceIdType.MESH
VM = pl.BlockSpec(memory_space=pltpu.VMEM)
HB = pl.BlockSpec(memory_space=pltpu.HBM)
LIMIT = 32 << 20
ORDER = (
    "p:0", "rows1", "p:1", "v", "cols1",
    "p:2", "p:3", "g:0", "r:0", "bt",
    "g:1", "r:1", "r:2", "tr", "r:3", "g:2", "r:4", "g:3",
    "r:5", "g:4", "x", "r:6", "r:7",
    "t:0", "t:1", "t:2", "t:3", "t:4", "t:5", "t:6", "t:7", "m",
    "b:0", "b:1", "d:1", "b:2", "b:3", "d:1",
    "b:4", "b:5", "d:1", "b:6", "d:1", "ans", "b:7",
    "f:0", "f:1", "own:0", "f:2", "f:3", "own:1", "c:0", "oth:0",
    "f:4", "f:5", "own:2", "c:1", "oth:1", "f:6", "c:2", "oth:2",
    "f:7", "own:3", "res", "c:3",
)

scope = jax.named_scope


def geometry():
    rows = lax.axis_size("frow")
    cols = lax.axis_size("fcol")
    nx = rows // 2
    ny = 1 << ((cols.bit_length() - 1) // 2)
    nz = cols // ny
    return rows, cols, nx, ny, nz


def position():
    _, _, _, ny, _ = geometry()
    frow = lax.axis_index("frow")
    fcol = lax.axis_index("fcol")
    return frow // 2, frow % 2, fcol % ny, fcol // ny


def phase(product):
    k = product & (SKY - 1)
    quarter = lax.shift_right_logical(k + SKY // 8, SKY.bit_length() - 3)
    t = (k - quarter * (SKY // 4)).astype(f32) * (2.0 * math.pi / SKY)
    t2 = t * t
    cos = 1.0 + t2 * (-1 / 2 + t2 * (1 / 24 + t2 * (-1 / 720 + t2 * (1 / 40320))))
    sin = t * (1.0 + t2 * (-1 / 6 + t2 * (1 / 120 + t2 * (-1 / 5040 + t2 * (1 / 362880)))))
    odd = (quarter & 1) == 1
    c = jnp.where(odd, sin, cos)
    s = jnp.where(odd, cos, sin)
    return jnp.where(((quarter + 1) & 2) == 0, c, -c), jnp.where((quarter & 2) == 0, s, -s)


def expand(first, places, c_ref, s_ref):
    n = places.shape[1]
    steps = lax.broadcasted_iota(i32, (16, n), 0)
    c0, s0 = phase(steps * places)
    c1, s1 = phase((first + 16 * steps) * places)
    for k in range(SG // 16):
        ck = c1[k : k + 1]
        sk = s1[k : k + 1]
        c_ref[k * 16 : k * 16 + 16, :] = (ck * c0 - sk * s0).astype(bf16)
        s_ref[k * 16 : k * 16 + 16, :] = (sk * c0 + ck * s0).astype(bf16)


def place(q):
    _, _, _, ny, nz = geometry()
    return lax.div(q, ny * nz), lax.rem(lax.div(q, nz), ny), lax.rem(q, nz)


def device(q, h):
    _, _, _, ny, _ = geometry()
    x, y, z = place(q)
    return (2 * x + h, z * ny + y)


def hots(cell, owned, lanes):
    row = jnp.floor(cell * (1.0 / SG))
    v = (cell - row * SG).astype(bf16)
    rows, cols = [], []
    for t in range(cell.shape[0]):
        hot = lanes == jnp.broadcast_to(v[t : t + 1], lanes.shape)
        cols.append(jnp.where(hot, jnp.ones_like(lanes), jnp.zeros_like(lanes)))
        rows.append(owned == row[t : t + 1])
    return rows, jnp.concatenate(cols, 1)


def pairs(count, body):
    if count <= 4:
        for t in range(0, count, 2):
            body(t)
        return

    def step(t, carry):
        body(2 * t)
        return carry

    lax.fori_loop(0, count // 2, step, 0)


def split(rows_own):
    return 2 if rows_own >= 16 else 1


def semaphores(waves):
    plan = {}
    total = 0
    kinds = (
        "plane", "z", "back_z", "back_plane", "cross",
        "facet", "cells", "cells_l", "cells_z", "sums", "model", "answers",
    )
    for at, kind in enumerate(kinds):
        if kind == "back_z":
            plan[kind] = (at,) + plan["plane"][1:]
            continue
        count = waves if at < 4 else (4 if kind == "cross" else 1)
        plan[kind] = (at, total, count)
        total += count
    return plan, total


def spread_rows(g_ref, at_ref, c, w, cut):
    wide = g_ref.shape[-1]
    parts = g_ref.shape[1] // 4
    tall = at_ref.shape[-1]
    g = jnp.concatenate([g_ref[c, w * parts : (w + 1) * parts, :, :, p].reshape(tall, wide) for p in range(2)], 1)
    one, two = (jnp.dot(at_ref[p, w % 2, cut], g, preferred_element_type=f32) for p in range(2))
    return jnp.concatenate([one[:, :wide] + two[:, wide:], one[:, wide:] - two[:, :wide]], 1)


def main_kernel(
    scale, facet_hbm, ro_hbm, co_hbm, sub_hbm, u_hbm, v_hbm, obs_hbm,
    acc_ref, g_ref, at_ref, bt_ref, res_ref, half_u,
    facet_ref, ro_ref, co_ref, sub_ref, u_ref, v_ref, obs_ref,
    kk, ks, kcol, krow, cc, cs, rc, rs, keep_col, keep_row, a_tab, p_ref, vis_all, other, z_ref, zb_ref, grid_acc, own_sum, pair_sum, got_sum, own_model, got_model, lanes,
    got, own_z, send_z, got_z, gz, model, vals, slots,
    ssem, rsem, lsem,
):
    rows, cols, nx, ny, nz = geometry()
    x, h, y, z = position()
    chips = nx * ny * nz
    me = (x * ny + y) * nz + z
    fs = facet_ref.shape[0]
    nv = obs_ref.shape[1]
    rows_own = NR * SG // chips
    parts = split(rows_own)
    hr = rows_own // (2 * parts)
    hlong = nz * hr
    part = 2 * parts * hlong
    wide = SG // 2
    sib = (2 * x + 1 - h, lax.axis_index("fcol"))
    barrier = pltpu.get_barrier_semaphore()

    plane = [(dx, dy) for dx in range(nx) for dy in range(ny)][1:]

    def across(k):
        px, py = lax.rem(x + plane[k][0], nx), lax.rem(y + plane[k][1], ny)
        return px, py, (2 * px + h, z * ny + py)

    def to_z(d):
        return 2 * x + h, lax.rem(z + d, nz) * ny + y

    own_xy = x * ny + y
    near = [sib] + [across(k)[2] for k in range(nx * ny - 1)]
    near += [to_z(d) for d in range(1, nz)]
    for to in near:
        pl.semaphore_signal(barrier, inc=1, device_id=to, device_id_type=MESH)

    def peers(act):
        if chips > 16:
            def step(d, carry):
                to = lax.rem(me + d, chips)
                px, py, pz = place(to)
                act(pz, px * ny + py, to, (2 * px + h, pz * ny + py))
                return carry

            lax.fori_loop(1, chips, step, 0)
            return
        for dx in range(nx):
            for dy in range(ny):
                for dz in range(nz):
                    if dx + dy + dz > 0:
                        px = lax.rem(x + dx, nx)
                        py = lax.rem(y + dy, ny)
                        pz = lax.rem(z + dz, nz)
                        act(pz, px * ny + py, (px * ny + py) * nz + pz, (2 * px + h, pz * ny + py))

    loads = []
    for k, (src, dst) in enumerate((
        (ro_hbm, ro_ref), (co_hbm, co_ref), (sub_hbm, sub_ref), (u_hbm, u_ref), (v_hbm, v_ref),
        (obs_hbm, obs_ref), (facet_hbm, facet_ref),
    )):
        loads.append(pltpu.make_async_copy(src, dst, lsem.at[k]))
        loads[-1].start()
    plan = semaphores(4 * parts)[0]

    def send(kind, w, src, dst, to):
        at, base, _ = plan[kind]
        pltpu.make_async_remote_copy(
            src, dst, ssem.at[at], rsem.at[base + w], device_id=to, device_id_type=MESH
        ).start()

    def land(kind, w, like):
        at, base, _ = plan[kind]
        pltpu.make_async_remote_copy(
            like, like, ssem.at[at], rsem.at[base + w], device_id=sib, device_id_type=MESH
        ).wait_recv()

    def sentall(kind, like):
        at, base, _ = plan[kind]
        pltpu.make_async_remote_copy(
            like, like, ssem.at[at], rsem.at[base], device_id=sib, device_id_type=MESH
        ).wait_send()

    with scope("expandK"):
        expand(0, lax.broadcasted_iota(i32, (1, SG), 1) * (SKY // SG), kk, ks)
        for q in range(2):
            cut = slice(q * wide, (q + 1) * wide)
            kcol[0, q, :wide] = kk[cut]
            kcol[0, q, wide:] = ks[cut]
            kcol[1, q, :wide] = ks[cut]
            kcol[1, q, wide:] = -kk[cut]
    col_places = (lax.axis_index("fcol") * fs + lax.broadcasted_iota(i32, (1, fs), 1)) * (SKY // (cols * fs))
    row_places = (x * (2 * fs) + lax.broadcasted_iota(i32, (1, 2 * fs), 1)) * (SKY // (rows * fs))

    def compose(k0, k1, c_ref, s_ref, out):
        n = c_ref.shape[1]
        for cut in (slice(0, n // 2), slice(n // 2, n)):
            both = jnp.dot(k0, c_ref[:, cut], preferred_element_type=f32)
            both += jnp.dot(k1, s_ref[:, cut], preferred_element_type=f32)
            out[:, cut] = both

    def shifted(both, places, offset):
        cos, sin = phase(offset * places)
        re = both[:wide]
        im = both[wide:]
        return (re * cos + im * sin).astype(bf16), (im * cos - re * sin).astype(bf16)

    def columns(c, q):
        bt_ref[c, q, :wide], bt_ref[c, q, wide:] = shifted(keep_col[q], col_places, co_ref[c])

    def columns_half(q):
        compose(kcol[0, q], kcol[1, q], cc, cs, keep_col.at[q])
        columns(h, q)

    def rows_half(e):
        if e > 0:
            compose(krow[0, e], krow[1, e], rc, rs, keep_row)
        for r in range(NR):
            pair = shifted(keep_row[...], row_places, ro_ref[r])
            n = wide // parts
            for p in range(2):
                for i in range(parts):
                    a_tab[p, e * parts + i, r * n : (r + 1) * n] = pair[p][i * n : (i + 1) * n]

    with scope("tables"):
        expand(0, col_places, cc, cs)
        compose(kcol[0, 0], kcol[1, 0], cc, cs, keep_col.at[0])
        per = SG // part
        for e in range(2):
            for i in range(parts * per):
                first = (i % per) * part + (e * parts + i // per) * hlong
                src = slice(first, first + hlong)
                dst = slice(i * hlong, (i + 1) * hlong)
                low = slice(wide + i * hlong, wide + (i + 1) * hlong)
                krow[0, e, dst] = kk[src]
                krow[0, e, low] = ks[src]
                krow[1, e, dst] = ks[src]
                krow[1, e, low] = -kk[src]
        expand(0, row_places, rc, rs)
        compose(krow[0, 0], krow[1, 0], rc, rs, keep_row)
    with scope("columns0"):
        loads[0].wait()
        loads[1].wait()
        columns(h, 0)
    with scope("cells"):
        for copy in loads[2:6]:
            copy.wait()
        sub = sub_ref[...]
        row = (lax.rem(sub, NC) * NR + lax.div(sub, NC)) * SG + u_ref[...]
        cell = (row * SG + v_ref[...]).astype(f32)
        for t in range(nv // 128):
            cut = slice(t * 128, (t + 1) * 128)
            vis_all[z, own_xy, 0, t : t + 1] = cell[:, cut]
            vis_all[z, own_xy, 1, t : t + 1] = obs_ref[0:1, cut]
            vis_all[z, own_xy, 2, t : t + 1] = obs_ref[1:2, cut]
    with scope("barwait"):
        pl.semaphore_wait(barrier, len(near))
    for k in range(nx * ny - 1):
        mine = vis_all.at[z, own_xy]
        send("cells", 0, mine, mine, across(k)[2])
    for d in range(1, nz):
        mine = vis_all.at[z, own_xy]
        send("cells_l", 0, mine, mine, to_z(d))
    loads[6].wait()
    send("facet", 0, facet_ref, other, sib)
    with scope("rows0"):
        rows_half(0)

    def project(ref, q, base):
        step = fs // 2
        for k in range(2):
            got = lax.dot_general(
                ref[k * step : (k + 1) * step], bt_ref[h, q], (((1,), (1,)), ((), ())),
                preferred_element_type=f32,
            )
            p_ref[pl.ds(pl.multiple_of(base + k * step, step), step)] = got.astype(bf16)

    own_cut = pl.ds(pl.multiple_of(h * fs, fs), fs)

    def produce(w):
        q, e = w // 2, w % 2
        if e == 0:
            project(facet_ref, q, h * fs)
            if q == 0:
                land("facet", 0, other)
            project(other, q, (1 - h) * fs)
        tall = parts * nx * ny * hlong
        one, two = (
            jnp.dot(a_tab[p, e * parts : (e + 1) * parts].reshape(tall, 2 * fs), p_ref[...], preferred_element_type=f32)
            for p in range(2)
        )
        zr = (one[:, :wide] - two[:, wide:]).reshape(parts, nx, ny, hlong, wide)
        zi = (one[:, wide:] + two[:, :wide]).reshape(parts, nx, ny, hlong, wide)
        for i in range(parts):
            for p, part_z in enumerate((zr, zi)):
                z_ref[w * parts + i, :, :, p] = part_z[i]
                zb_ref[w * parts + i, :, :, p] = part_z[i].astype(bf16)
            for k in range(nx * ny - 1):
                px, py, to = across(k)
                send("plane", w * parts + i, zb_ref.at[w * parts + i, px, py], got.at[w * parts + i, k], to)

    owned_row = lax.broadcasted_iota(i32, (2 * rows_own, 128), 0)
    column = owned_row // rows_own
    column = h + column - 2 * h * column
    owned_row = owned_row % rows_own
    owned_row = (x * ny + y) * part + z * hr + (owned_row // hr) * hlong + owned_row % hr
    owned_row = (owned_row + column * (NR * SG)).astype(f32)
    lanes[...] = lax.broadcasted_iota(i32, lanes.shape, 0).astype(f32).astype(bf16)

    def gridding(ds, ks):
        def one(level, k):
            vis = vis_all[level, k]
            hot_rows, hot_col = hots(vis[0], owned_row, lanes[...])
            left = []
            for t, hot in enumerate(hot_rows):
                values = [vis[1, t : t + 1], vis[2, t : t + 1], jnp.ones_like(vis[0, t : t + 1])]
                left.append(jnp.concatenate([jnp.where(hot, a, 0.0) for a in values], 0).astype(bf16))
            left = jnp.concatenate(left, 1)
            return lax.dot_general(left, hot_col, (((1,), (1,)), ((), ())), preferred_element_type=f32)

        def block(i, slot):
            level = lax.rem(z + ds.start + i // len(ks), nz)
            grid_acc[slot] += one(level, lax.rem(own_xy + ks.start + i % len(ks), nx * ny))

        if chips <= 16:
            for i in range(len(ds) * len(ks)):
                block(i, i % 2)
            return

        def step(i, carry):
            block(i, 0)
            return carry

        lax.fori_loop(0, len(ds) * len(ks), step, 0)

    def reduce(w):
        land("plane", w, got.at[w])
        total = z_ref[w, x, y]
        for k in range(nx * ny - 1):
            total = total + got[w, k].astype(f32)
        for k in range(nz):
            for p in range(2):
                rows_k = total[p, k * hr : (k + 1) * hr]
                own_z[w, k, :, p * wide : (p + 1) * wide] = rows_k
                send_z[w, k, :, p * wide : (p + 1) * wide] = rows_k.astype(bf16)
        for d in range(1, nz):
            send("z", w, send_z.at[w, lax.rem(z + d, nz)], got_z.at[w, d - 1], to_z(d))

    def turn(w):
        q, e = w // (2 * parts), w % (2 * parts)
        if w == 0:
            land("sums", 0, got_sum)
        land("z", w, got_z.at[w])
        total = own_z[w, z]
        for d in range(nz - 1):
            total = total + got_z[w, d].astype(f32)
        m = total * scale
        cut = slice(q * wide, (q + 1) * wide)
        half = slice(e * hr, (e + 1) * hr)
        sums = [own_sum[p, half, cut] + got_sum[p, half, cut] for p in range(3)]
        hat_re = sums[0] - sums[2] * m[:, :wide]
        hat_im = sums[1] - sums[2] * m[:, wide:]
        gz[w, z, :, :wide] = hat_re.astype(bf16)
        gz[w, z, :, wide:] = hat_im.astype(bf16)
        for d in range(1, nz):
            send("back_z", w, gz.at[w, z], gz.at[w, z], to_z(d))
        model[e * hr : (e + 1) * hr, cut] = m[:, :wide]
        model[rows_own + e * hr : rows_own + (e + 1) * hr, cut] = m[:, wide:]

    def over(w, px, py):
        src = g_ref.at[h, w, px, py]
        send("cross", w // parts, src, src, sib)

    def gather(w):
        land("back_z", w, gz.at[w, : nz - 1])
        for k in range(nz):
            cut = slice(k * hr, (k + 1) * hr)
            g_ref[h, w, x, y, 0, cut, :] = gz[w, k, :, :wide]
            g_ref[h, w, x, y, 1, cut, :] = gz[w, k, :, wide:]
        blk = g_ref.at[h, w, x, y]
        for k in range(nx * ny - 1):
            send("back_plane", w, blk, blk, across(k)[2])
        over(w, x, y)

    def finish(w):
        land("back_plane", w, got.at[w])
        for k in range(nx * ny - 1):
            px, py, _ = across(k)
            over(w, px, py)

    def crossed(w):
        land("cross", w, g_ref.at[1 - h, w * parts : (w + 1) * parts])

    def degrid(level):
        m = jnp.concatenate([own_model[...], got_model[...]], 0)

        def one(k):
            hot_rows, hot_col = hots(vis_all[level, k][0], owned_row, lanes[...])
            val = jnp.dot(m, hot_col, preferred_element_type=f32)
            out = []
            for p in range(2):
                line = []
                for t, hot in enumerate(hot_rows):
                    cut = slice(t * 128, (t + 1) * 128)
                    picked = [
                        jnp.where(hot[c * rows_own : (c + 1) * rows_own], val[(2 * c + p) * rows_own : (2 * c + p + 1) * rows_own, cut], 0.0)
                        for c in range(2)
                    ]
                    line.append(jnp.sum(picked[0] + picked[1], 0, keepdims=True))
                out.append(jnp.concatenate(line, 1))
            return jnp.concatenate(out, 0)

        def body(k):
            a = one(k)
            b = one(k + 1)
            vals[level, k] = a
            vals[level, k + 1] = b

        pairs(nx * ny, body)

    def image(side, w):
        c = h if side == 0 else 1 - h
        q, e = w // 2, w % 2
        u = spread_rows(g_ref, at_ref, c, w, slice(None))
        if e == 0:
            half_u[side] = u
            return
        total = (half_u[side] + u).astype(bf16)
        got = jnp.dot(total, bt_ref[c, q], preferred_element_type=f32)
        if q == 0 and side == 0:
            acc_ref[...] = got
        else:
            acc_ref[...] += got

    grid_acc[...] = jnp.zeros_like(grid_acc)
    done = {"degrid": 0}

    def grid(k):
        if k == 0:
            gridding(range(0, 1), range(0, nx * ny))
        elif k == 1:
            land("cells_l", 0, vis_all.at[: nz - 1, own_xy])
            gridding(range(1, nz), range(0, 1))
        else:
            if k == 2:
                land("cells_z", 0, vis_all.at[: nz - 1, : nx * ny - 1])
            last = nz if k == 4 else k
            gridding(range(k - 1, last), range(1, nx * ny))

    def exchange():
        for p in range(3):
            base = 2 * p * rows_own
            total = grid_acc[0, base : base + 2 * rows_own] + grid_acc[1, base : base + 2 * rows_own]
            own_sum[p] = total[:rows_own]
            pair_sum[p] = total[rows_own:]
        send("sums", 0, pair_sum, got_sum, sib)

    def models():
        own_model[...] = model[...].astype(bf16)
        send("model", 0, own_model, got_model, sib)

    def ungrid(n):
        for _ in range(n * nz // 4):
            k = done["degrid"]
            done["degrid"] += 1
            if k == 0:
                land("model", 0, got_model)
            with scope("degrid%d" % k):
                degrid(lax.rem(z + k, nz))

    def cells():
        land("cells", 0, vis_all.at[z, : nx * ny - 1])
        for k in range(1, nx * ny):
            block = vis_all.at[z, lax.rem(own_xy + k, nx * ny)]
            for d in range(1, nz):
                send("cells_z", 0, block, block, to_z(d))

    def answers():
        peers(lambda pz, pxy, slot, to: send("answers", 0, vals.at[pz, pxy], slots.at[me], to))

    def result():
        land("answers", 0, slots.at[: chips - 1])
        start = vals[z, own_xy]
        if chips > 16:
            total = lax.fori_loop(1, chips, lambda d, t: t + slots[lax.rem(me + d, chips)], start)
        else:
            total = start
            for d in range(1, chips):
                total = total + slots[lax.rem(me + d, chips)]
        res_ref[...] = obs_ref[...] - total

    def turned():
        for p in range(2):
            for e in range(2):
                block = a_tab[p, e * parts : (e + 1) * parts, :, own_cut].reshape(at_ref.shape[-1], fs)
                at_ref[p, e] = block.T

    def late_columns():
        columns(1 - h, 0)
        columns(1 - h, 1)

    acts = {
        "p": produce, "g": grid, "r": reduce, "t": turn, "b": gather, "f": finish, "c": crossed,
        "own": lambda w: image(0, w), "oth": lambda w: image(1, w),
    }
    simple = {
        "v": cells, "ans": answers, "res": result, "x": exchange, "m": models, "tr": turned,
        "rows1": lambda: rows_half(1), "cols1": lambda: columns_half(1), "bt": late_columns,
    }
    for word in ORDER:
        name, _, arg = word.partition(":")
        if name == "d":
            ungrid(int(arg))
        else:
            if name in ("r", "t", "b", "f") and int(arg) >= 4 * parts:
                continue
            with scope(name + arg):
                acts[name](int(arg)) if arg else simple[name]()
    with scope("drain"):
        for kind, like in (
            ("plane", got), ("z", got_z), ("back_z", got_z), ("back_plane", got),
            ("cross", g_ref.at[h]), ("facet", other), ("cells", vis_all.at[z, : nx * ny - 1]),
            ("cells_l", vis_all.at[: nz - 1, own_xy]), ("cells_z", vis_all.at[: nz - 1, : nx * ny - 1]), ("sums", got_sum), ("model", got_model), ("answers", slots.at[: chips - 1]),
        ):
            sentall(kind, like)


def main(ro, co, sub, u, v, obs, facet, scale):
    _, _, nx, ny, nz = geometry()
    chips = nx * ny * nz
    fs = facet.shape[0]
    nv = obs.shape[1]
    rows_own = NR * SG // chips
    parts = split(rows_own)
    waves = 4 * parts
    hr = rows_own // (2 * parts)
    hlong = nz * hr
    wide = SG // 2
    plan, total = semaphores(waves)
    dma = pltpu.SemaphoreType.DMA
    return pl.pallas_call(
        functools.partial(main_kernel, scale),
        out_shape=[
            jax.ShapeDtypeStruct((fs, fs), f32),
            jax.ShapeDtypeStruct((2, waves, nx, ny, 2, hlong, wide), bf16),
            jax.ShapeDtypeStruct((2, 2, fs, parts * nx * ny * hlong), bf16),
            jax.ShapeDtypeStruct((NC, 2, SG, fs), bf16),
            jax.ShapeDtypeStruct((2, nv), f32),
            jax.ShapeDtypeStruct((2, fs, SG), f32),
        ],
        in_specs=[HB] * 7,
        out_specs=[VM] * 6,
        scratch_shapes=[
            pltpu.VMEM((fs, fs), bf16),
            pltpu.SMEM((NR,), i32),
            pltpu.SMEM((NC,), i32),
            pltpu.VMEM((1, nv), i32),
            pltpu.VMEM((1, nv), i32),
            pltpu.VMEM((1, nv), i32),
            pltpu.VMEM((2, nv), f32),
            pltpu.VMEM((SG, SG), bf16),
            pltpu.VMEM((SG, SG), bf16),
            pltpu.VMEM((2, 2, SG, SG), bf16),
            pltpu.VMEM((2, 2, SG, SG), bf16),
            pltpu.VMEM((SG, fs), bf16),
            pltpu.VMEM((SG, fs), bf16),
            pltpu.VMEM((SG, 2 * fs), bf16),
            pltpu.VMEM((SG, 2 * fs), bf16),
            pltpu.VMEM((2, SG, fs), f32),
            pltpu.VMEM((SG, 2 * fs), f32),
            pltpu.VMEM((2, 2 * parts, nx * ny * hlong, 2 * fs), bf16),
            pltpu.VMEM((2 * fs, SG), bf16),
            pltpu.VMEM((nz, nx * ny, 3, nv // 128, 128), f32),
            pltpu.VMEM((fs, fs), bf16),
            pltpu.VMEM((waves, nx, ny, 2, hlong, wide), f32),
            pltpu.VMEM((waves, nx, ny, 2, hlong, wide), bf16),
            pltpu.VMEM((2, 6 * rows_own, SG), f32),
            pltpu.VMEM((3, rows_own, SG), f32),
            pltpu.VMEM((3, rows_own, SG), f32),
            pltpu.VMEM((3, rows_own, SG), f32),
            pltpu.VMEM((2 * rows_own, SG), bf16),
            pltpu.VMEM((2 * rows_own, SG), bf16),
            pltpu.VMEM((SG, 128), bf16),
            pltpu.VMEM((waves, nx * ny - 1, 2, hlong, wide), bf16),
            pltpu.VMEM((waves, nz, hr, SG), f32),
            pltpu.VMEM((waves, nz, hr, SG), bf16),
            pltpu.VMEM((waves, nz - 1, hr, SG), bf16),
            pltpu.VMEM((waves, nz, hr, SG), bf16),
            pltpu.VMEM((2 * rows_own, SG), f32),
            pltpu.VMEM((nz, nx * ny, 2, nv), f32),
            pltpu.VMEM((chips, 2, nv), f32),
            dma((len(plan),)),
            dma((total,)),
            dma((8,)),
        ],
        compiler_params=pltpu.CompilerParams(
            collective_id=0, has_side_effects=True, vmem_limit_bytes=LIMIT
        ),
        name="cycle",
    )(*(pltpu.with_memory_space_constraint(a, pltpu.HBM) for a in (facet, ro, co, sub, u, v, obs)))


def finish_kernel(scale, acc_ref, g_ref, at_ref, bt_ref, res_ref, half_u, image_hbm, out_hbm, buf, sem):
    _, h, _, _ = position()
    fs = acc_ref.shape[0]
    pieces = sem.shape[0] - 1
    step = fs // pieces
    copies = [pltpu.make_async_copy(res_ref, out_hbm, sem.at[pieces])]
    copies[0].start()
    for k in range(pieces):
        cut = slice(k * step, (k + 1) * step)
        u = spread_rows(g_ref, at_ref, 1 - h, 3, cut)
        u = (half_u[1, cut] + u).astype(bf16)
        buf[cut] = (acc_ref[cut] + jnp.dot(u, bt_ref[1 - h, 1], preferred_element_type=f32)) * scale
        copies.append(pltpu.make_async_copy(buf.at[cut], image_hbm.at[cut], sem.at[k]))
        copies[-1].start()
    for copy in copies:
        copy.wait()


def finish(acc, g, a_tab, bt, res, u, scale):
    fs = acc.shape[0]
    return pl.pallas_call(
        functools.partial(finish_kernel, scale),
        out_shape=[jax.ShapeDtypeStruct((fs, fs), f32), jax.ShapeDtypeStruct(res.shape, f32)],
        in_specs=[VM] * 6,
        out_specs=[HB] * 2,
        scratch_shapes=[pltpu.VMEM((fs, fs), f32), pltpu.SemaphoreType.DMA((3,))],
        compiler_params=pltpu.CompilerParams(vmem_limit_bytes=6 << 20),
        name="finish",
    )(acc, g, a_tab, bt, res, u)


def shards(facet_image, row_offsets, col_offsets, vis_subgrid, vis_u, vis_v, observed):
    rows, cols, _, _, _ = geometry()
    fs = facet_image.shape[0]
    scale_in = 1.0 / (fs * math.sqrt(rows * cols))
    scale_out = 1.0 / (SG * math.sqrt(NR * NC))
    acc, g, a_tab, bt, residual, u = main(
        row_offsets, col_offsets, vis_subgrid[None], vis_u[None], vis_v[None],
        observed, facet_image, scale_in / SG,
    )
    return tuple(finish(acc, g, a_tab, bt, residual, u, scale_out / SG))


def solution(mesh):
    in_specs = (
        P("frow", "fcol"),
        P(),
        P(),
        P(("frow", "fcol")),
        P(("frow", "fcol")),
        P(("frow", "fcol")),
        P(None, ("frow", "fcol")),
    )
    out_specs = (P("frow", "fcol"), P(None, ("frow", "fcol")))
    return jax.shard_map(shards, mesh=mesh, in_specs=in_specs, out_specs=out_specs, check_vma=False)
```

```python
import functools
import math

import jax
import jax.numpy as jnp
from jax import lax
from jax.experimental import pallas as pl
from jax.experimental.pallas import tpu as pltpu
from jax.sharding import PartitionSpec as P

SKY = 65536
SG = 256
NR = 2
NC = 2
f32 = jnp.float32
bf16 = jnp.bfloat16
i32 = jnp.int32
MESH = pl.DeviceIdType.MESH
VM = pl.BlockSpec(memory_space=pltpu.VMEM)
HB = pl.BlockSpec(memory_space=pltpu.HBM)
LIMIT = 32 << 20
ORDER = (
    "p:0", "rows1", "p:1", "v", "cols1",
    "p:2", "p:3", "r:0", "g:0", "r:1", "g:1",
    "r:2", "g:2", "r:3", "g:3", "r:4", "g:4", "x", "r:5", "bt", "r:6", "tr", "r:7",
    "t:0", "t:1", "t:2", "t:3", "t:4", "t:5", "b:0", "t:6", "t:7", "m", "b:1",
    "b:2", "b:3", "d:1", "b:4", "d:1",
    "b:5", "d:1", "b:6", "d:1", "ans", "b:7",
    "f:0", "f:1", "own:0", "f:2", "f:3", "own:1", "c:0", "oth:0",
    "f:4", "f:5", "own:2", "c:1", "oth:1", "f:6", "c:2", "oth:2",
    "f:7", "own:3", "res", "c:3",
)

scope = jax.named_scope


def geometry():
    rows = lax.axis_size("frow")
    cols = lax.axis_size("fcol")
    nx = rows // 2
    ny = 1 << ((cols.bit_length() - 1) // 2)
    nz = cols // ny
    return rows, cols, nx, ny, nz


def position():
    _, _, _, ny, _ = geometry()
    frow = lax.axis_index("frow")
    fcol = lax.axis_index("fcol")
    return frow // 2, frow % 2, fcol % ny, fcol // ny


def phase(product):
    k = product & (SKY - 1)
    quarter = lax.shift_right_logical(k + SKY // 8, SKY.bit_length() - 3)
    t = (k - quarter * (SKY // 4)).astype(f32) * (2.0 * math.pi / SKY)
    t2 = t * t
    cos = 1.0 + t2 * (-1 / 2 + t2 * (1 / 24 + t2 * (-1 / 720 + t2 * (1 / 40320))))
    sin = t * (1.0 + t2 * (-1 / 6 + t2 * (1 / 120 + t2 * (-1 / 5040 + t2 * (1 / 362880)))))
    odd = (quarter & 1) == 1
    c = jnp.where(odd, sin, cos)
    s = jnp.where(odd, cos, sin)
    return jnp.where(((quarter + 1) & 2) == 0, c, -c), jnp.where((quarter & 2) == 0, s, -s)


def expand(first, places, c_ref, s_ref):
    n = places.shape[1]
    steps = lax.broadcasted_iota(i32, (16, n), 0)
    c0, s0 = phase(steps * places)
    c1, s1 = phase((first + 16 * steps) * places)
    for k in range(SG // 16):
        ck = c1[k : k + 1]
        sk = s1[k : k + 1]
        c_ref[k * 16 : k * 16 + 16, :] = (ck * c0 - sk * s0).astype(bf16)
        s_ref[k * 16 : k * 16 + 16, :] = (sk * c0 + ck * s0).astype(bf16)


def place(q):
    _, _, _, ny, nz = geometry()
    return lax.div(q, ny * nz), lax.rem(lax.div(q, nz), ny), lax.rem(q, nz)


def device(q, h):
    _, _, _, ny, _ = geometry()
    x, y, z = place(q)
    return (2 * x + h, z * ny + y)


def hots(cell, owned, lanes):
    row = jnp.floor(cell * (1.0 / SG))
    v = (cell - row * SG).astype(bf16)
    rows, cols = [], []
    for t in range(cell.shape[0]):
        hot = lanes == jnp.broadcast_to(v[t : t + 1], lanes.shape)
        cols.append(jnp.where(hot, jnp.ones_like(lanes), jnp.zeros_like(lanes)))
        rows.append(owned == row[t : t + 1])
    return rows, jnp.concatenate(cols, 1)


def pairs(count, body):
    if count <= 4:
        for t in range(0, count, 2):
            body(t)
        return

    def step(t, carry):
        body(2 * t)
        return carry

    lax.fori_loop(0, count // 2, step, 0)


def split(rows_own):
    return 2 if rows_own >= 16 else 1


def semaphores(waves):
    plan = {}
    total = 0
    kinds = (
        "plane", "z", "back_z", "back_plane", "cross",
        "facet", "cells", "cells_l", "cells_z", "sums", "model", "answers",
    )
    for at, kind in enumerate(kinds):
        if kind == "back_z":
            plan[kind] = (at,) + plan["plane"][1:]
            continue
        count = waves if at < 4 else (4 if kind == "cross" else 1)
        plan[kind] = (at, total, count)
        total += count
    return plan, total


def spread_rows(g_ref, at_ref, c, w, cut):
    wide = g_ref.shape[-1]
    parts = g_ref.shape[1] // 4
    tall = at_ref.shape[-1]
    g = jnp.concatenate([g_ref[c, w * parts : (w + 1) * parts, :, :, p].reshape(tall, wide) for p in range(2)], 1)
    one, two = (jnp.dot(at_ref[p, w % 2, cut], g, preferred_element_type=f32) for p in range(2))
    return jnp.concatenate([one[:, :wide] + two[:, wide:], one[:, wide:] - two[:, :wide]], 1)


def main_kernel(
    scale, facet_hbm, ro_hbm, co_hbm, sub_hbm, u_hbm, v_hbm, obs_hbm,
    acc_ref, g_ref, at_ref, bt_ref, res_ref, half_u, full_u,
    facet_ref, ro_ref, co_ref, sub_ref, u_ref, v_ref, obs_ref,
    kk, ks, kcol, krow, cc, cs, rc, rs, keep_col, keep_row, a_tab, p_ref, vis_all, other, z_ref, zb_ref, grid_acc, own_sum, pair_sum, got_sum, own_model, got_model, lanes,
    got, own_z, send_z, got_z, gz, model, vals, slots,
    ssem, rsem, lsem,
):
    rows, cols, nx, ny, nz = geometry()
    x, h, y, z = position()
    chips = nx * ny * nz
    me = (x * ny + y) * nz + z
    fs = facet_ref.shape[0]
    nv = obs_ref.shape[1]
    rows_own = NR * SG // chips
    parts = split(rows_own)
    hr = rows_own // (2 * parts)
    hlong = nz * hr
    part = 2 * parts * hlong
    wide = SG // 2
    sib = (2 * x + 1 - h, lax.axis_index("fcol"))
    barrier = pltpu.get_barrier_semaphore()

    plane = [(dx, dy) for dx in range(nx) for dy in range(ny)][1:]

    def across(k):
        px, py = lax.rem(x + plane[k][0], nx), lax.rem(y + plane[k][1], ny)
        return px, py, (2 * px + h, z * ny + py)

    def to_z(d):
        return 2 * x + h, lax.rem(z + d, nz) * ny + y

    own_xy = x * ny + y
    near = [sib] + [across(k)[2] for k in range(nx * ny - 1)]
    near += [to_z(d) for d in range(1, nz)]
    for to in near:
        pl.semaphore_signal(barrier, inc=1, device_id=to, device_id_type=MESH)

    def peers(act):
        if chips > 16:
            def step(d, carry):
                to = lax.rem(me + d, chips)
                px, py, pz = place(to)
                act(pz, px * ny + py, to, (2 * px + h, pz * ny + py))
                return carry

            lax.fori_loop(1, chips, step, 0)
            return
        for dx in range(nx):
            for dy in range(ny):
                for dz in range(nz):
                    if dx + dy + dz > 0:
                        px = lax.rem(x + dx, nx)
                        py = lax.rem(y + dy, ny)
                        pz = lax.rem(z + dz, nz)
                        act(pz, px * ny + py, (px * ny + py) * nz + pz, (2 * px + h, pz * ny + py))

    loads = []
    for k, (src, dst) in enumerate((
        (ro_hbm, ro_ref), (co_hbm, co_ref), (sub_hbm, sub_ref), (u_hbm, u_ref), (v_hbm, v_ref),
        (obs_hbm, obs_ref), (facet_hbm, facet_ref),
    )):
        loads.append(pltpu.make_async_copy(src, dst, lsem.at[k]))
        loads[-1].start()
    plan = semaphores(4 * parts)[0]

    def send(kind, w, src, dst, to):
        at, base, _ = plan[kind]
        pltpu.make_async_remote_copy(
            src, dst, ssem.at[at], rsem.at[base + w], device_id=to, device_id_type=MESH
        ).start()

    def land(kind, w, like):
        at, base, _ = plan[kind]
        pltpu.make_async_remote_copy(
            like, like, ssem.at[at], rsem.at[base + w], device_id=sib, device_id_type=MESH
        ).wait_recv()

    def sentall(kind, like):
        at, base, _ = plan[kind]
        pltpu.make_async_remote_copy(
            like, like, ssem.at[at], rsem.at[base], device_id=sib, device_id_type=MESH
        ).wait_send()

    with scope("expandK"):
        expand(0, lax.broadcasted_iota(i32, (1, SG), 1) * (SKY // SG), kk, ks)
        for q in range(2):
            cut = slice(q * wide, (q + 1) * wide)
            kcol[0, q, :wide] = kk[cut]
            kcol[0, q, wide:] = ks[cut]
            kcol[1, q, :wide] = ks[cut]
            kcol[1, q, wide:] = -kk[cut]
    col_places = (lax.axis_index("fcol") * fs + lax.broadcasted_iota(i32, (1, fs), 1)) * (SKY // (cols * fs))
    row_places = (x * (2 * fs) + lax.broadcasted_iota(i32, (1, 2 * fs), 1)) * (SKY // (rows * fs))

    def compose(k0, k1, c_ref, s_ref, out):
        n = c_ref.shape[1]
        for cut in (slice(0, n // 2), slice(n // 2, n)):
            both = jnp.dot(k0, c_ref[:, cut], preferred_element_type=f32)
            both += jnp.dot(k1, s_ref[:, cut], preferred_element_type=f32)
            out[:, cut] = both

    def shifted(both, places, offset):
        cos, sin = phase(offset * places)
        re = both[:wide]
        im = both[wide:]
        return (re * cos + im * sin).astype(bf16), (im * cos - re * sin).astype(bf16)

    def columns(c, q):
        bt_ref[c, q, :wide], bt_ref[c, q, wide:] = shifted(keep_col[q], col_places, co_ref[c])

    def columns_half(q):
        compose(kcol[0, q], kcol[1, q], cc, cs, keep_col.at[q])
        columns(h, q)

    def rows_half(e):
        if e > 0:
            compose(krow[0, e], krow[1, e], rc, rs, keep_row)
        for r in range(NR):
            pair = shifted(keep_row[...], row_places, ro_ref[r])
            n = wide // parts
            for p in range(2):
                for i in range(parts):
                    a_tab[p, e * parts + i, r * n : (r + 1) * n] = pair[p][i * n : (i + 1) * n]

    with scope("tables"):
        expand(0, col_places, cc, cs)
        compose(kcol[0, 0], kcol[1, 0], cc, cs, keep_col.at[0])
        per = SG // part
        for e in range(2):
            for i in range(parts * per):
                first = (i % per) * part + (e * parts + i // per) * hlong
                src = slice(first, first + hlong)
                dst = slice(i * hlong, (i + 1) * hlong)
                low = slice(wide + i * hlong, wide + (i + 1) * hlong)
                krow[0, e, dst] = kk[src]
                krow[0, e, low] = ks[src]
                krow[1, e, dst] = ks[src]
                krow[1, e, low] = -kk[src]
        expand(0, row_places, rc, rs)
        compose(krow[0, 0], krow[1, 0], rc, rs, keep_row)
    with scope("columns0"):
        loads[0].wait()
        loads[1].wait()
        columns(h, 0)
    with scope("cells"):
        for copy in loads[2:6]:
            copy.wait()
        sub = sub_ref[...]
        row = (lax.rem(sub, NC) * NR + lax.div(sub, NC)) * SG + u_ref[...]
        cell = (row * SG + v_ref[...]).astype(f32)
        for t in range(nv // 128):
            cut = slice(t * 128, (t + 1) * 128)
            vis_all[z, own_xy, 0, t : t + 1] = cell[:, cut]
            vis_all[z, own_xy, 1, t : t + 1] = obs_ref[0:1, cut]
            vis_all[z, own_xy, 2, t : t + 1] = obs_ref[1:2, cut]
    with scope("barwait"):
        pl.semaphore_wait(barrier, len(near))
    for k in range(nx * ny - 1):
        mine = vis_all.at[z, own_xy]
        send("cells", 0, mine, mine, across(k)[2])
    for d in range(1, nz):
        mine = vis_all.at[z, own_xy]
        send("cells_l", 0, mine, mine, to_z(d))
    loads[6].wait()
    send("facet", 0, facet_ref, other, sib)
    with scope("rows0"):
        rows_half(0)

    def project(ref, q, base):
        step = fs // 2
        for k in range(2):
            got = lax.dot_general(
                ref[k * step : (k + 1) * step], bt_ref[h, q], (((1,), (1,)), ((), ())),
                preferred_element_type=f32,
            )
            p_ref[pl.ds(pl.multiple_of(base + k * step, step), step)] = got.astype(bf16)

    own_cut = pl.ds(pl.multiple_of(h * fs, fs), fs)

    def produce(w):
        q, e = w // 2, w % 2
        if e == 0:
            project(facet_ref, q, h * fs)
            if q == 0:
                land("facet", 0, other)
            project(other, q, (1 - h) * fs)
        tall = parts * nx * ny * hlong
        one, two = (
            jnp.dot(a_tab[p, e * parts : (e + 1) * parts].reshape(tall, 2 * fs), p_ref[...], preferred_element_type=f32)
            for p in range(2)
        )
        zr = (one[:, :wide] - two[:, wide:]).reshape(parts, nx, ny, hlong, wide)
        zi = (one[:, wide:] + two[:, :wide]).reshape(parts, nx, ny, hlong, wide)
        for i in range(parts):
            for p, part_z in enumerate((zr, zi)):
                z_ref[w * parts + i, :, :, p] = part_z[i]
                zb_ref[w * parts + i, :, :, p] = part_z[i].astype(bf16)
            for k in range(nx * ny - 1):
                px, py, to = across(k)
                send("plane", w * parts + i, zb_ref.at[w * parts + i, px, py], got.at[w * parts + i, k], to)

    owned_row = lax.broadcasted_iota(i32, (2 * rows_own, 128), 0)
    column = owned_row // rows_own
    column = h + column - 2 * h * column
    owned_row = owned_row % rows_own
    owned_row = (x * ny + y) * part + z * hr + (owned_row // hr) * hlong + owned_row % hr
    owned_row = (owned_row + column * (NR * SG)).astype(f32)
    lanes[...] = lax.broadcasted_iota(i32, lanes.shape, 0).astype(f32).astype(bf16)

    def gridding(ds, ks):
        def one(level, k):
            vis = vis_all[level, k]
            hot_rows, hot_col = hots(vis[0], owned_row, lanes[...])
            left = []
            for t, hot in enumerate(hot_rows):
                values = [vis[1, t : t + 1], vis[2, t : t + 1], jnp.ones_like(vis[0, t : t + 1])]
                left.append(jnp.concatenate([jnp.where(hot, a, 0.0) for a in values], 0).astype(bf16))
            left = jnp.concatenate(left, 1)
            return lax.dot_general(left, hot_col, (((1,), (1,)), ((), ())), preferred_element_type=f32)

        def block(i, slot):
            level = lax.rem(z + ds.start + i // len(ks), nz)
            grid_acc[slot] += one(level, lax.rem(own_xy + ks.start + i % len(ks), nx * ny))

        if chips <= 16:
            for i in range(len(ds) * len(ks)):
                block(i, i % 2)
            return

        def step(i, carry):
            block(i, 0)
            return carry

        lax.fori_loop(0, len(ds) * len(ks), step, 0)

    def reduce(w):
        land("plane", w, got.at[w])
        total = z_ref[w, x, y]
        for k in range(nx * ny - 1):
            total = total + got[w, k].astype(f32)
        for k in range(nz):
            for p in range(2):
                rows_k = total[p, k * hr : (k + 1) * hr]
                own_z[w, k, :, p * wide : (p + 1) * wide] = rows_k
                send_z[w, k, :, p * wide : (p + 1) * wide] = rows_k.astype(bf16)
        for d in range(1, nz):
            send("z", w, send_z.at[w, lax.rem(z + d, nz)], got_z.at[w, d - 1], to_z(d))

    def turn(w):
        q, e = w // (2 * parts), w % (2 * parts)
        if w == 0:
            land("sums", 0, got_sum)
        land("z", w, got_z.at[w])
        total = own_z[w, z]
        for d in range(nz - 1):
            total = total + got_z[w, d].astype(f32)
        m = total * scale
        cut = slice(q * wide, (q + 1) * wide)
        half = slice(e * hr, (e + 1) * hr)
        sums = [own_sum[p, half, cut] + got_sum[p, half, cut] for p in range(3)]
        hat_re = sums[0] - sums[2] * m[:, :wide]
        hat_im = sums[1] - sums[2] * m[:, wide:]
        gz[w, z, :, :wide] = hat_re.astype(bf16)
        gz[w, z, :, wide:] = hat_im.astype(bf16)
        for d in range(1, nz):
            send("back_z", w, gz.at[w, z], gz.at[w, z], to_z(d))
        model[e * hr : (e + 1) * hr, cut] = m[:, :wide]
        model[rows_own + e * hr : rows_own + (e + 1) * hr, cut] = m[:, wide:]

    def over(w, px, py):
        src = g_ref.at[h, w, px, py]
        send("cross", w // parts, src, src, sib)

    def gather(w):
        land("back_z", w, gz.at[w, : nz - 1])
        for k in range(nz):
            cut = slice(k * hr, (k + 1) * hr)
            g_ref[h, w, x, y, 0, cut, :] = gz[w, k, :, :wide]
            g_ref[h, w, x, y, 1, cut, :] = gz[w, k, :, wide:]
        blk = g_ref.at[h, w, x, y]
        for k in range(nx * ny - 1):
            send("back_plane", w, blk, blk, across(k)[2])
        over(w, x, y)

    def finish(w):
        land("back_plane", w, got.at[w])
        for k in range(nx * ny - 1):
            px, py, _ = across(k)
            over(w, px, py)

    def crossed(w):
        land("cross", w, g_ref.at[1 - h, w * parts : (w + 1) * parts])

    def degrid(level):
        m = jnp.concatenate([own_model[...], got_model[...]], 0)

        def one(k):
            hot_rows, hot_col = hots(vis_all[level, k][0], owned_row, lanes[...])
            val = jnp.dot(m, hot_col, preferred_element_type=f32)
            out = []
            for p in range(2):
                line = []
                for t, hot in enumerate(hot_rows):
                    cut = slice(t * 128, (t + 1) * 128)
                    picked = [
                        jnp.where(hot[c * rows_own : (c + 1) * rows_own], val[(2 * c + p) * rows_own : (2 * c + p + 1) * rows_own, cut], 0.0)
                        for c in range(2)
                    ]
                    line.append(jnp.sum(picked[0] + picked[1], 0, keepdims=True))
                out.append(jnp.concatenate(line, 1))
            return jnp.concatenate(out, 0)

        def body(k):
            a = one(k)
            b = one(k + 1)
            vals[level, k] = a
            vals[level, k + 1] = b

        pairs(nx * ny, body)

    def image(side, w):
        c = h if side == 0 else 1 - h
        q, e = w // 2, w % 2
        u = spread_rows(g_ref, at_ref, c, w, slice(None))
        if e == 0:
            half_u[side] = u
            return
        total = (half_u[side] + u).astype(bf16)
        if side == 0:
            full_u[...] = total
            return
        acc_ref[...] = jnp.dot(full_u[...], bt_ref[h, q], preferred_element_type=f32) + jnp.dot(
            total, bt_ref[1 - h, q], preferred_element_type=f32
        )

    grid_acc[...] = jnp.zeros_like(grid_acc)
    done = {"degrid": 0}

    def grid(k):
        if k == 0:
            gridding(range(0, 1), range(0, nx * ny))
        elif k == 1:
            land("cells_l", 0, vis_all.at[: nz - 1, own_xy])
            gridding(range(1, nz), range(0, 1))
        else:
            if k == 2:
                land("cells_z", 0, vis_all.at[: nz - 1, : nx * ny - 1])
            last = nz if k == 4 else k
            gridding(range(k - 1, last), range(1, nx * ny))

    def exchange():
        for p in range(3):
            base = 2 * p * rows_own
            total = grid_acc[0, base : base + 2 * rows_own] + grid_acc[1, base : base + 2 * rows_own]
            own_sum[p] = total[:rows_own]
            pair_sum[p] = total[rows_own:]
        send("sums", 0, pair_sum, got_sum, sib)

    def models():
        own_model[...] = model[...].astype(bf16)
        send("model", 0, own_model, got_model, sib)

    def ungrid(n):
        for _ in range(n * nz // 4):
            k = done["degrid"]
            done["degrid"] += 1
            if k == 0:
                land("model", 0, got_model)
            with scope("degrid%d" % k):
                degrid(lax.rem(z + k, nz))

    def cells():
        land("cells", 0, vis_all.at[z, : nx * ny - 1])
        for k in range(1, nx * ny):
            block = vis_all.at[z, lax.rem(own_xy + k, nx * ny)]
            for d in range(1, nz):
                send("cells_z", 0, block, block, to_z(d))

    def answers():
        peers(lambda pz, pxy, slot, to: send("answers", 0, vals.at[pz, pxy], slots.at[me], to))

    def result():
        land("answers", 0, slots.at[: chips - 1])
        start = vals[z, own_xy]
        if chips > 16:
            total = lax.fori_loop(1, chips, lambda d, t: t + slots[lax.rem(me + d, chips)], start)
        else:
            total = start
            for d in range(1, chips):
                total = total + slots[lax.rem(me + d, chips)]
        res_ref[...] = obs_ref[...] - total

    def turned():
        for p in range(2):
            for e in range(2):
                block = a_tab[p, e * parts : (e + 1) * parts, :, own_cut].reshape(at_ref.shape[-1], fs)
                at_ref[p, e] = block.T

    def late_columns():
        columns(1 - h, 0)
        columns(1 - h, 1)

    acts = {
        "p": produce, "g": grid, "r": reduce, "t": turn, "b": gather, "f": finish, "c": crossed,
        "own": lambda w: image(0, w), "oth": lambda w: image(1, w),
    }
    simple = {
        "v": cells, "ans": answers, "res": result, "x": exchange, "m": models, "tr": turned,
        "rows1": lambda: rows_half(1), "cols1": lambda: columns_half(1), "bt": late_columns,
    }
    for word in ORDER:
        name, _, arg = word.partition(":")
        if name == "d":
            ungrid(int(arg))
        else:
            if name in ("r", "t", "b", "f") and int(arg) >= 4 * parts:
                continue
            with scope(name + arg):
                acts[name](int(arg)) if arg else simple[name]()
    with scope("drain"):
        for kind, like in (
            ("plane", got), ("z", got_z), ("back_z", got_z), ("back_plane", got),
            ("cross", g_ref.at[h]), ("facet", other), ("cells", vis_all.at[z, : nx * ny - 1]),
            ("cells_l", vis_all.at[: nz - 1, own_xy]), ("cells_z", vis_all.at[: nz - 1, : nx * ny - 1]), ("sums", got_sum), ("model", got_model), ("answers", slots.at[: chips - 1]),
        ):
            sentall(kind, like)


def main(ro, co, sub, u, v, obs, facet, scale):
    _, _, nx, ny, nz = geometry()
    chips = nx * ny * nz
    fs = facet.shape[0]
    nv = obs.shape[1]
    rows_own = NR * SG // chips
    parts = split(rows_own)
    waves = 4 * parts
    hr = rows_own // (2 * parts)
    hlong = nz * hr
    wide = SG // 2
    plan, total = semaphores(waves)
    dma = pltpu.SemaphoreType.DMA
    return pl.pallas_call(
        functools.partial(main_kernel, scale),
        out_shape=[
            jax.ShapeDtypeStruct((fs, fs), f32),
            jax.ShapeDtypeStruct((2, waves, nx, ny, 2, hlong, wide), bf16),
            jax.ShapeDtypeStruct((2, 2, fs, parts * nx * ny * hlong), bf16),
            jax.ShapeDtypeStruct((NC, 2, SG, fs), bf16),
            jax.ShapeDtypeStruct((2, nv), f32),
            jax.ShapeDtypeStruct((2, fs, SG), f32),
            jax.ShapeDtypeStruct((fs, SG), bf16),
        ],
        in_specs=[HB] * 7,
        out_specs=[VM] * 7,
        scratch_shapes=[
            pltpu.VMEM((fs, fs), bf16),
            pltpu.SMEM((NR,), i32),
            pltpu.SMEM((NC,), i32),
            pltpu.VMEM((1, nv), i32),
            pltpu.VMEM((1, nv), i32),
            pltpu.VMEM((1, nv), i32),
            pltpu.VMEM((2, nv), f32),
            pltpu.VMEM((SG, SG), bf16),
            pltpu.VMEM((SG, SG), bf16),
            pltpu.VMEM((2, 2, SG, SG), bf16),
            pltpu.VMEM((2, 2, SG, SG), bf16),
            pltpu.VMEM((SG, fs), bf16),
            pltpu.VMEM((SG, fs), bf16),
            pltpu.VMEM((SG, 2 * fs), bf16),
            pltpu.VMEM((SG, 2 * fs), bf16),
            pltpu.VMEM((2, SG, fs), f32),
            pltpu.VMEM((SG, 2 * fs), f32),
            pltpu.VMEM((2, 2 * parts, nx * ny * hlong, 2 * fs), bf16),
            pltpu.VMEM((2 * fs, SG), bf16),
            pltpu.VMEM((nz, nx * ny, 3, nv // 128, 128), f32),
            pltpu.VMEM((fs, fs), bf16),
            pltpu.VMEM((waves, nx, ny, 2, hlong, wide), f32),
            pltpu.VMEM((waves, nx, ny, 2, hlong, wide), bf16),
            pltpu.VMEM((2, 6 * rows_own, SG), f32),
            pltpu.VMEM((3, rows_own, SG), f32),
            pltpu.VMEM((3, rows_own, SG), f32),
            pltpu.VMEM((3, rows_own, SG), f32),
            pltpu.VMEM((2 * rows_own, SG), bf16),
            pltpu.VMEM((2 * rows_own, SG), bf16),
            pltpu.VMEM((SG, 128), bf16),
            pltpu.VMEM((waves, nx * ny - 1, 2, hlong, wide), bf16),
            pltpu.VMEM((waves, nz, hr, SG), f32),
            pltpu.VMEM((waves, nz, hr, SG), bf16),
            pltpu.VMEM((waves, nz - 1, hr, SG), bf16),
            pltpu.VMEM((waves, nz, hr, SG), bf16),
            pltpu.VMEM((2 * rows_own, SG), f32),
            pltpu.VMEM((nz, nx * ny, 2, nv), f32),
            pltpu.VMEM((chips, 2, nv), f32),
            dma((len(plan),)),
            dma((total,)),
            dma((8,)),
        ],
        compiler_params=pltpu.CompilerParams(
            collective_id=0, has_side_effects=True, vmem_limit_bytes=LIMIT
        ),
        name="cycle",
    )(*(pltpu.with_memory_space_constraint(a, pltpu.HBM) for a in (facet, ro, co, sub, u, v, obs)))


def finish_kernel(
    scale, acc_ref, g_ref, at_ref, bt_ref, res_ref, half_u, full_u, image_hbm, out_hbm, buf, sem
):
    _, h, _, _ = position()
    fs = acc_ref.shape[0]
    pieces, each = 2, 2
    step = fs // pieces
    copies = [pltpu.make_async_copy(res_ref, out_hbm, sem.at[pieces * each])]
    copies[0].start()
    for k in range(pieces):
        cut = slice(k * step, (k + 1) * step)
        u = (half_u[1, cut] + spread_rows(g_ref, at_ref, 1 - h, 3, cut)).astype(bf16)
        got = jnp.dot(full_u[cut], bt_ref[h, 1], preferred_element_type=f32)
        got += jnp.dot(u, bt_ref[1 - h, 1], preferred_element_type=f32)
        buf[cut] = (acc_ref[cut] + got) * scale
        for i in range(each):
            row = k * step + i * (step // each)
            rows = slice(row, row + step // each)
            copies.append(pltpu.make_async_copy(buf.at[rows], image_hbm.at[rows], sem.at[k * each + i]))
            copies[-1].start()
    for copy in copies:
        copy.wait()


def finish(acc, g, at, bt, res, half_u, full_u, scale):
    fs = acc.shape[0]
    return pl.pallas_call(
        functools.partial(finish_kernel, scale),
        out_shape=[jax.ShapeDtypeStruct((fs, fs), f32), jax.ShapeDtypeStruct(res.shape, f32)],
        in_specs=[VM] * 7,
        out_specs=[HB] * 2,
        scratch_shapes=[pltpu.VMEM((fs, fs), f32), pltpu.SemaphoreType.DMA((5,))],
        compiler_params=pltpu.CompilerParams(vmem_limit_bytes=6 << 20),
        name="finish",
    )(acc, g, at, bt, res, half_u, full_u)


def shards(facet_image, row_offsets, col_offsets, vis_subgrid, vis_u, vis_v, observed):
    rows, cols, _, _, _ = geometry()
    fs = facet_image.shape[0]
    scale_in = 1.0 / (fs * math.sqrt(rows * cols))
    scale_out = 1.0 / (SG * math.sqrt(NR * NC))
    acc, g, at, bt, residual, half_u, full_u = main(
        row_offsets, col_offsets, vis_subgrid[None], vis_u[None], vis_v[None],
        observed, facet_image, scale_in / SG,
    )
    return tuple(finish(acc, g, at, bt, residual, half_u, full_u, scale_out / SG))


def solution(mesh):
    in_specs = (
        P("frow", "fcol"),
        P(),
        P(),
        P(("frow", "fcol")),
        P(("frow", "fcol")),
        P(("frow", "fcol")),
        P(None, ("frow", "fcol")),
    )
    out_specs = (P("frow", "fcol"), P(None, ("frow", "fcol")))
    return jax.shard_map(shards, mesh=mesh, in_specs=in_specs, out_specs=out_specs, check_vma=False)
```

```python
import functools
import math

import jax
import jax.numpy as jnp
from jax import lax
from jax.experimental import pallas as pl
from jax.experimental.pallas import tpu as pltpu
from jax.sharding import PartitionSpec as P

SKY = 65536
SG = 256
NR = 2
NC = 2
f32 = jnp.float32
bf16 = jnp.bfloat16
i32 = jnp.int32
MESH = pl.DeviceIdType.MESH
VM = pl.BlockSpec(memory_space=pltpu.VMEM)
HB = pl.BlockSpec(memory_space=pltpu.HBM)
LIMIT = 32 << 20
ORDER = (
    "p:0", "rows1", "p:1", "v", "cols1",
    "p:2", "p:3", "r:0", "g:0", "r:1", "g:1",
    "r:2", "g:2", "r:3", "g:3", "r:4", "g:4", "x", "r:5", "bt", "r:6", "tr", "r:7",
    "t:0", "t:1", "t:2", "t:3", "t:4", "t:5", "b:0", "t:6", "t:7", "m", "b:1",
    "b:2", "b:3", "d:1", "b:4", "d:1",
    "b:5", "d:1", "b:6", "b:7", "d:1", "ans",
    "f:0", "f:1", "own:0", "f:2", "f:3", "own:1", "c:0", "oth:0",
    "f:4", "f:5", "own:2", "c:1", "oth:1", "f:6", "c:2", "oth:2",
    "f:7", "own:3", "fin", "res", "c:3",
)

scope = jax.named_scope


def geometry():
    rows = lax.axis_size("frow")
    cols = lax.axis_size("fcol")
    nx = rows // 2
    ny = 1 << ((cols.bit_length() - 1) // 2)
    nz = cols // ny
    return rows, cols, nx, ny, nz


def position():
    _, _, _, ny, _ = geometry()
    frow = lax.axis_index("frow")
    fcol = lax.axis_index("fcol")
    return frow // 2, frow % 2, fcol % ny, fcol // ny


def phase(product):
    k = product & (SKY - 1)
    quarter = lax.shift_right_logical(k + SKY // 8, SKY.bit_length() - 3)
    t = (k - quarter * (SKY // 4)).astype(f32) * (2.0 * math.pi / SKY)
    t2 = t * t
    cos = 1.0 + t2 * (-1 / 2 + t2 * (1 / 24 + t2 * (-1 / 720 + t2 * (1 / 40320))))
    sin = t * (1.0 + t2 * (-1 / 6 + t2 * (1 / 120 + t2 * (-1 / 5040 + t2 * (1 / 362880)))))
    odd = (quarter & 1) == 1
    c = jnp.where(odd, sin, cos)
    s = jnp.where(odd, cos, sin)
    return jnp.where(((quarter + 1) & 2) == 0, c, -c), jnp.where((quarter & 2) == 0, s, -s)


def expand(first, places, c_ref, s_ref):
    n = places.shape[1]
    steps = lax.broadcasted_iota(i32, (16, n), 0)
    c0, s0 = phase(steps * places)
    c1, s1 = phase((first + 16 * steps) * places)
    for k in range(SG // 16):
        ck = c1[k : k + 1]
        sk = s1[k : k + 1]
        c_ref[k * 16 : k * 16 + 16, :] = (ck * c0 - sk * s0).astype(bf16)
        s_ref[k * 16 : k * 16 + 16, :] = (sk * c0 + ck * s0).astype(bf16)


def place(q):
    _, _, _, ny, nz = geometry()
    return lax.div(q, ny * nz), lax.rem(lax.div(q, nz), ny), lax.rem(q, nz)


def device(q, h):
    _, _, _, ny, _ = geometry()
    x, y, z = place(q)
    return (2 * x + h, z * ny + y)


def hots(cell, owned, lanes):
    row = jnp.floor(cell * (1.0 / SG))
    v = (cell - row * SG).astype(bf16)
    rows, cols = [], []
    for t in range(cell.shape[0]):
        hot = lanes == jnp.broadcast_to(v[t : t + 1], lanes.shape)
        cols.append(jnp.where(hot, jnp.ones_like(lanes), jnp.zeros_like(lanes)))
        rows.append(owned == row[t : t + 1])
    return rows, jnp.concatenate(cols, 1)


def pairs(count, body):
    if count <= 4:
        for t in range(0, count, 2):
            body(t)
        return

    def step(t, carry):
        body(2 * t)
        return carry

    lax.fori_loop(0, count // 2, step, 0)


def split(rows_own):
    return 2 if rows_own >= 16 else 1


def semaphores(waves):
    plan = {}
    total = 0
    kinds = (
        "plane", "z", "back_z", "back_plane", "cross",
        "facet", "cells", "cells_l", "cells_z", "sums", "model", "answers",
    )
    for at, kind in enumerate(kinds):
        if kind == "back_z":
            plan[kind] = (at,) + plan["plane"][1:]
            continue
        count = waves if at < 4 else (4 if kind == "cross" else 1)
        plan[kind] = (at, total, count)
        total += count
    return plan, total


def spread_rows(g_ref, at_ref, c, w, cut):
    wide = g_ref.shape[-1]
    parts = g_ref.shape[1] // 4
    tall = at_ref.shape[-1]
    g = jnp.concatenate([g_ref[c, w * parts : (w + 1) * parts, :, :, p].reshape(tall, wide) for p in range(2)], 1)
    one, two = (jnp.dot(at_ref[p, w % 2, cut], g, preferred_element_type=f32) for p in range(2))
    return jnp.concatenate([one[:, :wide] + two[:, wide:], one[:, wide:] - two[:, :wide]], 1)


def main_kernel(
    scale, facet_hbm, ro_hbm, co_hbm, sub_hbm, u_hbm, v_hbm, obs_hbm,
    acc_ref, g_ref, at_ref, bt_ref, res_ref, half_u,
    full_u, facet_ref, ro_ref, co_ref, sub_ref, u_ref, v_ref, obs_ref,
    kk, ks, kcol, krow, cc, cs, rc, rs, keep_col, keep_row, a_tab, p_ref, vis_all, other, z_ref, zb_ref, grid_acc, own_sum, pair_sum, got_sum, own_model, got_model, lanes,
    got, own_z, send_z, got_z, gz, model, vals, slots,
    ssem, rsem, lsem,
):
    rows, cols, nx, ny, nz = geometry()
    x, h, y, z = position()
    chips = nx * ny * nz
    me = (x * ny + y) * nz + z
    fs = facet_ref.shape[0]
    nv = obs_ref.shape[1]
    rows_own = NR * SG // chips
    parts = split(rows_own)
    hr = rows_own // (2 * parts)
    hlong = nz * hr
    part = 2 * parts * hlong
    wide = SG // 2
    sib = (2 * x + 1 - h, lax.axis_index("fcol"))
    barrier = pltpu.get_barrier_semaphore()

    plane = [(dx, dy) for dx in range(nx) for dy in range(ny)][1:]

    def across(k):
        px, py = lax.rem(x + plane[k][0], nx), lax.rem(y + plane[k][1], ny)
        return px, py, (2 * px + h, z * ny + py)

    def to_z(d):
        return 2 * x + h, lax.rem(z + d, nz) * ny + y

    own_xy = x * ny + y
    near = [sib] + [across(k)[2] for k in range(nx * ny - 1)]
    near += [to_z(d) for d in range(1, nz)]
    for to in near:
        pl.semaphore_signal(barrier, inc=1, device_id=to, device_id_type=MESH)

    def peers(act):
        if chips > 16:
            def step(d, carry):
                to = lax.rem(me + d, chips)
                px, py, pz = place(to)
                act(pz, px * ny + py, to, (2 * px + h, pz * ny + py))
                return carry

            lax.fori_loop(1, chips, step, 0)
            return
        for dx in range(nx):
            for dy in range(ny):
                for dz in range(nz):
                    if dx + dy + dz > 0:
                        px = lax.rem(x + dx, nx)
                        py = lax.rem(y + dy, ny)
                        pz = lax.rem(z + dz, nz)
                        act(pz, px * ny + py, (px * ny + py) * nz + pz, (2 * px + h, pz * ny + py))

    loads = []
    for k, (src, dst) in enumerate((
        (ro_hbm, ro_ref), (co_hbm, co_ref), (sub_hbm, sub_ref), (u_hbm, u_ref), (v_hbm, v_ref),
        (obs_hbm, obs_ref), (facet_hbm, facet_ref),
    )):
        loads.append(pltpu.make_async_copy(src, dst, lsem.at[k]))
        loads[-1].start()
    plan = semaphores(4 * parts)[0]

    def send(kind, w, src, dst, to):
        at, base, _ = plan[kind]
        pltpu.make_async_remote_copy(
            src, dst, ssem.at[at], rsem.at[base + w], device_id=to, device_id_type=MESH
        ).start()

    def land(kind, w, like):
        at, base, _ = plan[kind]
        pltpu.make_async_remote_copy(
            like, like, ssem.at[at], rsem.at[base + w], device_id=sib, device_id_type=MESH
        ).wait_recv()

    def sentall(kind, like):
        at, base, _ = plan[kind]
        pltpu.make_async_remote_copy(
            like, like, ssem.at[at], rsem.at[base], device_id=sib, device_id_type=MESH
        ).wait_send()

    with scope("expandK"):
        expand(0, lax.broadcasted_iota(i32, (1, SG), 1) * (SKY // SG), kk, ks)
        for q in range(2):
            cut = slice(q * wide, (q + 1) * wide)
            kcol[0, q, :wide] = kk[cut]
            kcol[0, q, wide:] = ks[cut]
            kcol[1, q, :wide] = ks[cut]
            kcol[1, q, wide:] = -kk[cut]
    col_places = (lax.axis_index("fcol") * fs + lax.broadcasted_iota(i32, (1, fs), 1)) * (SKY // (cols * fs))
    row_places = (x * (2 * fs) + lax.broadcasted_iota(i32, (1, 2 * fs), 1)) * (SKY // (rows * fs))

    def compose(k0, k1, c_ref, s_ref, out):
        n = c_ref.shape[1]
        for cut in (slice(0, n // 2), slice(n // 2, n)):
            both = jnp.dot(k0, c_ref[:, cut], preferred_element_type=f32)
            both += jnp.dot(k1, s_ref[:, cut], preferred_element_type=f32)
            out[:, cut] = both

    def shifted(both, places, offset):
        cos, sin = phase(offset * places)
        re = both[:wide]
        im = both[wide:]
        return (re * cos + im * sin).astype(bf16), (im * cos - re * sin).astype(bf16)

    def columns(c, q):
        bt_ref[c, q, :wide], bt_ref[c, q, wide:] = shifted(keep_col[q], col_places, co_ref[c])

    def columns_half(q):
        compose(kcol[0, q], kcol[1, q], cc, cs, keep_col.at[q])
        columns(h, q)

    def rows_half(e):
        if e > 0:
            compose(krow[0, e], krow[1, e], rc, rs, keep_row)
        for r in range(NR):
            pair = shifted(keep_row[...], row_places, ro_ref[r])
            n = wide // parts
            for p in range(2):
                for i in range(parts):
                    a_tab[p, e * parts + i, r * n : (r + 1) * n] = pair[p][i * n : (i + 1) * n]

    with scope("tables"):
        expand(0, col_places, cc, cs)
        compose(kcol[0, 0], kcol[1, 0], cc, cs, keep_col.at[0])
        per = SG // part
        for e in range(2):
            for i in range(parts * per):
                first = (i % per) * part + (e * parts + i // per) * hlong
                src = slice(first, first + hlong)
                dst = slice(i * hlong, (i + 1) * hlong)
                low = slice(wide + i * hlong, wide + (i + 1) * hlong)
                krow[0, e, dst] = kk[src]
                krow[0, e, low] = ks[src]
                krow[1, e, dst] = ks[src]
                krow[1, e, low] = -kk[src]
        expand(0, row_places, rc, rs)
        compose(krow[0, 0], krow[1, 0], rc, rs, keep_row)
    with scope("columns0"):
        loads[0].wait()
        loads[1].wait()
        columns(h, 0)
    with scope("cells"):
        for copy in loads[2:6]:
            copy.wait()
        sub = sub_ref[...]
        row = (lax.rem(sub, NC) * NR + lax.div(sub, NC)) * SG + u_ref[...]
        cell = (row * SG + v_ref[...]).astype(f32)
        for t in range(nv // 128):
            cut = slice(t * 128, (t + 1) * 128)
            vis_all[z, own_xy, 0, t : t + 1] = cell[:, cut]
            vis_all[z, own_xy, 1, t : t + 1] = obs_ref[0:1, cut]
            vis_all[z, own_xy, 2, t : t + 1] = obs_ref[1:2, cut]
    with scope("barwait"):
        pl.semaphore_wait(barrier, len(near))
    for k in range(nx * ny - 1):
        mine = vis_all.at[z, own_xy]
        send("cells", 0, mine, mine, across(k)[2])
    for d in range(1, nz):
        mine = vis_all.at[z, own_xy]
        send("cells_l", 0, mine, mine, to_z(d))
    loads[6].wait()
    send("facet", 0, facet_ref, other, sib)
    with scope("rows0"):
        rows_half(0)

    def project(ref, q, base):
        step = fs // 2
        for k in range(2):
            got = lax.dot_general(
                ref[k * step : (k + 1) * step], bt_ref[h, q], (((1,), (1,)), ((), ())),
                preferred_element_type=f32,
            )
            p_ref[pl.ds(pl.multiple_of(base + k * step, step), step)] = got.astype(bf16)

    own_cut = pl.ds(pl.multiple_of(h * fs, fs), fs)

    def produce(w):
        q, e = w // 2, w % 2
        if e == 0:
            project(facet_ref, q, h * fs)
            if q == 0:
                land("facet", 0, other)
            project(other, q, (1 - h) * fs)
        tall = parts * nx * ny * hlong
        one, two = (
            jnp.dot(a_tab[p, e * parts : (e + 1) * parts].reshape(tall, 2 * fs), p_ref[...], preferred_element_type=f32)
            for p in range(2)
        )
        zr = (one[:, :wide] - two[:, wide:]).reshape(parts, nx, ny, hlong, wide)
        zi = (one[:, wide:] + two[:, :wide]).reshape(parts, nx, ny, hlong, wide)
        for i in range(parts):
            for p, part_z in enumerate((zr, zi)):
                z_ref[w * parts + i, :, :, p] = part_z[i]
                zb_ref[w * parts + i, :, :, p] = part_z[i].astype(bf16)
            for k in range(nx * ny - 1):
                px, py, to = across(k)
                send("plane", w * parts + i, zb_ref.at[w * parts + i, px, py], got.at[w * parts + i, k], to)

    owned_row = lax.broadcasted_iota(i32, (2 * rows_own, 128), 0)
    column = owned_row // rows_own
    column = h + column - 2 * h * column
    owned_row = owned_row % rows_own
    owned_row = (x * ny + y) * part + z * hr + (owned_row // hr) * hlong + owned_row % hr
    owned_row = (owned_row + column * (NR * SG)).astype(f32)
    lanes[...] = lax.broadcasted_iota(i32, lanes.shape, 0).astype(f32).astype(bf16)

    def gridding(ds, ks):
        def one(level, k):
            vis = vis_all[level, k]
            hot_rows, hot_col = hots(vis[0], owned_row, lanes[...])
            left = []
            for t, hot in enumerate(hot_rows):
                values = [vis[1, t : t + 1], vis[2, t : t + 1], jnp.ones_like(vis[0, t : t + 1])]
                left.append(jnp.concatenate([jnp.where(hot, a, 0.0) for a in values], 0).astype(bf16))
            left = jnp.concatenate(left, 1)
            return lax.dot_general(left, hot_col, (((1,), (1,)), ((), ())), preferred_element_type=f32)

        def block(i, slot):
            level = lax.rem(z + ds.start + i // len(ks), nz)
            grid_acc[slot] += one(level, lax.rem(own_xy + ks.start + i % len(ks), nx * ny))

        if chips <= 16:
            for i in range(len(ds) * len(ks)):
                block(i, i % 2)
            return

        def step(i, carry):
            block(i, 0)
            return carry

        lax.fori_loop(0, len(ds) * len(ks), step, 0)

    def reduce(w):
        land("plane", w, got.at[w])
        total = z_ref[w, x, y]
        for k in range(nx * ny - 1):
            total = total + got[w, k].astype(f32)
        for k in range(nz):
            for p in range(2):
                rows_k = total[p, k * hr : (k + 1) * hr]
                own_z[w, k, :, p * wide : (p + 1) * wide] = rows_k
                send_z[w, k, :, p * wide : (p + 1) * wide] = rows_k.astype(bf16)
        for d in range(1, nz):
            send("z", w, send_z.at[w, lax.rem(z + d, nz)], got_z.at[w, d - 1], to_z(d))

    def turn(w):
        q, e = w // (2 * parts), w % (2 * parts)
        if w == 0:
            land("sums", 0, got_sum)
        land("z", w, got_z.at[w])
        total = own_z[w, z]
        for d in range(nz - 1):
            total = total + got_z[w, d].astype(f32)
        m = total * scale
        cut = slice(q * wide, (q + 1) * wide)
        half = slice(e * hr, (e + 1) * hr)
        sums = [own_sum[p, half, cut] + got_sum[p, half, cut] for p in range(3)]
        hat_re = sums[0] - sums[2] * m[:, :wide]
        hat_im = sums[1] - sums[2] * m[:, wide:]
        gz[w, z, :, :wide] = hat_re.astype(bf16)
        gz[w, z, :, wide:] = hat_im.astype(bf16)
        for d in range(1, nz):
            send("back_z", w, gz.at[w, z], gz.at[w, z], to_z(d))
        model[e * hr : (e + 1) * hr, cut] = m[:, :wide]
        model[rows_own + e * hr : rows_own + (e + 1) * hr, cut] = m[:, wide:]

    def over(w, px, py):
        src = g_ref.at[h, w, px, py]
        send("cross", w // parts, src, src, sib)

    def gather(w):
        land("back_z", w, gz.at[w, : nz - 1])
        for k in range(nz):
            cut = slice(k * hr, (k + 1) * hr)
            g_ref[h, w, x, y, 0, cut, :] = gz[w, k, :, :wide]
            g_ref[h, w, x, y, 1, cut, :] = gz[w, k, :, wide:]
        blk = g_ref.at[h, w, x, y]
        for k in range(nx * ny - 1):
            send("back_plane", w, blk, blk, across(k)[2])
        over(w, x, y)

    def finish(w):
        land("back_plane", w, got.at[w])
        for k in range(nx * ny - 1):
            px, py, _ = across(k)
            over(w, px, py)

    def crossed(w):
        land("cross", w, g_ref.at[1 - h, w * parts : (w + 1) * parts])

    def degrid(level):
        m = jnp.concatenate([own_model[...], got_model[...]], 0)

        def one(k):
            hot_rows, hot_col = hots(vis_all[level, k][0], owned_row, lanes[...])
            val = jnp.dot(m, hot_col, preferred_element_type=f32)
            out = []
            for p in range(2):
                line = []
                for t, hot in enumerate(hot_rows):
                    cut = slice(t * 128, (t + 1) * 128)
                    picked = [
                        jnp.where(hot[c * rows_own : (c + 1) * rows_own], val[(2 * c + p) * rows_own : (2 * c + p + 1) * rows_own, cut], 0.0)
                        for c in range(2)
                    ]
                    line.append(jnp.sum(picked[0] + picked[1], 0, keepdims=True))
                out.append(jnp.concatenate(line, 1))
            return jnp.concatenate(out, 0)

        def body(k):
            a = one(k)
            b = one(k + 1)
            vals[level, k] = a.astype(bf16)
            vals[level, k + 1] = b.astype(bf16)

        pairs(nx * ny, body)

    def image(side, w):
        c = h if side == 0 else 1 - h
        q, e = w // 2, w % 2
        u = spread_rows(g_ref, at_ref, c, w, slice(None))
        if e == 0:
            half_u[side] = u
            return
        total = (half_u[side] + u).astype(bf16)
        if side == 0:
            full_u[...] = total
            return
        acc_ref[...] = jnp.dot(full_u[...], bt_ref[h, q], preferred_element_type=f32) + jnp.dot(
            total, bt_ref[1 - h, q], preferred_element_type=f32
        )

    grid_acc[...] = jnp.zeros_like(grid_acc)
    done = {"degrid": 0}

    def grid(k):
        if k == 0:
            gridding(range(0, 1), range(0, nx * ny))
        elif k == 1:
            land("cells_l", 0, vis_all.at[: nz - 1, own_xy])
            gridding(range(1, nz), range(0, 1))
        else:
            if k == 2:
                land("cells_z", 0, vis_all.at[: nz - 1, : nx * ny - 1])
            last = nz if k == 4 else k
            gridding(range(k - 1, last), range(1, nx * ny))

    def exchange():
        for p in range(3):
            base = 2 * p * rows_own
            total = grid_acc[0, base : base + 2 * rows_own] + grid_acc[1, base : base + 2 * rows_own]
            own_sum[p] = total[:rows_own]
            pair_sum[p] = total[rows_own:]
        send("sums", 0, pair_sum, got_sum, sib)

    def models():
        own_model[...] = model[...].astype(bf16)
        send("model", 0, own_model, got_model, sib)

    def ungrid(n):
        for _ in range(n * nz // 4):
            k = done["degrid"]
            done["degrid"] += 1
            if k == 0:
                land("model", 0, got_model)
            with scope("degrid%d" % k):
                degrid(lax.rem(z + k, nz))

    def cells():
        land("cells", 0, vis_all.at[z, : nx * ny - 1])
        for k in range(1, nx * ny):
            block = vis_all.at[z, lax.rem(own_xy + k, nx * ny)]
            for d in range(1, nz):
                send("cells_z", 0, block, block, to_z(d))

    def answers():
        peers(lambda pz, pxy, slot, to: send("answers", 0, vals.at[pz, pxy], slots.at[me], to))

    def result():
        land("answers", 0, slots.at[: chips - 1])
        start = vals[z, own_xy].astype(f32)
        if chips > 16:
            total = lax.fori_loop(1, chips, lambda d, t: t + slots[lax.rem(me + d, chips)].astype(f32), start)
        else:
            total = start
            for d in range(1, chips):
                total = total + slots[lax.rem(me + d, chips)].astype(f32)
        res_ref[...] = obs_ref[...] - total

    def turned():
        for p in range(2):
            for e in range(2):
                block = a_tab[p, e * parts : (e + 1) * parts, :, own_cut].reshape(at_ref.shape[-1], fs)
                at_ref[p, e] = block.T

    def late_columns():
        columns(1 - h, 0)
        columns(1 - h, 1)

    def own_last():
        acc_ref[...] += jnp.dot(full_u[...], bt_ref[h, 1], preferred_element_type=f32)

    acts = {
        "p": produce, "g": grid, "r": reduce, "t": turn, "b": gather, "f": finish, "c": crossed,
        "own": lambda w: image(0, w), "oth": lambda w: image(1, w),
    }
    simple = {
        "v": cells, "ans": answers, "res": result, "x": exchange, "fin": own_last, "m": models, "tr": turned,
        "rows1": lambda: rows_half(1), "cols1": lambda: columns_half(1), "bt": late_columns,
    }
    for word in ORDER:
        name, _, arg = word.partition(":")
        if name == "d":
            ungrid(int(arg))
        else:
            if name in ("r", "t", "b", "f") and int(arg) >= 4 * parts:
                continue
            with scope(name + arg):
                acts[name](int(arg)) if arg else simple[name]()
    with scope("drain"):
        for kind, like in (
            ("plane", got), ("z", got_z), ("back_z", got_z), ("back_plane", got),
            ("cross", g_ref.at[h]), ("facet", other), ("cells", vis_all.at[z, : nx * ny - 1]),
            ("cells_l", vis_all.at[: nz - 1, own_xy]), ("cells_z", vis_all.at[: nz - 1, : nx * ny - 1]), ("sums", got_sum), ("model", got_model), ("answers", slots.at[: chips - 1]),
        ):
            sentall(kind, like)


def main(ro, co, sub, u, v, obs, facet, scale):
    _, _, nx, ny, nz = geometry()
    chips = nx * ny * nz
    fs = facet.shape[0]
    nv = obs.shape[1]
    rows_own = NR * SG // chips
    parts = split(rows_own)
    waves = 4 * parts
    hr = rows_own // (2 * parts)
    hlong = nz * hr
    wide = SG // 2
    plan, total = semaphores(waves)
    dma = pltpu.SemaphoreType.DMA
    return pl.pallas_call(
        functools.partial(main_kernel, scale),
        out_shape=[
            jax.ShapeDtypeStruct((fs, fs), f32),
            jax.ShapeDtypeStruct((2, waves, nx, ny, 2, hlong, wide), bf16),
            jax.ShapeDtypeStruct((2, 2, fs, parts * nx * ny * hlong), bf16),
            jax.ShapeDtypeStruct((NC, 2, SG, fs), bf16),
            jax.ShapeDtypeStruct((2, nv), f32),
            jax.ShapeDtypeStruct((2, fs, SG), f32),
        ],
        in_specs=[HB] * 7,
        out_specs=[VM] * 6,
        scratch_shapes=[
            pltpu.VMEM((fs, SG), bf16),
            pltpu.VMEM((fs, fs), bf16),
            pltpu.SMEM((NR,), i32),
            pltpu.SMEM((NC,), i32),
            pltpu.VMEM((1, nv), i32),
            pltpu.VMEM((1, nv), i32),
            pltpu.VMEM((1, nv), i32),
            pltpu.VMEM((2, nv), f32),
            pltpu.VMEM((SG, SG), bf16),
            pltpu.VMEM((SG, SG), bf16),
            pltpu.VMEM((2, 2, SG, SG), bf16),
            pltpu.VMEM((2, 2, SG, SG), bf16),
            pltpu.VMEM((SG, fs), bf16),
            pltpu.VMEM((SG, fs), bf16),
            pltpu.VMEM((SG, 2 * fs), bf16),
            pltpu.VMEM((SG, 2 * fs), bf16),
            pltpu.VMEM((2, SG, fs), f32),
            pltpu.VMEM((SG, 2 * fs), f32),
            pltpu.VMEM((2, 2 * parts, nx * ny * hlong, 2 * fs), bf16),
            pltpu.VMEM((2 * fs, SG), bf16),
            pltpu.VMEM((nz, nx * ny, 3, nv // 128, 128), f32),
            pltpu.VMEM((fs, fs), bf16),
            pltpu.VMEM((waves, nx, ny, 2, hlong, wide), f32),
            pltpu.VMEM((waves, nx, ny, 2, hlong, wide), bf16),
            pltpu.VMEM((2, 6 * rows_own, SG), f32),
            pltpu.VMEM((3, rows_own, SG), f32),
            pltpu.VMEM((3, rows_own, SG), f32),
            pltpu.VMEM((3, rows_own, SG), f32),
            pltpu.VMEM((2 * rows_own, SG), bf16),
            pltpu.VMEM((2 * rows_own, SG), bf16),
            pltpu.VMEM((SG, 128), bf16),
            pltpu.VMEM((waves, nx * ny - 1, 2, hlong, wide), bf16),
            pltpu.VMEM((waves, nz, hr, SG), f32),
            pltpu.VMEM((waves, nz, hr, SG), bf16),
            pltpu.VMEM((waves, nz - 1, hr, SG), bf16),
            pltpu.VMEM((waves, nz, hr, SG), bf16),
            pltpu.VMEM((2 * rows_own, SG), f32),
            pltpu.VMEM((nz, nx * ny, 2, nv), bf16),
            pltpu.VMEM((chips, 2, nv), bf16),
            dma((len(plan),)),
            dma((total,)),
            dma((8,)),
        ],
        compiler_params=pltpu.CompilerParams(
            collective_id=0, has_side_effects=True, vmem_limit_bytes=LIMIT
        ),
        name="cycle",
    )(*(pltpu.with_memory_space_constraint(a, pltpu.HBM) for a in (facet, ro, co, sub, u, v, obs)))


def finish_kernel(
    scale, acc_ref, g_ref, at_ref, bt_ref, res_ref, half_u, image_hbm, out_hbm, buf, sem
):
    _, h, _, _ = position()
    fs = acc_ref.shape[0]
    pieces, each = 2, 2
    step = fs // pieces
    copies = [pltpu.make_async_copy(res_ref, out_hbm, sem.at[pieces * each])]
    copies[0].start()
    for k in range(pieces):
        cut = slice(k * step, (k + 1) * step)
        u = (half_u[1, cut] + spread_rows(g_ref, at_ref, 1 - h, 3, cut)).astype(bf16)
        got = jnp.dot(u, bt_ref[1 - h, 1], preferred_element_type=f32)
        buf[cut] = (acc_ref[cut] + got) * scale
        for i in range(each):
            row = k * step + i * (step // each)
            rows = slice(row, row + step // each)
            copies.append(pltpu.make_async_copy(buf.at[rows], image_hbm.at[rows], sem.at[k * each + i]))
            copies[-1].start()
    for copy in copies:
        copy.wait()


def finish(acc, g, at, bt, res, half_u, scale):
    fs = acc.shape[0]
    return pl.pallas_call(
        functools.partial(finish_kernel, scale),
        out_shape=[jax.ShapeDtypeStruct((fs, fs), f32), jax.ShapeDtypeStruct(res.shape, f32)],
        in_specs=[VM] * 6,
        out_specs=[HB] * 2,
        scratch_shapes=[pltpu.VMEM((fs, fs), f32), pltpu.SemaphoreType.DMA((5,))],
        compiler_params=pltpu.CompilerParams(vmem_limit_bytes=6 << 20),
        name="finish",
    )(acc, g, at, bt, res, half_u)


def shards(facet_image, row_offsets, col_offsets, vis_subgrid, vis_u, vis_v, observed):
    rows, cols, _, _, _ = geometry()
    fs = facet_image.shape[0]
    scale_in = 1.0 / (fs * math.sqrt(rows * cols))
    scale_out = 1.0 / (SG * math.sqrt(NR * NC))
    acc, g, at, bt, residual, half_u = main(
        row_offsets, col_offsets, vis_subgrid[None], vis_u[None], vis_v[None],
        observed, facet_image, scale_in / SG,
    )
    return tuple(finish(acc, g, at, bt, residual, half_u, scale_out / SG))


def solution(mesh):
    in_specs = (
        P("frow", "fcol"),
        P(),
        P(),
        P(("frow", "fcol")),
        P(("frow", "fcol")),
        P(("frow", "fcol")),
        P(None, ("frow", "fcol")),
    )
    out_specs = (P("frow", "fcol"), P(None, ("frow", "fcol")))
    return jax.shard_map(shards, mesh=mesh, in_specs=in_specs, out_specs=out_specs, check_vma=False)
```

```python
import functools
import math

import jax
import jax.numpy as jnp
from jax import lax
from jax.experimental import pallas as pl
from jax.experimental.pallas import tpu as pltpu
from jax.sharding import PartitionSpec as P

SKY = 65536
SG = 256
NR = 2
NC = 2
f32 = jnp.float32
bf16 = jnp.bfloat16
i32 = jnp.int32
MESH = pl.DeviceIdType.MESH
VM = pl.BlockSpec(memory_space=pltpu.VMEM)
HB = pl.BlockSpec(memory_space=pltpu.HBM)
LIMIT = 32 << 20
ORDER = (
    "p:0", "rows1", "p:1", "v", "cols1",
    "p:2", "p:3", "r:0", "g:0", "r:1", "g:1",
    "r:2", "g:2", "r:3", "g:3", "r:4", "g:4", "x", "r:5", "bt", "r:6", "tr", "r:7",
    "t:0", "t:1", "t:2", "t:3", "t:4", "t:5", "b:0", "t:6", "t:7", "m", "b:1",
    "b:2", "b:3", "d:1", "b:4", "d:1",
    "b:5", "d:1", "b:6", "b:7", "d:1", "ans",
    "f:0", "f:1", "own:0", "f:2", "f:3", "own:1", "c:0", "oth:0",
    "f:4", "f:5", "own:2", "c:1", "oth:1", "f:6", "c:2", "oth:2",
    "f:7", "own:3", "fin", "res", "c:3",
)

scope = jax.named_scope


def geometry():
    rows = lax.axis_size("frow")
    cols = lax.axis_size("fcol")
    nx = rows // 2
    ny = 1 << ((cols.bit_length() - 1) // 2)
    nz = cols // ny
    return rows, cols, nx, ny, nz


def position():
    _, _, _, ny, _ = geometry()
    frow = lax.axis_index("frow")
    fcol = lax.axis_index("fcol")
    return frow // 2, frow % 2, fcol % ny, fcol // ny


def phase(product):
    k = product & (SKY - 1)
    quarter = lax.shift_right_logical(k + SKY // 8, SKY.bit_length() - 3)
    t = (k - quarter * (SKY // 4)).astype(f32) * (2.0 * math.pi / SKY)
    t2 = t * t
    cos = 1.0 + t2 * (-1 / 2 + t2 * (1 / 24 + t2 * (-1 / 720 + t2 * (1 / 40320))))
    sin = t * (1.0 + t2 * (-1 / 6 + t2 * (1 / 120 + t2 * (-1 / 5040 + t2 * (1 / 362880)))))
    odd = (quarter & 1) == 1
    c = jnp.where(odd, sin, cos)
    s = jnp.where(odd, cos, sin)
    return jnp.where(((quarter + 1) & 2) == 0, c, -c), jnp.where((quarter & 2) == 0, s, -s)


def expand(first, places, c_ref, s_ref):
    n = places.shape[1]
    steps = lax.broadcasted_iota(i32, (16, n), 0)
    c0, s0 = phase(steps * places)
    c1, s1 = phase((first + 16 * steps) * places)
    for k in range(SG // 16):
        ck = c1[k : k + 1]
        sk = s1[k : k + 1]
        c_ref[k * 16 : k * 16 + 16, :] = (ck * c0 - sk * s0).astype(bf16)
        s_ref[k * 16 : k * 16 + 16, :] = (sk * c0 + ck * s0).astype(bf16)


def place(q):
    _, _, _, ny, nz = geometry()
    return lax.div(q, ny * nz), lax.rem(lax.div(q, nz), ny), lax.rem(q, nz)


def device(q, h):
    _, _, _, ny, _ = geometry()
    x, y, z = place(q)
    return (2 * x + h, z * ny + y)


def hots(cell, owned, lanes):
    row = jnp.floor(cell * (1.0 / SG))
    v = (cell - row * SG).astype(bf16)
    rows, cols = [], []
    for t in range(cell.shape[0]):
        hot = lanes == jnp.broadcast_to(v[t : t + 1], lanes.shape)
        cols.append(jnp.where(hot, jnp.ones_like(lanes), jnp.zeros_like(lanes)))
        rows.append(owned == row[t : t + 1])
    return rows, jnp.concatenate(cols, 1)


def pairs(count, body):
    if count <= 4:
        for t in range(0, count, 2):
            body(t)
        return

    def step(t, carry):
        body(2 * t)
        return carry

    lax.fori_loop(0, count // 2, step, 0)


def split(rows_own):
    return 2 if rows_own >= 16 else 1


def semaphores(waves):
    plan = {}
    total = 0
    kinds = (
        "plane", "z", "back_z", "back_plane", "cross",
        "facet", "cells", "cells_l", "cells_z", "sums", "model", "answers",
    )
    for at, kind in enumerate(kinds):
        if kind == "back_z":
            plan[kind] = (at,) + plan["plane"][1:]
            continue
        count = waves if at < 4 else (4 if kind == "cross" else 1)
        plan[kind] = (at, total, count)
        total += count
    return plan, total


def spread_rows(g_ref, at_ref, c, w, cut):
    wide = g_ref.shape[-1]
    parts = g_ref.shape[1] // 4
    tall = at_ref.shape[-1]
    g = jnp.concatenate([g_ref[c, w * parts : (w + 1) * parts, :, :, p].reshape(tall, wide) for p in range(2)], 1)
    one, two = (jnp.dot(at_ref[p, w % 2, cut], g, preferred_element_type=f32) for p in range(2))
    return jnp.concatenate([one[:, :wide] + two[:, wide:], one[:, wide:] - two[:, :wide]], 1)


def main_kernel(
    scale, facet_hbm, ro_hbm, co_hbm, sub_hbm, u_hbm, v_hbm, obs_hbm,
    acc_ref, g_ref, at_ref, bt_ref, res_ref, half_u,
    full_u, facet_ref, ro_ref, co_ref, sub_ref, u_ref, v_ref, obs_ref,
    kk, ks, kcol, krow, cc, cs, rc, rs, keep_col, keep_row, a_tab, p_ref, vis_all, other, z_ref, zb_ref, grid_acc, own_sum, pair_sum, got_sum, own_model, got_model, lanes,
    got, own_z, send_z, got_z, gz, model, vals, slots,
    ssem, rsem, lsem,
):
    rows, cols, nx, ny, nz = geometry()
    x, h, y, z = position()
    chips = nx * ny * nz
    me = (x * ny + y) * nz + z
    fs = facet_ref.shape[0]
    nv = obs_ref.shape[1]
    rows_own = NR * SG // chips
    parts = split(rows_own)
    hr = rows_own // (2 * parts)
    hlong = nz * hr
    part = 2 * parts * hlong
    wide = SG // 2
    sib = (2 * x + 1 - h, lax.axis_index("fcol"))
    barrier = pltpu.get_barrier_semaphore()

    plane = [(dx, dy) for dx in range(nx) for dy in range(ny)][1:]

    def across(k):
        px, py = lax.rem(x + plane[k][0], nx), lax.rem(y + plane[k][1], ny)
        return px, py, (2 * px + h, z * ny + py)

    def to_z(d):
        return 2 * x + h, lax.rem(z + d, nz) * ny + y

    own_xy = x * ny + y
    near = [sib] + [across(k)[2] for k in range(nx * ny - 1)]
    near += [to_z(d) for d in range(1, nz)]
    for to in near:
        pl.semaphore_signal(barrier, inc=1, device_id=to, device_id_type=MESH)

    def peers(act):
        if chips > 16:
            def step(d, carry):
                to = lax.rem(me + d, chips)
                px, py, pz = place(to)
                act(pz, px * ny + py, to, (2 * px + h, pz * ny + py))
                return carry

            lax.fori_loop(1, chips, step, 0)
            return
        for dx in range(nx):
            for dy in range(ny):
                for dz in range(nz):
                    if dx + dy + dz > 0:
                        px = lax.rem(x + dx, nx)
                        py = lax.rem(y + dy, ny)
                        pz = lax.rem(z + dz, nz)
                        act(pz, px * ny + py, (px * ny + py) * nz + pz, (2 * px + h, pz * ny + py))

    loads = []
    for k, (src, dst) in enumerate((
        (ro_hbm, ro_ref), (co_hbm, co_ref), (sub_hbm, sub_ref), (u_hbm, u_ref), (v_hbm, v_ref),
        (obs_hbm, obs_ref), (facet_hbm, facet_ref),
    )):
        loads.append(pltpu.make_async_copy(src, dst, lsem.at[k]))
        loads[-1].start()
    plan = semaphores(4 * parts)[0]

    def send(kind, w, src, dst, to):
        at, base, _ = plan[kind]
        pltpu.make_async_remote_copy(
            src, dst, ssem.at[at], rsem.at[base + w], device_id=to, device_id_type=MESH
        ).start()

    def land(kind, w, like):
        at, base, _ = plan[kind]
        pltpu.make_async_remote_copy(
            like, like, ssem.at[at], rsem.at[base + w], device_id=sib, device_id_type=MESH
        ).wait_recv()

    def sentall(kind, like):
        at, base, _ = plan[kind]
        pltpu.make_async_remote_copy(
            like, like, ssem.at[at], rsem.at[base], device_id=sib, device_id_type=MESH
        ).wait_send()

    with scope("expandK"):
        expand(0, lax.broadcasted_iota(i32, (1, SG), 1) * (SKY // SG), kk, ks)
        for q in range(2):
            cut = slice(q * wide, (q + 1) * wide)
            kcol[0, q, :wide] = kk[cut]
            kcol[0, q, wide:] = ks[cut]
            kcol[1, q, :wide] = ks[cut]
            kcol[1, q, wide:] = -kk[cut]
    col_places = (lax.axis_index("fcol") * fs + lax.broadcasted_iota(i32, (1, fs), 1)) * (SKY // (cols * fs))
    row_places = (x * (2 * fs) + lax.broadcasted_iota(i32, (1, 2 * fs), 1)) * (SKY // (rows * fs))

    def compose(k0, k1, c_ref, s_ref, out):
        n = c_ref.shape[1]
        for cut in (slice(0, n // 2), slice(n // 2, n)):
            both = jnp.dot(k0, c_ref[:, cut], preferred_element_type=f32)
            both += jnp.dot(k1, s_ref[:, cut], preferred_element_type=f32)
            out[:, cut] = both

    def shifted(both, places, offset):
        cos, sin = phase(offset * places)
        re = both[:wide]
        im = both[wide:]
        return (re * cos + im * sin).astype(bf16), (im * cos - re * sin).astype(bf16)

    def columns(c, q):
        bt_ref[c, q, :wide], bt_ref[c, q, wide:] = shifted(keep_col[q], col_places, co_ref[c])

    def columns_half(q):
        compose(kcol[0, q], kcol[1, q], cc, cs, keep_col.at[q])
        columns(h, q)

    def rows_half(e):
        if e > 0:
            compose(krow[0, e], krow[1, e], rc, rs, keep_row)
        for r in range(NR):
            pair = shifted(keep_row[...], row_places, ro_ref[r])
            n = wide // parts
            for p in range(2):
                for i in range(parts):
                    a_tab[p, e * parts + i, r * n : (r + 1) * n] = pair[p][i * n : (i + 1) * n]

    with scope("tables"):
        expand(0, col_places, cc, cs)
        compose(kcol[0, 0], kcol[1, 0], cc, cs, keep_col.at[0])
        per = SG // part
        for e in range(2):
            for i in range(parts * per):
                first = (i % per) * part + (e * parts + i // per) * hlong
                src = slice(first, first + hlong)
                dst = slice(i * hlong, (i + 1) * hlong)
                low = slice(wide + i * hlong, wide + (i + 1) * hlong)
                krow[0, e, dst] = kk[src]
                krow[0, e, low] = ks[src]
                krow[1, e, dst] = ks[src]
                krow[1, e, low] = -kk[src]
        expand(0, row_places, rc, rs)
        compose(krow[0, 0], krow[1, 0], rc, rs, keep_row)
    with scope("columns0"):
        loads[0].wait()
        loads[1].wait()
        columns(h, 0)
    with scope("cells"):
        for copy in loads[2:6]:
            copy.wait()
        sub = sub_ref[...]
        row = (lax.rem(sub, NC) * NR + lax.div(sub, NC)) * SG + u_ref[...]
        cell = (row * SG + v_ref[...]).astype(f32)
        for t in range(nv // 128):
            cut = slice(t * 128, (t + 1) * 128)
            vis_all[z, own_xy, 0, t : t + 1] = cell[:, cut]
            vis_all[z, own_xy, 1, t : t + 1] = obs_ref[0:1, cut]
            vis_all[z, own_xy, 2, t : t + 1] = obs_ref[1:2, cut]
    with scope("barwait"):
        pl.semaphore_wait(barrier, len(near))
    for k in range(nx * ny - 1):
        mine = vis_all.at[z, own_xy]
        send("cells", 0, mine, mine, across(k)[2])
    for d in range(1, nz):
        mine = vis_all.at[z, own_xy]
        send("cells_l", 0, mine, mine, to_z(d))
    loads[6].wait()
    send("facet", 0, facet_ref, other, sib)
    with scope("rows0"):
        rows_half(0)

    def project(ref, q, base):
        step = fs // 2
        for k in range(2):
            got = lax.dot_general(
                ref[k * step : (k + 1) * step], bt_ref[h, q], (((1,), (1,)), ((), ())),
                preferred_element_type=f32,
            )
            p_ref[pl.ds(pl.multiple_of(base + k * step, step), step)] = got.astype(bf16)

    own_cut = pl.ds(pl.multiple_of(h * fs, fs), fs)

    def produce(w):
        q, e = w // 2, w % 2
        if e == 0:
            project(facet_ref, q, h * fs)
            if q == 0:
                land("facet", 0, other)
            project(other, q, (1 - h) * fs)
        tall = parts * nx * ny * hlong
        one, two = (
            jnp.dot(a_tab[p, e * parts : (e + 1) * parts].reshape(tall, 2 * fs), p_ref[...], preferred_element_type=f32)
            for p in range(2)
        )
        zr = (one[:, :wide] - two[:, wide:]).reshape(parts, nx, ny, hlong, wide)
        zi = (one[:, wide:] + two[:, :wide]).reshape(parts, nx, ny, hlong, wide)
        for i in range(parts):
            for p, part_z in enumerate((zr, zi)):
                z_ref[w * parts + i, :, :, p] = part_z[i]
                zb_ref[w * parts + i, :, :, p] = part_z[i].astype(bf16)
            for k in range(nx * ny - 1):
                px, py, to = across(k)
                send("plane", w * parts + i, zb_ref.at[w * parts + i, px, py], got.at[w * parts + i, k], to)

    owned_row = lax.broadcasted_iota(i32, (2 * rows_own, 128), 0)
    column = owned_row // rows_own
    column = h + column - 2 * h * column
    owned_row = owned_row % rows_own
    owned_row = (x * ny + y) * part + z * hr + (owned_row // hr) * hlong + owned_row % hr
    owned_row = (owned_row + column * (NR * SG)).astype(f32)
    lanes[...] = lax.broadcasted_iota(i32, lanes.shape, 0).astype(f32).astype(bf16)

    def gridding(ds, ks):
        def one(level, k):
            vis = vis_all[level, k]
            hot_rows, hot_col = hots(vis[0], owned_row, lanes[...])
            left = []
            for t, hot in enumerate(hot_rows):
                values = [vis[1, t : t + 1], vis[2, t : t + 1], jnp.ones_like(vis[0, t : t + 1])]
                left.append(jnp.concatenate([jnp.where(hot, a, 0.0) for a in values], 0).astype(bf16))
            left = jnp.concatenate(left, 1)
            return lax.dot_general(left, hot_col, (((1,), (1,)), ((), ())), preferred_element_type=f32)

        def block(i, slot):
            level = lax.rem(z + ds.start + i // len(ks), nz)
            grid_acc[slot] += one(level, lax.rem(own_xy + ks.start + i % len(ks), nx * ny))

        if chips <= 16:
            for i in range(len(ds) * len(ks)):
                block(i, i % 2)
            return

        def step(i, carry):
            block(i, 0)
            return carry

        lax.fori_loop(0, len(ds) * len(ks), step, 0)

    def reduce(w):
        land("plane", w, got.at[w])
        total = z_ref[w, x, y]
        for k in range(nx * ny - 1):
            total = total + got[w, k].astype(f32)
        for k in range(nz):
            for p in range(2):
                rows_k = total[p, k * hr : (k + 1) * hr]
                own_z[w, k, :, p * wide : (p + 1) * wide] = rows_k
                send_z[w, k, :, p * wide : (p + 1) * wide] = rows_k.astype(bf16)
        for d in range(1, nz):
            send("z", w, send_z.at[w, lax.rem(z + d, nz)], got_z.at[w, d - 1], to_z(d))

    def turn(w):
        q, e = w // (2 * parts), w % (2 * parts)
        if w == 0:
            land("sums", 0, got_sum)
        land("z", w, got_z.at[w])
        total = own_z[w, z]
        for d in range(nz - 1):
            total = total + got_z[w, d].astype(f32)
        m = total * scale
        cut = slice(q * wide, (q + 1) * wide)
        half = slice(e * hr, (e + 1) * hr)
        sums = [own_sum[p, half, cut] + got_sum[p, half, cut] for p in range(3)]
        hat_re = sums[0] - sums[2] * m[:, :wide]
        hat_im = sums[1] - sums[2] * m[:, wide:]
        gz[w, z, :, :wide] = hat_re.astype(bf16)
        gz[w, z, :, wide:] = hat_im.astype(bf16)
        for d in range(1, nz):
            send("back_z", w, gz.at[w, z], gz.at[w, z], to_z(d))
        model[e * hr : (e + 1) * hr, cut] = m[:, :wide]
        model[rows_own + e * hr : rows_own + (e + 1) * hr, cut] = m[:, wide:]

    def over(w, px, py):
        src = g_ref.at[h, w, px, py]
        send("cross", w // parts, src, src, sib)

    def gather(w):
        land("back_z", w, gz.at[w, : nz - 1])
        for k in range(nz):
            cut = slice(k * hr, (k + 1) * hr)
            g_ref[h, w, x, y, 0, cut, :] = gz[w, k, :, :wide]
            g_ref[h, w, x, y, 1, cut, :] = gz[w, k, :, wide:]
        blk = g_ref.at[h, w, x, y]
        for k in range(nx * ny - 1):
            send("back_plane", w, blk, blk, across(k)[2])
        over(w, x, y)

    def finish(w):
        land("back_plane", w, got.at[w])
        for k in range(nx * ny - 1):
            px, py, _ = across(k)
            over(w, px, py)

    def crossed(w):
        land("cross", w, g_ref.at[1 - h, w * parts : (w + 1) * parts])

    def degrid(level):
        m = jnp.concatenate([own_model[...], got_model[...]], 0)

        def one(k):
            hot_rows, hot_col = hots(vis_all[level, k][0], owned_row, lanes[...])
            val = jnp.dot(m, hot_col, preferred_element_type=f32)
            out = []
            for p in range(2):
                line = []
                for t, hot in enumerate(hot_rows):
                    cut = slice(t * 128, (t + 1) * 128)
                    picked = [
                        jnp.where(hot[c * rows_own : (c + 1) * rows_own], val[(2 * c + p) * rows_own : (2 * c + p + 1) * rows_own, cut], 0.0)
                        for c in range(2)
                    ]
                    line.append(jnp.sum(picked[0] + picked[1], 0, keepdims=True))
                out.append(jnp.concatenate(line, 1))
            return jnp.concatenate(out, 0)

        def body(k):
            a = one(k)
            b = one(k + 1)
            vals[level, k] = a.astype(bf16)
            vals[level, k + 1] = b.astype(bf16)

        pairs(nx * ny, body)

    def image(side, w):
        c = h if side == 0 else 1 - h
        q, e = w // 2, w % 2
        u = spread_rows(g_ref, at_ref, c, w, slice(None))
        if e == 0:
            half_u[side] = u
            return
        total = (half_u[side] + u).astype(bf16)
        if side == 0:
            full_u[...] = total
            return
        acc_ref[...] = jnp.dot(full_u[...], bt_ref[h, q], preferred_element_type=f32) + jnp.dot(
            total, bt_ref[1 - h, q], preferred_element_type=f32
        )

    grid_acc[...] = jnp.zeros_like(grid_acc)
    done = {"degrid": 0}

    def grid(k):
        if k == 0:
            gridding(range(0, 1), range(0, nx * ny))
        elif k == 1:
            land("cells_l", 0, vis_all.at[: nz - 1, own_xy])
            gridding(range(1, nz), range(0, 1))
        else:
            if k == 2:
                land("cells_z", 0, vis_all.at[: nz - 1, : nx * ny - 1])
            last = nz if k == 4 else k
            gridding(range(k - 1, last), range(1, nx * ny))

    def exchange():
        for p in range(3):
            base = 2 * p * rows_own
            total = grid_acc[0, base : base + 2 * rows_own] + grid_acc[1, base : base + 2 * rows_own]
            own_sum[p] = total[:rows_own]
            pair_sum[p] = total[rows_own:]
        send("sums", 0, pair_sum, got_sum, sib)

    def models():
        own_model[...] = model[...].astype(bf16)
        send("model", 0, own_model, got_model, sib)

    def ungrid(n):
        for _ in range(n * nz // 4):
            k = done["degrid"]
            done["degrid"] += 1
            if k == 0:
                land("model", 0, got_model)
            with scope("degrid%d" % k):
                degrid(lax.rem(z + k, nz))

    def cells():
        land("cells", 0, vis_all.at[z, : nx * ny - 1])
        for k in range(1, nx * ny):
            block = vis_all.at[z, lax.rem(own_xy + k, nx * ny)]
            for d in range(1, nz):
                send("cells_z", 0, block, block, to_z(d))

    def answers():
        peers(lambda pz, pxy, slot, to: send("answers", 0, vals.at[pz, pxy], slots.at[me], to))

    def result():
        land("answers", 0, slots.at[: chips - 1])
        start = vals[z, own_xy].astype(f32)
        if chips > 16:
            total = lax.fori_loop(1, chips, lambda d, t: t + slots[lax.rem(me + d, chips)].astype(f32), start)
        else:
            total = start
            for d in range(1, chips):
                total = total + slots[lax.rem(me + d, chips)].astype(f32)
        res_ref[...] = obs_ref[...] - total

    def turned():
        for p in range(2):
            for e in range(2):
                block = a_tab[p, e * parts : (e + 1) * parts, :, own_cut].reshape(at_ref.shape[-1], fs)
                at_ref[p, e] = block.T

    def late_columns():
        columns(1 - h, 0)
        columns(1 - h, 1)

    def own_last():
        acc_ref[...] += jnp.dot(full_u[...], bt_ref[h, 1], preferred_element_type=f32)

    acts = {
        "p": produce, "g": grid, "r": reduce, "t": turn, "b": gather, "f": finish, "c": crossed,
        "own": lambda w: image(0, w), "oth": lambda w: image(1, w),
    }
    simple = {
        "v": cells, "ans": answers, "res": result, "x": exchange, "fin": own_last, "m": models, "tr": turned,
        "rows1": lambda: rows_half(1), "cols1": lambda: columns_half(1), "bt": late_columns,
    }
    for word in ORDER:
        name, _, arg = word.partition(":")
        if name == "d":
            ungrid(int(arg))
        else:
            if name in ("r", "t", "b", "f") and int(arg) >= 4 * parts:
                continue
            with scope(name + arg):
                acts[name](int(arg)) if arg else simple[name]()
    with scope("drain"):
        for kind, like in (
            ("plane", got), ("z", got_z), ("back_z", got_z), ("back_plane", got),
            ("cross", g_ref.at[h]), ("facet", other), ("cells", vis_all.at[z, : nx * ny - 1]),
            ("cells_l", vis_all.at[: nz - 1, own_xy]), ("cells_z", vis_all.at[: nz - 1, : nx * ny - 1]), ("sums", got_sum), ("model", got_model), ("answers", slots.at[: chips - 1]),
        ):
            sentall(kind, like)


def main(ro, co, sub, u, v, obs, facet, scale):
    _, _, nx, ny, nz = geometry()
    chips = nx * ny * nz
    fs = facet.shape[0]
    nv = obs.shape[1]
    rows_own = NR * SG // chips
    parts = split(rows_own)
    waves = 4 * parts
    hr = rows_own // (2 * parts)
    hlong = nz * hr
    wide = SG // 2
    plan, total = semaphores(waves)
    dma = pltpu.SemaphoreType.DMA
    return pl.pallas_call(
        functools.partial(main_kernel, scale),
        out_shape=[
            jax.ShapeDtypeStruct((fs, fs), f32),
            jax.ShapeDtypeStruct((2, waves, nx, ny, 2, hlong, wide), bf16),
            jax.ShapeDtypeStruct((2, 2, fs, parts * nx * ny * hlong), bf16),
            jax.ShapeDtypeStruct((NC, 2, SG, fs), bf16),
            jax.ShapeDtypeStruct((2, nv), f32),
            jax.ShapeDtypeStruct((2, fs, SG), f32),
        ],
        in_specs=[HB] * 7,
        out_specs=[VM] * 6,
        scratch_shapes=[
            pltpu.VMEM((fs, SG), bf16),
            pltpu.VMEM((fs, fs), bf16),
            pltpu.SMEM((NR,), i32),
            pltpu.SMEM((NC,), i32),
            pltpu.VMEM((1, nv), i32),
            pltpu.VMEM((1, nv), i32),
            pltpu.VMEM((1, nv), i32),
            pltpu.VMEM((2, nv), f32),
            pltpu.VMEM((SG, SG), bf16),
            pltpu.VMEM((SG, SG), bf16),
            pltpu.VMEM((2, 2, SG, SG), bf16),
            pltpu.VMEM((2, 2, SG, SG), bf16),
            pltpu.VMEM((SG, fs), bf16),
            pltpu.VMEM((SG, fs), bf16),
            pltpu.VMEM((SG, 2 * fs), bf16),
            pltpu.VMEM((SG, 2 * fs), bf16),
            pltpu.VMEM((2, SG, fs), f32),
            pltpu.VMEM((SG, 2 * fs), f32),
            pltpu.VMEM((2, 2 * parts, nx * ny * hlong, 2 * fs), bf16),
            pltpu.VMEM((2 * fs, SG), bf16),
            pltpu.VMEM((nz, nx * ny, 3, nv // 128, 128), f32),
            pltpu.VMEM((fs, fs), bf16),
            pltpu.VMEM((waves, nx, ny, 2, hlong, wide), f32),
            pltpu.VMEM((waves, nx, ny, 2, hlong, wide), bf16),
            pltpu.VMEM((2, 6 * rows_own, SG), f32),
            pltpu.VMEM((3, rows_own, SG), f32),
            pltpu.VMEM((3, rows_own, SG), f32),
            pltpu.VMEM((3, rows_own, SG), f32),
            pltpu.VMEM((2 * rows_own, SG), bf16),
            pltpu.VMEM((2 * rows_own, SG), bf16),
            pltpu.VMEM((SG, 128), bf16),
            pltpu.VMEM((waves, nx * ny - 1, 2, hlong, wide), bf16),
            pltpu.VMEM((waves, nz, hr, SG), f32),
            pltpu.VMEM((waves, nz, hr, SG), bf16),
            pltpu.VMEM((waves, nz - 1, hr, SG), bf16),
            pltpu.VMEM((waves, nz, hr, SG), bf16),
            pltpu.VMEM((2 * rows_own, SG), f32),
            pltpu.VMEM((nz, nx * ny, 2, nv), bf16),
            pltpu.VMEM((chips, 2, nv), bf16),
            dma((len(plan),)),
            dma((total,)),
            dma((7,)),
        ],
        compiler_params=pltpu.CompilerParams(
            collective_id=0, has_side_effects=True, vmem_limit_bytes=LIMIT
        ),
        name="cycle",
    )(*(pltpu.with_memory_space_constraint(a, pltpu.HBM) for a in (facet, ro, co, sub, u, v, obs)))


def finish_kernel(
    scale, acc_ref, g_ref, at_ref, bt_ref, res_ref, half_u, image_hbm, out_hbm, buf, sem
):
    _, h, _, _ = position()
    fs = acc_ref.shape[0]
    edges = (0, fs * 5 // 8, fs)
    pieces = len(edges) - 1
    copies = [pltpu.make_async_copy(res_ref, out_hbm, sem.at[pieces])]
    copies[0].start()
    for k in range(pieces):
        cut = slice(edges[k], edges[k + 1])
        u = (half_u[1, cut] + spread_rows(g_ref, at_ref, 1 - h, 3, cut)).astype(bf16)
        got = jnp.dot(u, bt_ref[1 - h, 1], preferred_element_type=f32)
        buf[cut] = (acc_ref[cut] + got) * scale
        copies.append(pltpu.make_async_copy(buf.at[cut], image_hbm.at[cut], sem.at[k]))
        copies[-1].start()
    for copy in copies:
        copy.wait()


def finish(acc, g, at, bt, res, half_u, scale):
    fs = acc.shape[0]
    return pl.pallas_call(
        functools.partial(finish_kernel, scale),
        out_shape=[jax.ShapeDtypeStruct((fs, fs), f32), jax.ShapeDtypeStruct(res.shape, f32)],
        in_specs=[VM] * 6,
        out_specs=[HB] * 2,
        scratch_shapes=[pltpu.VMEM((fs, fs), f32), pltpu.SemaphoreType.DMA((3,))],
        compiler_params=pltpu.CompilerParams(vmem_limit_bytes=6 << 20),
        name="finish",
    )(acc, g, at, bt, res, half_u)


def shards(facet_image, row_offsets, col_offsets, vis_subgrid, vis_u, vis_v, observed):
    rows, cols, _, _, _ = geometry()
    fs = facet_image.shape[0]
    scale_in = 1.0 / (fs * math.sqrt(rows * cols))
    scale_out = 1.0 / (SG * math.sqrt(NR * NC))
    acc, g, at, bt, residual, half_u = main(
        row_offsets, col_offsets, vis_subgrid[None], vis_u[None], vis_v[None],
        observed, facet_image, scale_in / SG,
    )
    return tuple(finish(acc, g, at, bt, residual, half_u, scale_out / SG))


def solution(mesh):
    in_specs = (
        P("frow", "fcol"),
        P(),
        P(),
        P(("frow", "fcol")),
        P(("frow", "fcol")),
        P(("frow", "fcol")),
        P(None, ("frow", "fcol")),
    )
    out_specs = (P("frow", "fcol"), P(None, ("frow", "fcol")))
    return jax.shard_map(shards, mesh=mesh, in_specs=in_specs, out_specs=out_specs, check_vma=False)
```
